256 devices in a mesh: panel: 2 (over y_hi), colat: 4 (over y_lo, core), lon: 32 (over x, z).
Axes of the slice: x: 4, y: 4 (y_hi: 2, y_lo: 2; y = y_hi * 2 + y_lo), z: 8, core: 2. Of those that a mesh axis runs over, the one named last changes fastest.
Arguments:
- heat_anomaly: float32 [2, 8, 128, 4096], P('panel', None, 'colat', 'lon'), may hold values from -6 to 6
- prior_flow: float32 [2, 3, 8, 128, 4096], P('panel', None, None, 'colat', 'lon'), may hold values from -6 to 6
- stiffness_profile: float32 [8], replicated, may hold values from 1 to 30
- source_site_lookup: int32 [2, 4, 20480], P('panel', 'colat', 'lon'), may hold values from 0 to 4095
- frame_turning_phase: float32 [2, 4, 10240], P('panel', 'colat', 'lon'), may hold values from -3.140625 to 3.140625
Outputs:
- heat_after_step: float32 [2, 8, 128, 4096], P('panel', None, 'colat', 'lon')
- new_velocity: float32 [2, 3, 8, 128, 4096], P('panel', None, None, 'colat', 'lon')
The draws below stay inside these ranges and needn't reach their ends.
Inputs may be any that keep to these rules, and one draw needn't show every extreme that they name: `source_site_lookup`: a flat cell of the donor tile, row times 128 plus column.
All inputs are finite; a program needn't handle non-finite values.
Results may differ from the reference program's by a relative error of at most 0.00002.
Values sent between devices are 32-bit elements; how exact they have to be, the bound alone decides.
A program may use at most 64 MiB of HBM per device.

```python
import math
import jax
import jax.numpy as jnp

DEPTH_COUNT = 8
CT = 32
CL = 128
ITERS = 8
POLAR_COUNT = 128
AZIMUTH_COUNT = 4096
RIM = 640
RIM1 = 320
N_COLAT = 4
N_LON = 32


def with_ends(values, own_key, least, high):
    index_at = [jax.random.randint(jax.random.fold_in(own_key, axis), (), 0, length) for axis, length in enumerate(values.shape)]
    longest = values.shape.index(max(values.shape))
    next_to = index_at[:longest] + [(index_at[longest] + 1) % values.shape[longest]] + index_at[longest + 1:]
    return values.at[tuple(index_at)].set(least).at[tuple(next_to)].set(high)


def level_of(rng, extent, split, low, largest):
    gain, own = 1.0, jax.random.fold_in(rng, 6)
    for dim, shards_of in split:
        steps = jnp.exp(jax.random.uniform(jax.random.fold_in(own, dim), (shards_of,), jnp.float32, low / len(split), largest / len(split)))
        gain = gain * jnp.repeat(steps, extent[dim] // shards_of).reshape([-1 if axis == dim else 1 for axis in range(len(extent))])
    return gain


def scatter_about(rng, dims, width, most, pieces=(), held_as=jnp.bfloat16):
    drawn = jax.random.normal(rng, dims, jnp.float32) * width
    if len(pieces) > 0:
        drawn = level_of(rng, dims, pieces, -0.22, 0.18) * drawn
    return jnp.clip(drawn, min=-most, max=most).astype(held_as)


def setup_inputs(seed: int = 0) -> dict:
    seeds = jax.random.split(jax.random.key(seed), 6)
    heat_anomaly = scatter_about(seeds[0], (2, DEPTH_COUNT, POLAR_COUNT, AZIMUTH_COUNT), 1.0, 6.0, ((0, 2), (2, 4), (3, 32)), jnp.float32)
    prior_flow = scatter_about(seeds[1], (2, 3, DEPTH_COUNT, POLAR_COUNT, AZIMUTH_COUNT), 1.0, 6.0, ((0, 2), (3, 4), (4, 32)), jnp.float32)
    stiffness_profile = jnp.clip(jnp.exp(jax.random.uniform(seeds[2], (DEPTH_COUNT,), jnp.float32, math.log(1.0), math.log(30.0))), 1.0, 30.0)
    source_site_lookup = with_ends(jax.random.randint(seeds[3], (2, N_COLAT, N_LON * RIM), 0, CT * CL), jax.random.fold_in(seeds[3], 1), 0, (CT * CL) - 1).astype(jnp.int32)
    frame_turning_phase = jnp.clip(jax.random.uniform(seeds[4], (2, N_COLAT, N_LON * RIM1), jnp.float32, -3.140625, 3.140625), -3.140625, 3.140625)
    return {"heat_anomaly": heat_anomaly, "prior_flow": prior_flow, "stiffness_profile": stiffness_profile, "source_site_lookup": source_site_lookup, "frame_turning_phase": frame_turning_phase}


TIME_STEP = 0.1
BUOYANCY_FACTOR = 10.0
DRAG_COEF = 1.0


def march_heat_state(framed_array, arriving_flow):
    centre_val = framed_array[..., 2:-2, 2:-2]
    grad_colat = (8.0 * (framed_array[..., 3:-1, 2:-2] - framed_array[..., 1:-3, 2:-2]) - (framed_array[..., 4:, 2:-2] - framed_array[..., :-4, 2:-2])) / 12.0
    grad_lon = (8.0 * (framed_array[..., 2:-2, 3:-1] - framed_array[..., 2:-2, 1:-3]) - (framed_array[..., 2:-2, 4:] - framed_array[..., 2:-2, :-4])) / 12.0
    level_above = jnp.concatenate([centre_val[..., 1:, :, :], centre_val[..., -1:, :, :]], axis=-3)
    level_below = jnp.concatenate([centre_val[..., :1, :, :], centre_val[..., :-1, :, :]], axis=-3)
    grad_rad = (level_above - level_below) / 2.0
    laplace = framed_array[..., 3:-1, 2:-2] + framed_array[..., 1:-3, 2:-2] + framed_array[..., 2:-2, 3:-1] + framed_array[..., 2:-2, 1:-3] + level_above + level_below - 6.0 * centre_val
    advect = arriving_flow[..., 0, :, :, :] * grad_rad + arriving_flow[..., 1, :, :, :] * grad_colat + arriving_flow[..., 2, :, :, :] * grad_lon
    return centre_val + TIME_STEP * (laplace - advect)


def coefficients(stiffness_profile):
    interface = 0.5 * (stiffness_profile[:-1] + stiffness_profile[1:])
    zero_pad = jnp.zeros_like(stiffness_profile[:1])
    upper_coef = jnp.concatenate([interface, zero_pad])
    lower_coef = jnp.concatenate([zero_pad, interface])
    diagonal = DRAG_COEF + 4.0 * stiffness_profile + upper_coef + lower_coef
    return upper_coef, lower_coef, diagonal


def neighbours(framed_array):
    return framed_array[..., 2:, 1:-1] + framed_array[..., :-2, 1:-1] + framed_array[..., 1:-1, 2:] + framed_array[..., 1:-1, :-2]


def sweep(field_in, near_sum, buoyancy_source, stiffness_profile, upper_coef, lower_coef, diagonal):
    col_shape = (stiffness_profile.shape[0], 1, 1)
    zero_level = jnp.zeros_like(field_in[..., :1, :, :])
    level_above = jnp.concatenate([field_in[..., 1:, :, :], zero_level], axis=-3)
    level_below = jnp.concatenate([zero_level, field_in[..., :-1, :, :]], axis=-3)
    numerator = buoyancy_source + stiffness_profile.reshape(col_shape) * near_sum + upper_coef.reshape(col_shape) * level_above + lower_coef.reshape(col_shape) * level_below
    return numerator / diagonal.reshape(col_shape)


def rotate(values, cos_term, sine_term):
    first = values[..., 1, :, :]
    second = values[..., 2, :, :]
    return jnp.stack([values[..., 0, :, :], cos_term * first + sine_term * second, cos_term * second - sine_term * first], axis=-3)


def inner_slots(source_site_position, patch_height, patch_breadth):
    base = 4 * patch_breadth
    return jnp.concatenate([
        source_site_position[..., patch_breadth:2 * patch_breadth],
        source_site_position[..., 2 * patch_breadth:3 * patch_breadth],
        source_site_position[..., base + 1:base + 2 * patch_height:2],
        source_site_position[..., base + 2 * patch_height:base + 4 * patch_height:2],
    ], axis=-1)


def tile_view(field_in):
    lead_dims = field_in.shape[:-2]
    lead_count = len(lead_dims)
    split_view = field_in.reshape(lead_dims + (N_COLAT, CT, N_LON, CL))
    axis_order = (0, lead_count, lead_count + 2) + tuple(range(1, lead_count)) + (lead_count + 1, lead_count + 3)
    return split_view.transpose(axis_order).reshape((2, N_COLAT, N_LON) + lead_dims[1:] + (CT * CL,))


def take_cells(tile_data, cell_index):
    return jnp.take(tile_data, cell_index, axis=-1)


def collect_sites(field_in, source_site_position):
    return jax.vmap(jax.vmap(jax.vmap(take_cells)))(tile_view(field_in), source_site_position)


def reference(heat_anomaly, prior_flow, stiffness_profile, source_site_lookup, frame_turning_phase):
    source_site_position = source_site_lookup.reshape(2, N_COLAT, N_LON, RIM).astype(jnp.int32)
    slot_angle = frame_turning_phase.reshape(2, N_COLAT, N_LON, RIM1)
    obtained_broad_strip = collect_sites(heat_anomaly, source_site_position)[::-1]
    broad_margin = jnp.pad(heat_anomaly, ((0, 0), (0, 0), (2, 2), (2, 2)))
    north_rim = obtained_broad_strip[:, 0, :, :, 0:2 * CL].reshape(2, N_LON, DEPTH_COUNT, 2, CL).transpose(0, 2, 3, 1, 4).reshape(2, DEPTH_COUNT, 2, AZIMUTH_COUNT)
    south_rim = obtained_broad_strip[:, N_COLAT - 1, :, :, 2 * CL:4 * CL].reshape(2, N_LON, DEPTH_COUNT, 2, CL).transpose(0, 2, 3, 1, 4).reshape(2, DEPTH_COUNT, 2, AZIMUTH_COUNT)
    west_rim = obtained_broad_strip[:, :, 0, :, 4 * CL:4 * CL + 2 * CT].reshape(2, N_COLAT, DEPTH_COUNT, CT, 2).transpose(0, 2, 1, 3, 4).reshape(2, DEPTH_COUNT, POLAR_COUNT, 2)
    east_rim = obtained_broad_strip[:, :, N_LON - 1, :, 4 * CL + 2 * CT:].reshape(2, N_COLAT, DEPTH_COUNT, CT, 2).transpose(0, 2, 1, 3, 4).reshape(2, DEPTH_COUNT, POLAR_COUNT, 2)
    broad_margin = broad_margin.at[:, :, 0:2, 2:AZIMUTH_COUNT + 2].set(north_rim)
    broad_margin = broad_margin.at[:, :, POLAR_COUNT + 2:POLAR_COUNT + 4, 2:AZIMUTH_COUNT + 2].set(south_rim)
    broad_margin = broad_margin.at[:, :, 2:POLAR_COUNT + 2, 0:2].set(west_rim)
    broad_margin = broad_margin.at[:, :, 2:POLAR_COUNT + 2, AZIMUTH_COUNT + 2:AZIMUTH_COUNT + 4].set(east_rim)
    heat_after_step = march_heat_state(broad_margin, prior_flow)

    upper_coef, lower_coef, diagonal = coefficients(stiffness_profile)
    blank_array = jnp.zeros_like(heat_after_step)
    buoyancy_source = jnp.stack([BUOYANCY_FACTOR * heat_after_step, blank_array, blank_array], axis=1)
    inner_index = inner_slots(source_site_position, CT, CL)
    cos_term = jnp.cos(slot_angle)[..., None, :]
    sine_term = jnp.sin(slot_angle)[..., None, :]
    flow_array = prior_flow
    for sweep_no in range(ITERS):
        got_thin = rotate(collect_sites(flow_array, inner_index), cos_term, sine_term)[::-1]
        thin = jnp.pad(flow_array, ((0, 0), (0, 0), (0, 0), (1, 1), (1, 1)))
        north_rim = got_thin[:, 0, :, :, :, 0:CL].transpose(0, 2, 3, 1, 4).reshape(2, 3, DEPTH_COUNT, AZIMUTH_COUNT)
        south_rim = got_thin[:, N_COLAT - 1, :, :, :, CL:2 * CL].transpose(0, 2, 3, 1, 4).reshape(2, 3, DEPTH_COUNT, AZIMUTH_COUNT)
        west_rim = got_thin[:, :, 0, :, :, 2 * CL:2 * CL + CT].transpose(0, 2, 3, 1, 4).reshape(2, 3, DEPTH_COUNT, POLAR_COUNT)
        east_rim = got_thin[:, :, N_LON - 1, :, :, 2 * CL + CT:].transpose(0, 2, 3, 1, 4).reshape(2, 3, DEPTH_COUNT, POLAR_COUNT)
        thin = thin.at[:, :, :, 0, 1:AZIMUTH_COUNT + 1].set(north_rim)
        thin = thin.at[:, :, :, POLAR_COUNT + 1, 1:AZIMUTH_COUNT + 1].set(south_rim)
        thin = thin.at[:, :, :, 1:POLAR_COUNT + 1, 0].set(west_rim)
        thin = thin.at[:, :, :, 1:POLAR_COUNT + 1, AZIMUTH_COUNT + 1].set(east_rim)
        flow_array = sweep(flow_array, neighbours(thin), buoyancy_source, stiffness_profile, upper_coef, lower_coef, diagonal)
    return heat_after_step, flow_array
```

```python
import jax
import jax.numpy as jnp
from jax import lax
from jax.experimental import pallas as pl
from jax.experimental.pallas import tpu as pltpu
from jax.sharding import PartitionSpec as P

ITERS = 8
TIME_STEP = 0.1
BUOYANCY_FACTOR = 10.0
DRAG_COEF = 1.0
MESH = pl.DeviceIdType.MESH
LEVELS, ROWS, COLS = 8, 32, 128


def lane_take(value, index):
    return jnp.take_along_axis(value, index, axis=1, mode="promise_in_bounds")


def kernel(
    n_colat, n_lon,
    heat_in, flow_in, stiff_in, site_in, phase_in,
    heat_out, flow_out,
    flow, source, send_ns, send_we, halo_ns, halo_we, send_sem, recv_sem,
):
    p, c, l = (lax.axis_index(a) for a in ("panel", "colat", "lon"))
    lane = lax.broadcasted_iota(jnp.int32, (LEVELS, COLS), 1)
    level = lax.broadcasted_iota(jnp.int32, (LEVELS, COLS), 0)
    north, south = (c == 0).astype(jnp.int32), (c == n_colat - 1).astype(jnp.int32)
    west, east = (l == 0).astype(jnp.int32), (l == n_lon - 1).astype(jnp.int32)
    other = 1 - p

    def across(edge):
        return p + edge * (other - p)

    sides = (
        ((across(north), c - 1 + north, l), 1 - north),
        ((across(south), c + 1 - south, l), south),
        ((across(west), c, l - 1 + west), 3 - west),
        ((across(east), c, l + 1 - east), 2 + east),
    )
    barrier = pltpu.get_barrier_semaphore()
    for device, _ in sides:
        pl.semaphore_signal(barrier, inc=1, device_id=device, device_id_type=MESH)

    stiff = jnp.zeros((LEVELS, COLS), jnp.float32)
    for k in range(LEVELS):
        stiff = jnp.where(level == k, stiff_in[k], stiff)
    upper = jnp.where(level < LEVELS - 1, 0.5 * (stiff + pltpu.roll(stiff, LEVELS - 1, 0)), 0.0)
    lower = jnp.where(level > 0, 0.5 * (stiff + pltpu.roll(stiff, 1, 0)), 0.0)
    inverse = 1.0 / (DRAG_COEF + 4.0 * stiff + upper + lower)
    coef, above_coef, below_coef = stiff * inverse, upper * inverse, lower * inverse
    buoyancy = BUOYANCY_FACTOR * inverse

    row_of_lane, part_of_lane = lane & (ROWS - 1), lane >> 5

    def sites(j):
        return jnp.broadcast_to(site_in[0, 0:1, COLS * j : COLS * (j + 1)], (LEVELS, COLS))

    def pick(flag, yes, no):
        return jnp.where(flag == 1, yes, no)

    ns_site = pick(north, sites(1), sites(2))
    ns_heat = (pick(north, sites(0), sites(2)), pick(north, sites(1), sites(3)))
    we_site = lane_take(sites(4), pick(west, 2 * row_of_lane + 1, 2 * ROWS + 2 * row_of_lane))
    we_heat = lane_take(
        sites(4), (pick(west, 0, 2 * ROWS) + 2 * row_of_lane + (part_of_lane & 1))
    )
    ns_angle = jnp.broadcast_to(
        pick(north, phase_in[0, 0:1, 0:COLS], phase_in[0, 0:1, COLS : 2 * COLS]), (LEVELS, COLS)
    )
    tail = phase_in[0, 0:1, 2 * COLS : 2 * COLS + 2 * ROWS]
    tail = jnp.broadcast_to(jnp.concatenate([tail, tail], axis=1), (LEVELS, COLS))
    we_angle = lane_take(tail, pick(west, row_of_lane, ROWS + row_of_lane))
    ns_cos, ns_sin = jnp.cos(ns_angle), jnp.sin(ns_angle)
    we_cos, we_sin = jnp.cos(we_angle), jnp.sin(we_angle)

    def heat_row(r):
        return heat_in[pl.ds(r, LEVELS, stride=ROWS), :]

    def collect(index, rows, count):
        at_row, at_col = index >> 7, index & (COLS - 1)
        found = [jnp.zeros((LEVELS, COLS), jnp.float32)] * count
        for r in range(ROWS):
            here = at_row == r
            found = [jnp.where(here, lane_take(rows(r, i), at_col), f) for i, f in enumerate(found)]
        return found

    def flow_row(r, i):
        return flow[r, i]

    def rotated(index, cos, sin):
        a, b, d = collect(index, flow_row, 3)
        return a, cos * b + sin * d, cos * d - sin * b

    def pack(packed, value, t, at):
        return jnp.where(lane == t, pltpu.roll(value, (t - at) % COLS, 1), packed)

    def copies(k, first):
        for side, (device, facing) in enumerate(sides):
            ns = side < 2
            buf, halo = (send_ns, halo_ns) if ns else (send_we, halo_we)
            own, theirs = (side, facing) if ns else (side - 2, facing - 2)
            n = (5 if first else 3) if ns else (2 if first else 1)
            yield pltpu.make_async_remote_copy(
                src_ref=buf.at[k, own, 0:n],
                dst_ref=halo.at[k, theirs, 0:n],
                send_sem=send_sem.at[k, side],
                recv_sem=recv_sem.at[k, facing],
                device_id=device,
                device_id_type=MESH,
            )

    def arrivals(k, first):
        for side, (device, _) in enumerate(sides):
            ns = side < 2
            buf, halo = (send_ns, halo_ns) if ns else (send_we, halo_we)
            own = side if ns else side - 2
            n = (5 if first else 3) if ns else (2 if first else 1)
            yield pltpu.make_async_remote_copy(
                src_ref=buf.at[k, own, 0:n],
                dst_ref=halo.at[k, own, 0:n],
                send_sem=send_sem.at[k, side],
                recv_sem=recv_sem.at[k, side],
                device_id=device,
                device_id_type=MESH,
            )

    def fill_sends(k, packed_west, packed_east):
        for i in range(3):
            send_ns[k, 0, i] = flow[0, i]
            send_ns[k, 1, i] = flow[ROWS - 1, i]
        send_we[k, 0, 0] = packed_west
        send_we[k, 1, 0] = packed_east

        @pl.when((north == 1) | (south == 1))
        def _():
            for i, v in enumerate(rotated(ns_site, ns_cos, ns_sin)):
                send_ns[k, south, i] = v

        @pl.when((west == 1) | (east == 1))
        def _():
            a, b, d = rotated(we_site, we_cos, we_sin)
            send_we[k, east, 0] = jnp.where(
                part_of_lane == 0, a, jnp.where(part_of_lane == 1, b, d)
            )

    zero = jnp.zeros((LEVELS, COLS), jnp.float32)
    packed_west, packed_east, heat_west, heat_east = zero, zero, zero, zero
    for r in range(ROWS):
        for i in range(3):
            value = flow_in[pl.ds(i * LEVELS * ROWS + r, LEVELS, stride=ROWS), :]
            flow[r, i] = value
            packed_west = pack(packed_west, value, i * ROWS + r, 0)
            packed_east = pack(packed_east, value, i * ROWS + r, COLS - 1)
        value = heat_row(r)
        for j in range(2):
            heat_west = pack(heat_west, value, j * ROWS + r, j)
            heat_east = pack(heat_east, value, j * ROWS + r, COLS - 2 + j)
    for j in range(2):
        send_ns[0, 0, 3 + j] = heat_row(j)
        send_ns[0, 1, 3 + j] = heat_row(ROWS - 2 + j)
    send_we[0, 0, 1] = heat_west
    send_we[0, 1, 1] = heat_east
    fill_sends(0, packed_west, packed_east)

    @pl.when((north == 1) | (south == 1))
    def _():
        for j in range(2):
            send_ns[0, south, 3 + j] = collect(ns_heat[j], lambda r, _: heat_row(r), 1)[0]

    @pl.when((west == 1) | (east == 1))
    def _():
        send_we[0, east, 1] = collect(we_heat, lambda r, _: heat_row(r), 1)[0]

    pl.semaphore_wait(barrier, 4)
    for copy in copies(0, True):
        copy.start()
    for copy in arrivals(0, True):
        copy.wait_recv()

    def wide_row(r):
        if r < 0:
            return halo_ns[0, 0, 5 + r]
        if r >= ROWS:
            return halo_ns[0, 1, 3 + r - ROWS]
        return heat_row(r)

    def put(value, packed, t, at):
        return jnp.where(lane == at, pltpu.roll(packed, (at - t) % COLS, 1), value)

    from_west, from_east = halo_we[0, 0, 1], halo_we[0, 1, 1]
    window = [wide_row(r) for r in range(-2, 2)]
    for r in range(ROWS):
        window.append(wide_row(r + 2))
        up2, up1, here, down1, down2 = window[r : r + 5]
        west1 = put(pltpu.roll(here, 1, 1), from_west, ROWS + r, 0)
        west2 = put(put(pltpu.roll(here, 2, 1), from_west, r, 0), from_west, ROWS + r, 1)
        east1 = put(pltpu.roll(here, COLS - 1, 1), from_east, r, COLS - 1)
        east2 = put(
            put(pltpu.roll(here, COLS - 2, 1), from_east, r, COLS - 2), from_east, ROWS + r, COLS - 1
        )
        above = jnp.where(level == LEVELS - 1, here, pltpu.roll(here, LEVELS - 1, 0))
        below = jnp.where(level == 0, here, pltpu.roll(here, 1, 0))
        grad_colat = (8.0 * (down1 - up1) - (down2 - up2)) * (1.0 / 12.0)
        grad_lon = (8.0 * (east1 - west1) - (east2 - west2)) * (1.0 / 12.0)
        grad_rad = (above - below) * 0.5
        laplace = down1 + up1 + east1 + west1 + above + below - 6.0 * here
        advect = flow[r, 0] * grad_rad + flow[r, 1] * grad_colat + flow[r, 2] * grad_lon
        stepped = here + TIME_STEP * (laplace - advect)
        heat_out[pl.ds(r, LEVELS, stride=ROWS), :] = stepped
        source[r] = buoyancy * stepped

    def relax(k, store):
        from_west, from_east = halo_we[k, 0, 0], halo_we[k, 1, 0]
        before = [halo_ns[k, 0, i] for i in range(3)]
        now = [flow[0, i] for i in range(3)]
        for r in range(ROWS):
            after = [halo_ns[k, 1, i] if r == ROWS - 1 else flow[r + 1, i] for i in range(3)]
            for i in range(3):
                t = i * ROWS + r
                here = now[i]
                near = (
                    before[i]
                    + after[i]
                    + put(pltpu.roll(here, 1, 1), from_west, t, 0)
                    + put(pltpu.roll(here, COLS - 1, 1), from_east, t, COLS - 1)
                )
                value = (
                    coef * near
                    + above_coef * pltpu.roll(here, LEVELS - 1, 0)
                    + below_coef * pltpu.roll(here, 1, 0)
                )
                if i == 0:
                    value = value + source[r]
                store(r, i, value)
            before, now = now, after

    def sweep(k, carry):
        packed = [zero, zero]

        def keep(r, i, value):
            flow[r, i] = value
            packed[0] = pack(packed[0], value, i * ROWS + r, 0)
            packed[1] = pack(packed[1], value, i * ROWS + r, COLS - 1)

        relax(k, keep)
        fill_sends(k + 1, *packed)
        for copy in copies(k + 1, False):
            copy.start()
        for copy in arrivals(k + 1, False):
            copy.wait_recv()
        return carry

    lax.fori_loop(0, ITERS - 1, sweep, 0)

    def finish(r, i, value):
        flow_out[pl.ds(i * LEVELS * ROWS + r, LEVELS, stride=ROWS), :] = value

    relax(ITERS - 1, finish)
    for k in range(ITERS):
        for copy in copies(k, k == 0):
            copy.wait_send()


def solution(mesh):
    n_colat, n_lon = mesh.shape["colat"], mesh.shape["lon"]

    def on_device(heat, flow, stiffness, site, phase):
        vmem = pl.BlockSpec(memory_space=pltpu.VMEM)
        block = (LEVELS, COLS)
        heat_out, flow_out = pl.pallas_call(
            lambda *refs: kernel(n_colat, n_lon, *refs),
            out_shape=(
                jax.ShapeDtypeStruct((LEVELS * ROWS, COLS), jnp.float32),
                jax.ShapeDtypeStruct((3 * LEVELS * ROWS, COLS), jnp.float32),
            ),
            in_specs=[vmem, vmem, pl.BlockSpec(memory_space=pltpu.SMEM), vmem, vmem],
            out_specs=(vmem, vmem),
            scratch_shapes=[
                pltpu.VMEM((ROWS, 3, *block), jnp.float32),
                pltpu.VMEM((ROWS, *block), jnp.float32),
                pltpu.VMEM((ITERS, 2, 5, *block), jnp.float32),
                pltpu.VMEM((ITERS, 2, 2, *block), jnp.float32),
                pltpu.VMEM((ITERS, 2, 5, *block), jnp.float32),
                pltpu.VMEM((ITERS, 2, 2, *block), jnp.float32),
                pltpu.SemaphoreType.DMA((ITERS, 4)),
                pltpu.SemaphoreType.DMA((ITERS, 4)),
            ],
            compiler_params=pltpu.CompilerParams(collective_id=0, has_side_effects=True),
            name="mantle_step",
        )(
            heat.reshape(LEVELS * ROWS, COLS),
            flow.reshape(3 * LEVELS * ROWS, COLS),
            stiffness,
            site,
            phase,
        )
        return heat_out.reshape(heat.shape), flow_out.reshape(flow.shape)

    return jax.shard_map(
        on_device,
        mesh=mesh,
        in_specs=(
            P("panel", None, "colat", "lon"),
            P("panel", None, None, "colat", "lon"),
            P(),
            P("panel", "colat", "lon"),
            P("panel", "colat", "lon"),
        ),
        out_specs=(P("panel", None, "colat", "lon"), P("panel", None, None, "colat", "lon")),
        check_vma=False,
    )
```

```python
import jax
import jax.numpy as jnp
from jax import lax
from jax.experimental import pallas as pl
from jax.experimental.pallas import tpu as pltpu
from jax.sharding import PartitionSpec as P

ITERS = 8
TIME_STEP = 0.1
BUOYANCY_FACTOR = 10.0
DRAG_COEF = 1.0
MESH = pl.DeviceIdType.MESH
LEVELS, ROWS, COLS = 8, 32, 128


def lane_take(value, index):
    return jnp.take_along_axis(value, index, axis=1, mode="promise_in_bounds")


def kernel(
    n_colat, n_lon,
    heat_in, flow_in, stiff_in, site_in, phase_in,
    heat_out, flow_out,
    flow, source, found, send_ns, send_we, halo_ns, halo_we, send_sem, recv_sem,
):
    p, c, l = (lax.axis_index(a) for a in ("panel", "colat", "lon"))
    lane = lax.broadcasted_iota(jnp.int32, (LEVELS, COLS), 1)
    level = lax.broadcasted_iota(jnp.int32, (LEVELS, COLS), 0)
    north, south = (c == 0).astype(jnp.int32), (c == n_colat - 1).astype(jnp.int32)
    west, east = (l == 0).astype(jnp.int32), (l == n_lon - 1).astype(jnp.int32)
    at_rim = (north, south, west, east)

    def across(edge):
        return p + edge * (1 - 2 * p)

    sides = (
        ((across(north), c - 1 + north, l), 1 - north),
        ((across(south), c + 1 - south, l), south),
        ((across(west), c, l - 1 + west), 3 - west),
        ((across(east), c, l + 1 - east), 2 + east),
    )
    barrier = pltpu.get_barrier_semaphore()
    for device, _ in sides:
        pl.semaphore_signal(barrier, inc=1, device_id=device, device_id_type=MESH)

    stiff = jnp.zeros((LEVELS, COLS), jnp.float32)
    for k in range(LEVELS):
        stiff = jnp.where(level == k, stiff_in[k], stiff)
    upper = jnp.where(level < LEVELS - 1, 0.5 * (stiff + pltpu.roll(stiff, LEVELS - 1, 0)), 0.0)
    lower = jnp.where(level > 0, 0.5 * (stiff + pltpu.roll(stiff, 1, 0)), 0.0)
    inverse = 1.0 / (DRAG_COEF + 4.0 * stiff + upper + lower)
    coef, above_coef, below_coef = stiff * inverse, upper * inverse, lower * inverse
    buoyancy = BUOYANCY_FACTOR * inverse

    zero = jnp.zeros((LEVELS, COLS), jnp.float32)
    is_even = (lane & 1) == 0
    on_edge = (lane == 0) | (lane == COLS - 1)

    def shift(value, by):
        return pltpu.roll(value, by % COLS, 1)

    def pick(flag, yes, no):
        return jnp.where(flag == 1, yes, no)

    slot = (lane + west) & (COLS - 1)
    slot_row, slot_part = slot & (ROWS - 1), slot >> 5
    heat_slot = (lane + 2 * west) & (COLS - 1)

    def sites(j):
        return jnp.broadcast_to(site_in[0, 0:1, COLS * j : COLS * (j + 1)], (LEVELS, COLS))

    ns_site = pick(north, sites(1), sites(2))
    ns_heat = (pick(north, sites(0), sites(2)), pick(north, sites(1), sites(3)))
    we_base = pick(west, 0, 2 * ROWS)
    we_site = lane_take(sites(4), we_base + west + 2 * slot_row)
    we_heat = lane_take(sites(4), we_base + 2 * (heat_slot >> 2) + (heat_slot & 1))
    ns_angle = jnp.broadcast_to(
        pick(north, phase_in[0, 0:1, 0:COLS], phase_in[0, 0:1, COLS : 2 * COLS]), (LEVELS, COLS)
    )
    tail = phase_in[0, 0:1, 2 * COLS : 2 * COLS + 2 * ROWS]
    tail = jnp.broadcast_to(jnp.concatenate([tail, tail], axis=1), (LEVELS, COLS))
    we_angle = lane_take(tail, pick(west, 0, ROWS) + slot_row)

    def heat_row(r):
        return heat_in[pl.ds(r, LEVELS, stride=ROWS), :]

    def collect(index, rows, count):
        at_row, at_col = index >> 7, index & (COLS - 1)
        values = [zero] * count
        for r in range(ROWS):
            here = at_row == r
            values = [
                jnp.where(here, lane_take(rows(r, i), at_col), v) for i, v in enumerate(values)
            ]
        return values

    def flow_row(r, i):
        return flow[r, i]

    def copy(k, par, first, side, arriving=False):
        device, facing = sides[side]
        ns = side < 2
        buf, halo = (send_ns, halo_ns) if ns else (send_we, halo_we)
        own, theirs = (side, facing) if ns else (side - 2, facing - 2)
        n = (5 if first else 3) if ns else (2 if first else 1)

        at, seen = (own, side) if arriving else (theirs, facing)
        return pltpu.make_async_remote_copy(
            src_ref=buf.at[k, own, 0:n],
            dst_ref=halo.at[k, at, 0:n],
            send_sem=send_sem.at[par, side],
            recv_sem=recv_sem.at[par, seen],
            device_id=device,
            device_id_type=MESH,
        )

    def on_rim(flag_a, flag_b):
        return pl.when((flag_a == 1) | (flag_b == 1))

    def start(k, par, first, side):
        copy(k, par, first, side).start()

    def wait_all(k, par, first):
        for side in range(4):
            copy(k, par, first, side, arriving=True).wait_recv()

    def wait_sent(k, par, first):
        for side in range(4):
            copy(k, par, first, side).wait_send()

    def pack_all(rows):
        packed = [[zero, zero], [zero, zero]]
        for r in range(ROWS):
            for i in range(3):
                part = shift(jnp.where(on_edge, rows(r, i), 0.0), i * ROWS + r)
                packed[r & 1][(r >> 1) & 1] = packed[r & 1][(r >> 1) & 1] + part
        return packed[0][0] + packed[0][1], packed[1][0] + packed[1][1]

    def find(rows):
        @on_rim(north, south)
        def _():
            for i, v in enumerate(collect(ns_site, rows, 3)):
                found[i] = v

        @on_rim(west, east)
        def _():
            for i, v in enumerate(collect(we_site, rows, 3)):
                found[3 + i] = v

    def rotated(values, angle):
        a, b, d = values
        cos, sin = found[angle], found[angle + 1]
        return a, cos * b + sin * d, cos * d - sin * b

    def send_found(k, par, first, patch):
        @on_rim(north, south)
        def _():
            values = patch([found[i] for i in range(3)], ns_site)
            for i, v in enumerate(rotated(values, 6)):
                send_ns[k, south, i] = v

            @pl.when(north == 1)
            def _():
                start(k, par, first, 0)

            @pl.when(south == 1)
            def _():
                start(k, par, first, 1)

        @on_rim(west, east)
        def _():
            values = patch([found[3 + i] for i in range(3)], we_site)
            a, b, d = rotated(values, 8)
            send_we[k, east, 0] = jnp.where(slot_part == 0, a, jnp.where(slot_part == 1, b, d))

            @pl.when(west == 1)
            def _():
                start(k, par, first, 2)

            @pl.when(east == 1)
            def _():
                start(k, par, first, 3)

    def send_inside(k, par, first):
        for side in (2, 3, 0, 1):

            @pl.when(at_rim[side] == 0)
            def _(side=side):
                start(k, par, first, side)

    def first_row(r, i):
        return flow_in[pl.ds(i * LEVELS * ROWS + r, LEVELS, stride=ROWS), :]

    even, odd = pack_all(first_row)
    near_edge = (lane < 2) | (lane >= COLS - 2)
    heat_packed = [zero, zero]
    for r in range(ROWS):
        part = shift(jnp.where(near_edge, heat_row(r), 0.0), 4 * r)
        heat_packed[r & 1] = heat_packed[r & 1] + part
    heat_packed = heat_packed[0] + heat_packed[1]
    for j in range(2):
        send_ns[0, 0, 3 + j] = heat_row(j)
        send_ns[0, 1, 3 + j] = heat_row(ROWS - 2 + j)
        send_we[0, j, 1] = heat_packed
    for i in range(3):
        send_ns[0, 0, i] = first_row(0, i)
        send_ns[0, 1, i] = first_row(ROWS - 1, i)
    send_we[0, 0, 0] = jnp.where(is_even, even, odd)
    send_we[0, 1, 0] = jnp.where(is_even, odd, even)

    @on_rim(north, south)
    def _():
        found[6], found[7] = jnp.cos(ns_angle), jnp.sin(ns_angle)
        for j in range(2):
            send_ns[0, south, 3 + j] = collect(ns_heat[j], lambda r, _: heat_row(r), 1)[0]

    @on_rim(west, east)
    def _():
        found[8], found[9] = jnp.cos(we_angle), jnp.sin(we_angle)
        send_we[0, east, 1] = collect(we_heat, lambda r, _: heat_row(r), 1)[0]

    find(first_row)
    pl.semaphore_wait(barrier, 4)
    send_inside(0, 0, True)
    send_found(0, 0, True, lambda values, index: values)

    def relax(rows, source=None):
        before = [zero] * 3
        now = [rows(0, i) for i in range(3)]
        for r in range(ROWS):
            after = [rows(r + 1, i) for i in range(3)] if r < ROWS - 1 else [zero] * 3
            for i in range(3):
                here = now[i]
                near = (
                    (before[i] + after[i])
                    + jnp.where(lane == 0, 0.0, shift(here, 1))
                    + jnp.where(lane == COLS - 1, 0.0, shift(here, -1))
                )
                value = (
                    coef * near
                    + above_coef * pltpu.roll(here, LEVELS - 1, 0)
                    + below_coef * pltpu.roll(here, 1, 0)
                )
                if i == 0 and source is not None:
                    value = value + source[r]
                flow[r, i] = value
            before, now = now, after

    def completed(k):
        first_cols, last_cols = halo_we[k, 1, 0], shift(halo_we[k, 0, 0], 2)
        pair = (
            coef * jnp.where(is_even, first_cols, last_cols),
            coef * jnp.where(is_even, last_cols, first_cols),
        )

        def rows(r, i):
            value = flow[r, i] + jnp.where(on_edge, shift(pair[r & 1], COLS - 1 - i * ROWS - r), 0.0)
            if r == 0:
                value = value + coef * halo_ns[k, 0, i]
            if r == ROWS - 1:
                value = value + coef * halo_ns[k, 1, i]
            return value

        return rows

    def send_edges(k, par, even, odd):
        above = [coef * halo_ns[k, 0, i] for i in range(3)]
        below = [coef * halo_ns[k, 1, i] for i in range(3)]
        last, first = coef * halo_we[k, 0, 0], coef * halo_we[k, 1, 0]
        for i in range(3):
            even = even + shift(jnp.where(on_edge, above[i], 0.0), i * ROWS)
            odd = odd + shift(jnp.where(on_edge, below[i], 0.0), i * ROWS + ROWS - 1)
        send_we[k + 1, 0, 0] = jnp.where(is_even, even, odd) + shift(last, 1)
        send_we[k + 1, 1, 0] = jnp.where(is_even, odd, even) + shift(first, -1)
        for own, r, halo in ((0, 0, above), (1, ROWS - 1, below)):
            for i in range(3):
                t = i * ROWS + r
                send_ns[k + 1, own, i] = (
                    flow[r, i]
                    + halo[i]
                    + jnp.where(lane == 0, shift(last, 1 - t), 0.0)
                    + jnp.where(lane == COLS - 1, shift(first, COLS - 1 - t), 0.0)
                )
        send_inside(k + 1, par, False)

        def patch(values, index):
            at_row, at_col = index >> 7, index & (COLS - 1)
            for i in range(3):
                slot = i * ROWS + at_row
                add = jnp.where(at_row == 0, lane_take(above[i], at_col), 0.0)
                add = add + jnp.where(at_row == ROWS - 1, lane_take(below[i], at_col), 0.0)
                add = add + jnp.where(at_col == 0, lane_take(last, (slot - 1) & (COLS - 1)), 0.0)
                add = add + jnp.where(at_col == COLS - 1, lane_take(first, slot), 0.0)
                values[i] = values[i] + add
            return values

        send_found(k + 1, par, False, patch)

    relax(first_row)
    wait_all(0, 0, True)

    def wide_row(r):
        if r < 0:
            return halo_ns[0, 0, 5 + r]
        if r >= ROWS:
            return halo_ns[0, 1, 3 + r - ROWS]
        return heat_row(r)

    around = jnp.where((lane & 3) < 2, halo_we[0, 1, 1], halo_we[0, 0, 1])
    window = [wide_row(r) for r in range(-2, 2)]
    for r in range(ROWS):
        window.append(wide_row(r + 2))
        up2, up1, here, down1, down2 = window[r : r + 5]
        rim = shift(around, -4 * r)
        west1 = shift(jnp.where(lane == COLS - 1, rim, here), 1)
        west2 = shift(jnp.where(lane >= COLS - 2, rim, here), 2)
        east1 = shift(jnp.where(lane == 0, rim, here), -1)
        east2 = shift(jnp.where(lane < 2, rim, here), -2)
        above = jnp.where(level == LEVELS - 1, here, pltpu.roll(here, LEVELS - 1, 0))
        below = jnp.where(level == 0, here, pltpu.roll(here, 1, 0))
        grad_colat = (8.0 * (down1 - up1) - (down2 - up2)) * (1.0 / 12.0)
        grad_lon = (8.0 * (east1 - west1) - (east2 - west2)) * (1.0 / 12.0)
        grad_rad = (above - below) * 0.5
        laplace = down1 + up1 + east1 + west1 + above + below - 6.0 * here
        advect = first_row(r, 0) * grad_rad + first_row(r, 1) * grad_colat + first_row(r, 2) * grad_lon
        stepped = here + TIME_STEP * (laplace - advect)
        heat_out[pl.ds(r, LEVELS, stride=ROWS), :] = stepped
        source[r] = buoyancy * stepped
        flow[r, 0] = flow[r, 0] + source[r]

    even, odd = pack_all(flow_row)
    find(flow_row)
    send_edges(0, 1, even, odd)

    def step(k, carry):
        par = k & 1
        relax(completed(k - 1), source)
        even, odd = pack_all(flow_row)
        find(flow_row)
        wait_all(k, par, False)

        @pl.when(k > 1)
        def _():
            wait_sent(k - 1, 1 - par, False)

        send_edges(k, 1 - par, even, odd)
        return carry

    wait_sent(0, 0, True)
    lax.fori_loop(1, ITERS - 1, step, 0)
    relax(completed(ITERS - 2), source)
    last_par = (ITERS - 1) & 1
    wait_all(ITERS - 1, last_par, False)
    rows = completed(ITERS - 1)
    for r in range(ROWS):
        for i in range(3):
            flow_out[pl.ds(i * LEVELS * ROWS + r, LEVELS, stride=ROWS), :] = rows(r, i)
    wait_sent(ITERS - 2, 1 - last_par, False)
    wait_sent(ITERS - 1, last_par, False)


def solution(mesh):
    n_colat, n_lon = mesh.shape["colat"], mesh.shape["lon"]

    def on_device(heat, flow, stiffness, site, phase):
        vmem = pl.BlockSpec(memory_space=pltpu.VMEM)
        block = (LEVELS, COLS)
        heat_out, flow_out = pl.pallas_call(
            lambda *refs: kernel(n_colat, n_lon, *refs),
            out_shape=(
                jax.ShapeDtypeStruct((LEVELS * ROWS, COLS), jnp.float32),
                jax.ShapeDtypeStruct((3 * LEVELS * ROWS, COLS), jnp.float32),
            ),
            in_specs=[vmem, vmem, pl.BlockSpec(memory_space=pltpu.SMEM), vmem, vmem],
            out_specs=(vmem, vmem),
            scratch_shapes=[
                pltpu.VMEM((ROWS, 3, *block), jnp.float32),
                pltpu.VMEM((ROWS, *block), jnp.float32),
                pltpu.VMEM((10, *block), jnp.float32),
                pltpu.VMEM((ITERS, 2, 5, *block), jnp.float32),
                pltpu.VMEM((ITERS, 2, 2, *block), jnp.float32),
                pltpu.VMEM((ITERS, 2, 5, *block), jnp.float32),
                pltpu.VMEM((ITERS, 2, 2, *block), jnp.float32),
                pltpu.SemaphoreType.DMA((2, 4)),
                pltpu.SemaphoreType.DMA((2, 4)),
            ],
            compiler_params=pltpu.CompilerParams(collective_id=0, has_side_effects=True),
            name="mantle_step",
        )(
            heat.reshape(LEVELS * ROWS, COLS),
            flow.reshape(3 * LEVELS * ROWS, COLS),
            stiffness,
            site,
            phase,
        )
        return heat_out.reshape(heat.shape), flow_out.reshape(flow.shape)

    return jax.shard_map(
        on_device,
        mesh=mesh,
        in_specs=(
            P("panel", None, "colat", "lon"),
            P("panel", None, None, "colat", "lon"),
            P(),
            P("panel", "colat", "lon"),
            P("panel", "colat", "lon"),
        ),
        out_specs=(P("panel", None, "colat", "lon"), P("panel", None, None, "colat", "lon")),
        check_vma=False,
    )
```

```python
import jax
import jax.numpy as jnp
from jax import lax
from jax.experimental import pallas as pl
from jax.experimental.pallas import tpu as pltpu
from jax.sharding import PartitionSpec as P

ITERS = 8
TIME_STEP = 0.1
BUOYANCY_FACTOR = 10.0
DRAG_COEF = 1.0
MESH = pl.DeviceIdType.MESH
LEVELS, ROWS, COLS = 8, 32, 128


def lane_take(value, index):
    return jnp.take_along_axis(value, index, axis=1, mode="promise_in_bounds")


def kernel(
    n_colat, n_lon,
    heat_hbm, flow_hbm, stiff_hbm, site_hbm, phase_hbm,
    heat_done, flow_done,
    heat_in, flow_in, stiff_in, site_in, phase_in, heat_out, flow_out, in_sem, out_sem,
    flow, source, found, send_ns, send_we, halo_ns, halo_we, send_sem, recv_sem,
):
    p, c, l = (lax.axis_index(a) for a in ("panel", "colat", "lon"))
    lane = lax.broadcasted_iota(jnp.int32, (LEVELS, COLS), 1)
    level = lax.broadcasted_iota(jnp.int32, (LEVELS, COLS), 0)
    north, south = (c == 0).astype(jnp.int32), (c == n_colat - 1).astype(jnp.int32)
    west, east = (l == 0).astype(jnp.int32), (l == n_lon - 1).astype(jnp.int32)
    at_rim = (north, south, west, east)

    def across(edge):
        return p + edge * (1 - 2 * p)

    sides = (
        ((across(north), c - 1 + north, l), 1 - north),
        ((across(south), c + 1 - south, l), south),
        ((across(west), c, l - 1 + west), 3 - west),
        ((across(east), c, l + 1 - east), 2 + east),
    )
    barrier = pltpu.get_barrier_semaphore()
    for device, _ in sides:
        pl.semaphore_signal(barrier, inc=1, device_id=device, device_id_type=MESH)
    inputs = [
        pltpu.make_async_copy(src, dst, in_sem.at[n])
        for n, (src, dst) in enumerate(
            (
                (stiff_hbm, stiff_in),
                (site_hbm, site_in),
                (phase_hbm, phase_in),
                (flow_hbm, flow_in),
                (heat_hbm, heat_in),
            )
        )
    ]
    for n in (3, 4, 0, 1, 2):
        inputs[n].start()
    for n in (0, 1, 2):
        inputs[n].wait()

    stiff = jnp.zeros((LEVELS, COLS), jnp.float32)
    for k in range(LEVELS):
        stiff = jnp.where(level == k, stiff_in[k], stiff)
    upper = jnp.where(level < LEVELS - 1, 0.5 * (stiff + pltpu.roll(stiff, LEVELS - 1, 0)), 0.0)
    lower = jnp.where(level > 0, 0.5 * (stiff + pltpu.roll(stiff, 1, 0)), 0.0)
    inverse = 1.0 / (DRAG_COEF + 4.0 * stiff + upper + lower)
    coef, above_coef, below_coef = stiff * inverse, upper * inverse, lower * inverse
    buoyancy = BUOYANCY_FACTOR * inverse

    zero = jnp.zeros((LEVELS, COLS), jnp.float32)
    is_even = (lane & 1) == 0
    on_edge = (lane == 0) | (lane == COLS - 1)

    def shift(value, by):
        return pltpu.roll(value, by % COLS, 1)

    def pick(flag, yes, no):
        return jnp.where(flag == 1, yes, no)

    slot = (lane + west) & (COLS - 1)
    slot_row, slot_part = slot & (ROWS - 1), slot >> 5
    heat_slot = (lane + 2 * west) & (COLS - 1)

    def sites(j):
        return jnp.broadcast_to(site_in[0, 0:1, COLS * j : COLS * (j + 1)], (LEVELS, COLS))

    ns_site = pick(north, sites(1), sites(2))
    ns_heat = (pick(north, sites(0), sites(2)), pick(north, sites(1), sites(3)))
    we_base = pick(west, 0, 2 * ROWS)
    we_site = lane_take(sites(4), we_base + west + 2 * slot_row)
    we_heat = lane_take(sites(4), we_base + 2 * (heat_slot >> 2) + (heat_slot & 1))
    ns_angle = jnp.broadcast_to(
        pick(north, phase_in[0, 0:1, 0:COLS], phase_in[0, 0:1, COLS : 2 * COLS]), (LEVELS, COLS)
    )
    tail = phase_in[0, 0:1, 2 * COLS : 2 * COLS + 2 * ROWS]
    tail = jnp.broadcast_to(jnp.concatenate([tail, tail], axis=1), (LEVELS, COLS))
    we_angle = lane_take(tail, pick(west, 0, ROWS) + slot_row)

    def heat_row(r):
        return heat_in[pl.ds(r, LEVELS, stride=ROWS), :]

    def collect(index, rows, count):
        at_row, at_col = index >> 7, index & (COLS - 1)
        values = [zero] * count
        for r in range(ROWS):
            here = at_row == r
            values = [
                jnp.where(here, lane_take(rows(r, i), at_col), v) for i, v in enumerate(values)
            ]
        return values

    def flow_row(r, i):
        return flow[r, i]

    def copy(k, par, first, side, arriving=False):
        device, facing = sides[side]
        ns = side < 2
        buf, halo = (send_ns, halo_ns) if ns else (send_we, halo_we)
        own, theirs = (side, facing) if ns else (side - 2, facing - 2)
        n = (5 if first else 3) if ns else (2 if first else 1)

        at, seen = (own, side) if arriving else (theirs, facing)
        return pltpu.make_async_remote_copy(
            src_ref=buf.at[k, own, 0:n],
            dst_ref=halo.at[k, at, 0:n],
            send_sem=send_sem.at[par, side],
            recv_sem=recv_sem.at[par, seen],
            device_id=device,
            device_id_type=MESH,
        )

    def on_rim(flag_a, flag_b):
        return pl.when((flag_a == 1) | (flag_b == 1))

    def start(k, par, first, side):
        copy(k, par, first, side).start()

    def wait_all(k, par, first):
        for side in range(4):
            copy(k, par, first, side, arriving=True).wait_recv()

    def wait_sent(k, par, first):
        for side in range(4):
            copy(k, par, first, side).wait_send()

    def pack_all(rows):
        packed = [[zero, zero], [zero, zero]]
        for r in range(ROWS):
            for i in range(3):
                part = shift(jnp.where(on_edge, rows(r, i), 0.0), i * ROWS + r)
                packed[r & 1][(r >> 1) & 1] = packed[r & 1][(r >> 1) & 1] + part
        return packed[0][0] + packed[0][1], packed[1][0] + packed[1][1]

    def find(rows):
        @on_rim(north, south)
        def _():
            for i, v in enumerate(collect(ns_site, rows, 3)):
                found[i] = v

        @on_rim(west, east)
        def _():
            for i, v in enumerate(collect(we_site, rows, 3)):
                found[3 + i] = v

    def rotated(values, angle):
        a, b, d = values
        cos, sin = found[angle], found[angle + 1]
        return a, cos * b + sin * d, cos * d - sin * b

    def send_found(k, par, first, patch):
        @on_rim(north, south)
        def _():
            values = patch([found[i] for i in range(3)], ns_site)
            for i, v in enumerate(rotated(values, 6)):
                send_ns[k, south, i] = v

            @pl.when(north == 1)
            def _():
                start(k, par, first, 0)

            @pl.when(south == 1)
            def _():
                start(k, par, first, 1)

        @on_rim(west, east)
        def _():
            values = patch([found[3 + i] for i in range(3)], we_site)
            a, b, d = rotated(values, 8)
            send_we[k, east, 0] = jnp.where(slot_part == 0, a, jnp.where(slot_part == 1, b, d))

            @pl.when(west == 1)
            def _():
                start(k, par, first, 2)

            @pl.when(east == 1)
            def _():
                start(k, par, first, 3)

    def send_inside(k, par, first):
        for side in (2, 3, 0, 1):

            @pl.when(at_rim[side] == 0)
            def _(side=side):
                start(k, par, first, side)

    def first_row(r, i):
        return flow_in[pl.ds(i * LEVELS * ROWS + r, LEVELS, stride=ROWS), :]

    @on_rim(north, south)
    def _():
        found[6], found[7] = jnp.cos(ns_angle), jnp.sin(ns_angle)

    @on_rim(west, east)
    def _():
        found[8], found[9] = jnp.cos(we_angle), jnp.sin(we_angle)

    inputs[3].wait()
    even, odd = pack_all(first_row)
    inputs[4].wait()
    near_edge = (lane < 2) | (lane >= COLS - 2)
    heat_packed = [zero, zero]
    for r in range(ROWS):
        part = shift(jnp.where(near_edge, heat_row(r), 0.0), 4 * r)
        heat_packed[r & 1] = heat_packed[r & 1] + part
    heat_packed = heat_packed[0] + heat_packed[1]
    for j in range(2):
        send_ns[0, 0, 3 + j] = heat_row(j)
        send_ns[0, 1, 3 + j] = heat_row(ROWS - 2 + j)
        send_we[0, j, 1] = heat_packed
    for i in range(3):
        send_ns[0, 0, i] = first_row(0, i)
        send_ns[0, 1, i] = first_row(ROWS - 1, i)
    send_we[0, 0, 0] = jnp.where(is_even, even, odd)
    send_we[0, 1, 0] = jnp.where(is_even, odd, even)

    pl.semaphore_wait(barrier, 4)
    send_inside(0, 0, True)

    @on_rim(north, south)
    def _():
        for j in range(2):
            send_ns[0, south, 3 + j] = collect(ns_heat[j], lambda r, _: heat_row(r), 1)[0]

    @on_rim(west, east)
    def _():
        send_we[0, east, 1] = collect(we_heat, lambda r, _: heat_row(r), 1)[0]

    find(first_row)
    send_found(0, 0, True, lambda values, index: values)

    def relax(rows, source=None):
        before = [zero] * 3
        now = [rows(0, i) for i in range(3)]
        for r in range(ROWS):
            after = [rows(r + 1, i) for i in range(3)] if r < ROWS - 1 else [zero] * 3
            for i in range(3):
                here = now[i]
                near = (
                    (before[i] + after[i])
                    + jnp.where(lane == 0, 0.0, shift(here, 1))
                    + jnp.where(lane == COLS - 1, 0.0, shift(here, -1))
                )
                value = (
                    coef * near
                    + above_coef * pltpu.roll(here, LEVELS - 1, 0)
                    + below_coef * pltpu.roll(here, 1, 0)
                )
                if i == 0 and source is not None:
                    value = value + source[r]
                flow[r, i] = value
            before, now = now, after

    def completed(k):
        first_cols, last_cols = halo_we[k, 1, 0], shift(halo_we[k, 0, 0], 2)
        pair = (
            coef * jnp.where(is_even, first_cols, last_cols),
            coef * jnp.where(is_even, last_cols, first_cols),
        )

        def rows(r, i):
            value = flow[r, i] + jnp.where(on_edge, shift(pair[r & 1], COLS - 1 - i * ROWS - r), 0.0)
            if r == 0:
                value = value + coef * halo_ns[k, 0, i]
            if r == ROWS - 1:
                value = value + coef * halo_ns[k, 1, i]
            return value

        return rows

    def send_edges(k, par, even, odd):
        above = [coef * halo_ns[k, 0, i] for i in range(3)]
        below = [coef * halo_ns[k, 1, i] for i in range(3)]
        last, first = coef * halo_we[k, 0, 0], coef * halo_we[k, 1, 0]
        for i in range(3):
            even = even + shift(jnp.where(on_edge, above[i], 0.0), i * ROWS)
            odd = odd + shift(jnp.where(on_edge, below[i], 0.0), i * ROWS + ROWS - 1)
        send_we[k + 1, 0, 0] = jnp.where(is_even, even, odd) + shift(last, 1)
        send_we[k + 1, 1, 0] = jnp.where(is_even, odd, even) + shift(first, -1)
        for own, r, halo in ((0, 0, above), (1, ROWS - 1, below)):
            for i in range(3):
                t = i * ROWS + r
                send_ns[k + 1, own, i] = (
                    flow[r, i]
                    + halo[i]
                    + jnp.where(lane == 0, shift(last, 1 - t), 0.0)
                    + jnp.where(lane == COLS - 1, shift(first, COLS - 1 - t), 0.0)
                )
        send_inside(k + 1, par, False)

        def patch(values, index):
            at_row, at_col = index >> 7, index & (COLS - 1)
            for i in range(3):
                slot = i * ROWS + at_row
                add = jnp.where(at_row == 0, lane_take(above[i], at_col), 0.0)
                add = add + jnp.where(at_row == ROWS - 1, lane_take(below[i], at_col), 0.0)
                add = add + jnp.where(at_col == 0, lane_take(last, (slot - 1) & (COLS - 1)), 0.0)
                add = add + jnp.where(at_col == COLS - 1, lane_take(first, slot), 0.0)
                values[i] = values[i] + add
            return values

        send_found(k + 1, par, False, patch)

    relax(first_row)
    wait_all(0, 0, True)

    def wide_row(r):
        if r < 0:
            return halo_ns[0, 0, 5 + r]
        if r >= ROWS:
            return halo_ns[0, 1, 3 + r - ROWS]
        return heat_row(r)

    around = jnp.where((lane & 3) < 2, halo_we[0, 1, 1], halo_we[0, 0, 1])
    window = [wide_row(r) for r in range(-2, 2)]
    for r in range(ROWS):
        window.append(wide_row(r + 2))
        up2, up1, here, down1, down2 = window[r : r + 5]
        rim = shift(around, -4 * r)
        west1 = shift(jnp.where(lane == COLS - 1, rim, here), 1)
        west2 = shift(jnp.where(lane >= COLS - 2, rim, here), 2)
        east1 = shift(jnp.where(lane == 0, rim, here), -1)
        east2 = shift(jnp.where(lane < 2, rim, here), -2)
        above = jnp.where(level == LEVELS - 1, here, pltpu.roll(here, LEVELS - 1, 0))
        below = jnp.where(level == 0, here, pltpu.roll(here, 1, 0))
        grad_colat = (8.0 * (down1 - up1) - (down2 - up2)) * (1.0 / 12.0)
        grad_lon = (8.0 * (east1 - west1) - (east2 - west2)) * (1.0 / 12.0)
        grad_rad = (above - below) * 0.5
        laplace = down1 + up1 + east1 + west1 + above + below - 6.0 * here
        advect = first_row(r, 0) * grad_rad + first_row(r, 1) * grad_colat + first_row(r, 2) * grad_lon
        stepped = here + TIME_STEP * (laplace - advect)
        heat_out[pl.ds(r, LEVELS, stride=ROWS), :] = stepped
        source[r] = buoyancy * stepped
        flow[r, 0] = flow[r, 0] + source[r]
    heat_copy = pltpu.make_async_copy(heat_out, heat_done, out_sem.at[3])
    heat_copy.start()

    even, odd = pack_all(flow_row)
    find(flow_row)
    send_edges(0, 1, even, odd)

    def step(k, carry):
        par = k & 1
        relax(completed(k - 1), source)
        even, odd = pack_all(flow_row)
        find(flow_row)
        wait_all(k, par, False)

        @pl.when(k > 1)
        def _():
            wait_sent(k - 1, 1 - par, False)

        send_edges(k, 1 - par, even, odd)
        return carry

    wait_sent(0, 0, True)
    lax.fori_loop(1, ITERS - 1, step, 0)
    relax(completed(ITERS - 2), source)
    last_par = (ITERS - 1) & 1
    wait_all(ITERS - 1, last_par, False)
    rows = completed(ITERS - 1)
    results = []
    for i in range(3):
        for r in range(ROWS):
            flow_out[pl.ds(i * LEVELS * ROWS + r, LEVELS, stride=ROWS), :] = rows(r, i)
        span = pl.ds(i * LEVELS * ROWS, LEVELS * ROWS)
        results.append(pltpu.make_async_copy(flow_out.at[span], flow_done.at[span], out_sem.at[i]))
        results[-1].start()
    wait_sent(ITERS - 2, 1 - last_par, False)
    wait_sent(ITERS - 1, last_par, False)
    heat_copy.wait()
    for result in results:
        result.wait()


def deliver(heat_in, flow_in, heat_out, flow_out, heat, flow, sem):
    size = LEVELS * ROWS
    pieces = [(heat_in, heat, heat_out, pl.ds(0, size))]
    pieces += [(flow_in, flow, flow_out, pl.ds(i * size, size)) for i in range(3)]
    into = [
        pltpu.make_async_copy(src.at[span], held.at[span], sem.at[0, n])
        for n, (src, held, _, span) in enumerate(pieces)
    ]
    out = [
        pltpu.make_async_copy(held.at[span], dst.at[span], sem.at[1, n])
        for n, (_, held, dst, span) in enumerate(pieces)
    ]
    for copy in into:
        copy.start()
    for first, second in zip(into, out):
        first.wait()
        second.start()
    for copy in out:
        copy.wait()


def solution(mesh):
    n_colat, n_lon = mesh.shape["colat"], mesh.shape["lon"]

    block = (LEVELS, COLS)
    heat_shape = jax.ShapeDtypeStruct((LEVELS * ROWS, COLS), jnp.float32)
    flow_shape = jax.ShapeDtypeStruct((3 * LEVELS * ROWS, COLS), jnp.float32)
    anywhere = pl.BlockSpec(memory_space=pl.ANY)
    step = pl.pallas_call(
        lambda *refs: kernel(n_colat, n_lon, *refs),
        out_shape=(heat_shape, flow_shape),
        in_specs=[anywhere] * 5,
        out_specs=(anywhere, anywhere),
        scratch_shapes=[
            pltpu.VMEM(heat_shape.shape, jnp.float32),
            pltpu.VMEM(flow_shape.shape, jnp.float32),
            pltpu.SMEM((LEVELS,), jnp.float32),
            pltpu.VMEM((1, 1, 4 * (COLS + ROWS)), jnp.int32),
            pltpu.VMEM((1, 1, 2 * (COLS + ROWS)), jnp.float32),
            pltpu.VMEM(heat_shape.shape, jnp.float32),
            pltpu.VMEM(flow_shape.shape, jnp.float32),
            pltpu.SemaphoreType.DMA((5,)),
            pltpu.SemaphoreType.DMA((4,)),
            pltpu.VMEM((ROWS, 3, *block), jnp.float32),
            pltpu.VMEM((ROWS, *block), jnp.float32),
            pltpu.VMEM((10, *block), jnp.float32),
            pltpu.VMEM((ITERS, 2, 5, *block), jnp.float32),
            pltpu.VMEM((ITERS, 2, 2, *block), jnp.float32),
            pltpu.VMEM((ITERS, 2, 5, *block), jnp.float32),
            pltpu.VMEM((ITERS, 2, 2, *block), jnp.float32),
            pltpu.SemaphoreType.DMA((2, 4)),
            pltpu.SemaphoreType.DMA((2, 4)),
        ],
        compiler_params=pltpu.CompilerParams(collective_id=0, has_side_effects=True, vmem_limit_bytes=8 << 20),
        name="mantle_step",
    )
    place = pl.pallas_call(
        deliver,
        out_shape=(heat_shape, flow_shape),
        in_specs=[anywhere] * 2,
        out_specs=(anywhere, anywhere),
        scratch_shapes=[
            pltpu.VMEM(heat_shape.shape, jnp.float32),
            pltpu.VMEM(flow_shape.shape, jnp.float32),
            pltpu.SemaphoreType.DMA((2, 4)),
        ],
        compiler_params=pltpu.CompilerParams(vmem_limit_bytes=4 << 20),
        name="deliver",
    )

    def on_device(heat, flow, stiffness, site, phase):
        heat_out, flow_out = place(
            *step(
                heat.reshape(heat_shape.shape), flow.reshape(flow_shape.shape), stiffness, site, phase
            )
        )
        return heat_out.reshape(heat.shape), flow_out.reshape(flow.shape)

    return jax.shard_map(
        on_device,
        mesh=mesh,
        in_specs=(
            P("panel", None, "colat", "lon"),
            P("panel", None, None, "colat", "lon"),
            P(),
            P("panel", "colat", "lon"),
            P("panel", "colat", "lon"),
        ),
        out_specs=(P("panel", None, "colat", "lon"), P("panel", None, None, "colat", "lon")),
        check_vma=False,
    )
```

```python
import jax
import jax.numpy as jnp
from jax import lax
from jax.experimental import pallas as pl
from jax.experimental.pallas import tpu as pltpu
from jax.sharding import PartitionSpec as P

ITERS = 8
TIME_STEP = 0.1
BUOYANCY_FACTOR = 10.0
DRAG_COEF = 1.0
MESH = pl.DeviceIdType.MESH
LEVELS, ROWS, COLS = 8, 32, 128


def lane_take(value, index):
    return jnp.take_along_axis(value, index, axis=1, mode="promise_in_bounds")


def kernel(
    n_colat, n_lon,
    heat_hbm, flow_hbm, stiff_hbm, site_hbm, phase_hbm,
    heat_done, flow_done,
    heat_in, flow_in, stiff_in, site_in, phase_in, heat_out, flow_out, in_sem, out_sem,
    flow, source, found, send_ns, send_we, halo_ns, halo_we, send_sem, recv_sem,
):
    p, c, l = (lax.axis_index(a) for a in ("panel", "colat", "lon"))
    lane = lax.broadcasted_iota(jnp.int32, (LEVELS, COLS), 1)
    level = lax.broadcasted_iota(jnp.int32, (LEVELS, COLS), 0)
    north, south = (c == 0).astype(jnp.int32), (c == n_colat - 1).astype(jnp.int32)
    west, east = (l == 0).astype(jnp.int32), (l == n_lon - 1).astype(jnp.int32)
    at_rim = (north, south, west, east)

    def across(edge):
        return p + edge * (1 - 2 * p)

    sides = (
        ((across(north), c - 1 + north, l), 1 - north),
        ((across(south), c + 1 - south, l), south),
        ((across(west), c, l - 1 + west), 3 - west),
        ((across(east), c, l + 1 - east), 2 + east),
    )
    barrier = pltpu.get_barrier_semaphore()
    for device, _ in sides:
        pl.semaphore_signal(barrier, inc=1, device_id=device, device_id_type=MESH)
    inputs = [
        pltpu.make_async_copy(src, dst, in_sem.at[n])
        for n, (src, dst) in enumerate(
            (
                (stiff_hbm, stiff_in),
                (site_hbm, site_in),
                (phase_hbm, phase_in),
                (flow_hbm, flow_in),
                (heat_hbm, heat_in),
            )
        )
    ]
    for n in (3, 4, 0, 1, 2):
        inputs[n].start()
    for n in (0, 1, 2):
        inputs[n].wait()

    stiff = jnp.zeros((LEVELS, COLS), jnp.float32)
    for k in range(LEVELS):
        stiff = jnp.where(level == k, stiff_in[k], stiff)
    upper = jnp.where(level < LEVELS - 1, 0.5 * (stiff + pltpu.roll(stiff, LEVELS - 1, 0)), 0.0)
    lower = jnp.where(level > 0, 0.5 * (stiff + pltpu.roll(stiff, 1, 0)), 0.0)
    inverse = 1.0 / (DRAG_COEF + 4.0 * stiff + upper + lower)
    coef, above_coef, below_coef = stiff * inverse, upper * inverse, lower * inverse
    buoyancy = BUOYANCY_FACTOR * inverse

    zero = jnp.zeros((LEVELS, COLS), jnp.float32)
    is_even = (lane & 1) == 0
    on_edge = (lane == 0) | (lane == COLS - 1)

    def shift(value, by):
        return pltpu.roll(value, by % COLS, 1)

    def pick(flag, yes, no):
        return jnp.where(flag == 1, yes, no)

    slot = (lane + west) & (COLS - 1)
    slot_row, slot_part = slot & (ROWS - 1), slot >> 5
    heat_slot = (lane + 2 * west) & (COLS - 1)

    def sites(j):
        return jnp.broadcast_to(site_in[0, 0:1, COLS * j : COLS * (j + 1)], (LEVELS, COLS))

    ns_site = pick(north, sites(1), sites(2))
    ns_heat = (pick(north, sites(0), sites(2)), pick(north, sites(1), sites(3)))
    we_base = pick(west, 0, 2 * ROWS)
    we_site = lane_take(sites(4), we_base + west + 2 * slot_row)
    we_heat = lane_take(sites(4), we_base + 2 * (heat_slot >> 2) + (heat_slot & 1))
    ns_angle = jnp.broadcast_to(
        pick(north, phase_in[0, 0:1, 0:COLS], phase_in[0, 0:1, COLS : 2 * COLS]), (LEVELS, COLS)
    )
    tail = phase_in[0, 0:1, 2 * COLS : 2 * COLS + 2 * ROWS]
    tail = jnp.broadcast_to(jnp.concatenate([tail, tail], axis=1), (LEVELS, COLS))
    we_angle = lane_take(tail, pick(west, 0, ROWS) + slot_row)

    def heat_row(r):
        return heat_in[pl.ds(r, LEVELS, stride=ROWS), :]

    def collect(index, rows, count):
        at_row, at_col = index >> 7, index & (COLS - 1)
        values = [zero] * count
        for r in range(ROWS):
            here = at_row == r
            values = [
                jnp.where(here, lane_take(rows(r, i), at_col), v) for i, v in enumerate(values)
            ]
        return values

    def flow_row(r, i):
        return flow[r, i]

    def copy(k, par, first, side, arriving=False):
        device, facing = sides[side]
        ns = side < 2
        buf, halo = (send_ns, halo_ns) if ns else (send_we, halo_we)
        own, theirs = (side, facing) if ns else (side - 2, facing - 2)
        n = (5 if first else 3) if ns else (2 if first else 1)

        at, seen = (own, side) if arriving else (theirs, facing)
        return pltpu.make_async_remote_copy(
            src_ref=buf.at[k, own, 0:n],
            dst_ref=halo.at[k, at, 0:n],
            send_sem=send_sem.at[par, side],
            recv_sem=recv_sem.at[par, seen],
            device_id=device,
            device_id_type=MESH,
        )

    def on_rim(flag_a, flag_b):
        return pl.when((flag_a == 1) | (flag_b == 1))

    def start(k, par, first, side):
        copy(k, par, first, side).start()

    def wait_all(k, par, first):
        for side in range(4):
            copy(k, par, first, side, arriving=True).wait_recv()

    def wait_sent(k, par, first):
        for side in range(4):
            copy(k, par, first, side).wait_send()

    def pack_all(rows):
        packed = [[zero, zero], [zero, zero]]
        for r in range(ROWS):
            for i in range(3):
                part = shift(jnp.where(on_edge, rows(r, i), 0.0), i * ROWS + r)
                packed[r & 1][(r >> 1) & 1] = packed[r & 1][(r >> 1) & 1] + part
        return packed[0][0] + packed[0][1], packed[1][0] + packed[1][1]

    def find(rows):
        @on_rim(north, south)
        def _():
            for i, v in enumerate(collect(ns_site, rows, 3)):
                found[i] = v

        @on_rim(west, east)
        def _():
            for i, v in enumerate(collect(we_site, rows, 3)):
                found[3 + i] = v

    def rotated(values, angle):
        a, b, d = values
        cos, sin = found[angle], found[angle + 1]
        return a, cos * b + sin * d, cos * d - sin * b

    def send_found(k, par, first, patch):
        @on_rim(north, south)
        def _():
            values = patch([found[i] for i in range(3)], ns_site)
            for i, v in enumerate(rotated(values, 6)):
                send_ns[k, south, i] = v

            @pl.when(north == 1)
            def _():
                start(k, par, first, 0)

            @pl.when(south == 1)
            def _():
                start(k, par, first, 1)

        @on_rim(west, east)
        def _():
            values = patch([found[3 + i] for i in range(3)], we_site)
            a, b, d = rotated(values, 8)
            send_we[k, east, 0] = jnp.where(slot_part == 0, a, jnp.where(slot_part == 1, b, d))

            @pl.when(west == 1)
            def _():
                start(k, par, first, 2)

            @pl.when(east == 1)
            def _():
                start(k, par, first, 3)

    def send_inside(k, par, first):
        for side in (2, 3, 0, 1):

            @pl.when(at_rim[side] == 0)
            def _(side=side):
                start(k, par, first, side)

    def first_row(r, i):
        return flow_in[pl.ds(i * LEVELS * ROWS + r, LEVELS, stride=ROWS), :]

    @on_rim(north, south)
    def _():
        found[6], found[7] = jnp.cos(ns_angle), jnp.sin(ns_angle)

    @on_rim(west, east)
    def _():
        found[8], found[9] = jnp.cos(we_angle), jnp.sin(we_angle)

    inputs[3].wait()
    even, odd = pack_all(first_row)
    inputs[4].wait()
    near_edge = (lane < 2) | (lane >= COLS - 2)
    heat_packed = [zero, zero]
    for r in range(ROWS):
        part = shift(jnp.where(near_edge, heat_row(r), 0.0), 4 * r)
        heat_packed[r & 1] = heat_packed[r & 1] + part
    heat_packed = heat_packed[0] + heat_packed[1]
    for j in range(2):
        send_ns[0, 0, 3 + j] = heat_row(j)
        send_ns[0, 1, 3 + j] = heat_row(ROWS - 2 + j)
        send_we[0, j, 1] = heat_packed
    for i in range(3):
        send_ns[0, 0, i] = first_row(0, i)
        send_ns[0, 1, i] = first_row(ROWS - 1, i)
    send_we[0, 0, 0] = jnp.where(is_even, even, odd)
    send_we[0, 1, 0] = jnp.where(is_even, odd, even)

    pl.semaphore_wait(barrier, 4)
    send_inside(0, 0, True)

    @on_rim(north, south)
    def _():
        for j in range(2):
            send_ns[0, south, 3 + j] = collect(ns_heat[j], lambda r, _: heat_row(r), 1)[0]

    @on_rim(west, east)
    def _():
        send_we[0, east, 1] = collect(we_heat, lambda r, _: heat_row(r), 1)[0]

    find(first_row)
    send_found(0, 0, True, lambda values, index: values)

    def relax(rows, source=None):
        before = [zero] * 3
        now = [rows(0, i) for i in range(3)]
        for r in range(ROWS):
            after = [rows(r + 1, i) for i in range(3)] if r < ROWS - 1 else [zero] * 3
            for i in range(3):
                here = now[i]
                near = (
                    (before[i] + after[i])
                    + jnp.where(lane == 0, 0.0, shift(here, 1))
                    + jnp.where(lane == COLS - 1, 0.0, shift(here, -1))
                )
                value = (
                    coef * near
                    + above_coef * pltpu.roll(here, LEVELS - 1, 0)
                    + below_coef * pltpu.roll(here, 1, 0)
                )
                if i == 0 and source is not None:
                    value = value + source[r]
                flow[r, i] = value
            before, now = now, after

    def completed(k):
        first_cols, last_cols = halo_we[k, 1, 0], shift(halo_we[k, 0, 0], 2)
        pair = (
            coef * jnp.where(is_even, first_cols, last_cols),
            coef * jnp.where(is_even, last_cols, first_cols),
        )

        def rows(r, i):
            value = flow[r, i] + jnp.where(on_edge, shift(pair[r & 1], COLS - 1 - i * ROWS - r), 0.0)
            if r == 0:
                value = value + coef * halo_ns[k, 0, i]
            if r == ROWS - 1:
                value = value + coef * halo_ns[k, 1, i]
            return value

        return rows

    def send_edges(k, par, even, odd):
        above = [coef * halo_ns[k, 0, i] for i in range(3)]
        below = [coef * halo_ns[k, 1, i] for i in range(3)]
        last, first = coef * halo_we[k, 0, 0], coef * halo_we[k, 1, 0]
        for i in range(3):
            even = even + shift(jnp.where(on_edge, above[i], 0.0), i * ROWS)
            odd = odd + shift(jnp.where(on_edge, below[i], 0.0), i * ROWS + ROWS - 1)
        send_we[k + 1, 0, 0] = jnp.where(is_even, even, odd) + shift(last, 1)
        send_we[k + 1, 1, 0] = jnp.where(is_even, odd, even) + shift(first, -1)
        for own, r, halo in ((0, 0, above), (1, ROWS - 1, below)):
            for i in range(3):
                t = i * ROWS + r
                send_ns[k + 1, own, i] = (
                    flow[r, i]
                    + halo[i]
                    + jnp.where(lane == 0, shift(last, 1 - t), 0.0)
                    + jnp.where(lane == COLS - 1, shift(first, COLS - 1 - t), 0.0)
                )
        send_inside(k + 1, par, False)

        def patch(values, index):
            at_row, at_col = index >> 7, index & (COLS - 1)
            for i in range(3):
                slot = i * ROWS + at_row
                add = jnp.where(at_row == 0, lane_take(above[i], at_col), 0.0)
                add = add + jnp.where(at_row == ROWS - 1, lane_take(below[i], at_col), 0.0)
                add = add + jnp.where(at_col == 0, lane_take(last, (slot - 1) & (COLS - 1)), 0.0)
                add = add + jnp.where(at_col == COLS - 1, lane_take(first, slot), 0.0)
                values[i] = values[i] + add
            return values

        send_found(k + 1, par, False, patch)

    relax(first_row)
    wait_all(0, 0, True)

    def wide_row(r):
        if r < 0:
            return halo_ns[0, 0, 5 + r]
        if r >= ROWS:
            return halo_ns[0, 1, 3 + r - ROWS]
        return heat_row(r)

    around = jnp.where((lane & 3) < 2, halo_we[0, 1, 1], halo_we[0, 0, 1])
    window = [wide_row(r) for r in range(-2, 2)]
    for r in range(ROWS):
        window.append(wide_row(r + 2))
        up2, up1, here, down1, down2 = window[r : r + 5]
        rim = shift(around, -4 * r)
        west1 = shift(jnp.where(lane == COLS - 1, rim, here), 1)
        west2 = shift(jnp.where(lane >= COLS - 2, rim, here), 2)
        east1 = shift(jnp.where(lane == 0, rim, here), -1)
        east2 = shift(jnp.where(lane < 2, rim, here), -2)
        above = jnp.where(level == LEVELS - 1, here, pltpu.roll(here, LEVELS - 1, 0))
        below = jnp.where(level == 0, here, pltpu.roll(here, 1, 0))
        grad_colat = (8.0 * (down1 - up1) - (down2 - up2)) * (1.0 / 12.0)
        grad_lon = (8.0 * (east1 - west1) - (east2 - west2)) * (1.0 / 12.0)
        grad_rad = (above - below) * 0.5
        laplace = down1 + up1 + east1 + west1 + above + below - 6.0 * here
        advect = first_row(r, 0) * grad_rad + first_row(r, 1) * grad_colat + first_row(r, 2) * grad_lon
        stepped = here + TIME_STEP * (laplace - advect)
        heat_out[pl.ds(r, LEVELS, stride=ROWS), :] = stepped
        source[r] = buoyancy * stepped
        flow[r, 0] = flow[r, 0] + source[r]
    heat_copy = pltpu.make_async_copy(heat_out, heat_done, out_sem.at[3])
    heat_copy.start()

    even, odd = pack_all(flow_row)
    find(flow_row)
    send_edges(0, 1, even, odd)

    def step(k, carry):
        par = k & 1
        relax(completed(k - 1), source)
        even, odd = pack_all(flow_row)
        find(flow_row)
        wait_all(k, par, False)

        @pl.when(k > 1)
        def _():
            wait_sent(k - 1, 1 - par, False)

        send_edges(k, 1 - par, even, odd)
        return carry

    wait_sent(0, 0, True)
    lax.fori_loop(1, ITERS - 1, step, 0)
    relax(completed(ITERS - 2), source)
    last_par = (ITERS - 1) & 1
    wait_all(ITERS - 1, last_par, False)
    rows = completed(ITERS - 1)
    results = []
    for i in range(3):
        for r in range(ROWS):
            flow_out[pl.ds(i * LEVELS * ROWS + r, LEVELS, stride=ROWS), :] = rows(r, i)
        span = pl.ds(i * LEVELS * ROWS, LEVELS * ROWS)
        results.append(pltpu.make_async_copy(flow_out.at[span], flow_done.at[span], out_sem.at[i]))
        results[-1].start()
    wait_sent(ITERS - 2, 1 - last_par, False)
    wait_sent(ITERS - 1, last_par, False)
    heat_copy.wait()
    for result in results:
        result.wait()


def deliver(heat_in, flow_in, heat_out, flow_out, sem):
    copies = [
        pltpu.make_async_copy(heat_in, heat_out, sem.at[0]),
        pltpu.make_async_copy(flow_in, flow_out, sem.at[1]),
    ]
    for copy in copies:
        copy.start()
    for copy in copies:
        copy.wait()


def solution(mesh):
    n_colat, n_lon = mesh.shape["colat"], mesh.shape["lon"]

    block = (LEVELS, COLS)
    heat_shape = jax.ShapeDtypeStruct((LEVELS * ROWS, COLS), jnp.float32)
    flow_shape = jax.ShapeDtypeStruct((3 * LEVELS * ROWS, COLS), jnp.float32)
    anywhere = pl.BlockSpec(memory_space=pl.ANY)
    step = pl.pallas_call(
        lambda *refs: kernel(n_colat, n_lon, *refs),
        out_shape=(heat_shape, flow_shape),
        in_specs=[pl.BlockSpec(memory_space=pltpu.HBM)] * 5,
        out_specs=(anywhere, anywhere),
        scratch_shapes=[
            pltpu.VMEM(heat_shape.shape, jnp.float32),
            pltpu.VMEM(flow_shape.shape, jnp.float32),
            pltpu.SMEM((LEVELS,), jnp.float32),
            pltpu.VMEM((1, 1, 4 * (COLS + ROWS)), jnp.int32),
            pltpu.VMEM((1, 1, 2 * (COLS + ROWS)), jnp.float32),
            pltpu.VMEM(heat_shape.shape, jnp.float32),
            pltpu.VMEM(flow_shape.shape, jnp.float32),
            pltpu.SemaphoreType.DMA((5,)),
            pltpu.SemaphoreType.DMA((4,)),
            pltpu.VMEM((ROWS, 3, *block), jnp.float32),
            pltpu.VMEM((ROWS, *block), jnp.float32),
            pltpu.VMEM((10, *block), jnp.float32),
            pltpu.VMEM((ITERS, 2, 5, *block), jnp.float32),
            pltpu.VMEM((ITERS, 2, 2, *block), jnp.float32),
            pltpu.VMEM((ITERS, 2, 5, *block), jnp.float32),
            pltpu.VMEM((ITERS, 2, 2, *block), jnp.float32),
            pltpu.SemaphoreType.DMA((2, 4)),
            pltpu.SemaphoreType.DMA((2, 4)),
        ],
        compiler_params=pltpu.CompilerParams(collective_id=0, has_side_effects=True, vmem_limit_bytes=8 << 20),
        name="mantle_step",
    )
    place = pl.pallas_call(
        deliver,
        out_shape=(heat_shape, flow_shape),
        in_specs=[anywhere] * 2,
        out_specs=(pl.BlockSpec(memory_space=pltpu.HBM),) * 2,
        scratch_shapes=[pltpu.SemaphoreType.DMA((2,))],
        compiler_params=pltpu.CompilerParams(vmem_limit_bytes=4 << 20),
        name="deliver",
    )

    def on_device(heat, flow, stiffness, site, phase):
        heat_out, flow_out = place(
            *step(
                heat.reshape(heat_shape.shape), flow.reshape(flow_shape.shape), stiffness, site, phase
            )
        )
        return heat_out.reshape(heat.shape), flow_out.reshape(flow.shape)

    return jax.shard_map(
        on_device,
        mesh=mesh,
        in_specs=(
            P("panel", None, "colat", "lon"),
            P("panel", None, None, "colat", "lon"),
            P(),
            P("panel", "colat", "lon"),
            P("panel", "colat", "lon"),
        ),
        out_specs=(P("panel", None, "colat", "lon"), P("panel", None, None, "colat", "lon")),
        check_vma=False,
    )
```

```python
import jax
import jax.numpy as jnp
from jax import lax
from jax.experimental import pallas as pl
from jax.experimental.pallas import tpu as pltpu
from jax.sharding import PartitionSpec as P

ITERS = 8
TIME_STEP = 0.1
BUOYANCY_FACTOR = 10.0
DRAG_COEF = 1.0
MESH = pl.DeviceIdType.MESH
LEVELS, ROWS, COLS = 8, 32, 128


def lane_take(value, index):
    return jnp.take_along_axis(value, index, axis=1, mode="promise_in_bounds")


def kernel(
    n_colat, n_lon,
    heat_hbm, flow_hbm, stiff_hbm, site_hbm, phase_hbm,
    heat_done, flow_done,
    heat_in, flow_in, stiff_in, site_in, phase_in, heat_out, flow_out, in_sem, out_sem,
    flow, source, found, send_ns, send_we, halo_ns, halo_we, send_sem, recv_sem,
):
    p, c, l = (lax.axis_index(a) for a in ("panel", "colat", "lon"))
    lane = lax.broadcasted_iota(jnp.int32, (LEVELS, COLS), 1)
    level = lax.broadcasted_iota(jnp.int32, (LEVELS, COLS), 0)
    north, south = (c == 0).astype(jnp.int32), (c == n_colat - 1).astype(jnp.int32)
    west, east = (l == 0).astype(jnp.int32), (l == n_lon - 1).astype(jnp.int32)
    at_rim = (north, south, west, east)

    def across(edge):
        return p + edge * (1 - 2 * p)

    sides = (
        ((across(north), c - 1 + north, l), 1 - north),
        ((across(south), c + 1 - south, l), south),
        ((across(west), c, l - 1 + west), 3 - west),
        ((across(east), c, l + 1 - east), 2 + east),
    )
    barrier = pltpu.get_barrier_semaphore()
    for device, _ in sides:
        pl.semaphore_signal(barrier, inc=1, device_id=device, device_id_type=MESH)
    inputs = [
        pltpu.make_async_copy(src, dst, in_sem.at[n])
        for n, (src, dst) in enumerate(
            (
                (stiff_hbm, stiff_in),
                (site_hbm, site_in),
                (phase_hbm, phase_in),
                (flow_hbm, flow_in),
                (heat_hbm, heat_in),
            )
        )
    ]
    for n in (3, 4, 0, 1, 2):
        inputs[n].start()
    for n in (0, 1, 2):
        inputs[n].wait()

    stiff = jnp.zeros((LEVELS, COLS), jnp.float32)
    for k in range(LEVELS):
        stiff = jnp.where(level == k, stiff_in[k], stiff)
    upper = jnp.where(level < LEVELS - 1, 0.5 * (stiff + pltpu.roll(stiff, LEVELS - 1, 0)), 0.0)
    lower = jnp.where(level > 0, 0.5 * (stiff + pltpu.roll(stiff, 1, 0)), 0.0)
    inverse = 1.0 / (DRAG_COEF + 4.0 * stiff + upper + lower)
    coef, above_coef, below_coef = stiff * inverse, upper * inverse, lower * inverse
    buoyancy = BUOYANCY_FACTOR * inverse

    zero = jnp.zeros((LEVELS, COLS), jnp.float32)
    is_even = (lane & 1) == 0
    on_edge = (lane == 0) | (lane == COLS - 1)

    def shift(value, by):
        return pltpu.roll(value, by % COLS, 1)

    def pick(flag, yes, no):
        return jnp.where(flag == 1, yes, no)

    slot = (lane + west) & (COLS - 1)
    slot_row, slot_part = slot & (ROWS - 1), slot >> 5
    heat_slot = (lane + 2 * west) & (COLS - 1)

    def sites(j):
        return jnp.broadcast_to(site_in[0, 0:1, COLS * j : COLS * (j + 1)], (LEVELS, COLS))

    ns_site = pick(north, sites(1), sites(2))
    ns_heat = (pick(north, sites(0), sites(2)), pick(north, sites(1), sites(3)))
    we_base = pick(west, 0, 2 * ROWS)
    we_site = lane_take(sites(4), we_base + west + 2 * slot_row)
    we_heat = lane_take(sites(4), we_base + 2 * (heat_slot >> 2) + (heat_slot & 1))
    ns_angle = jnp.broadcast_to(
        pick(north, phase_in[0, 0:1, 0:COLS], phase_in[0, 0:1, COLS : 2 * COLS]), (LEVELS, COLS)
    )
    tail = phase_in[0, 0:1, 2 * COLS : 2 * COLS + 2 * ROWS]
    tail = jnp.broadcast_to(jnp.concatenate([tail, tail], axis=1), (LEVELS, COLS))
    we_angle = lane_take(tail, pick(west, 0, ROWS) + slot_row)

    def heat_row(r):
        return heat_in[pl.ds(r, LEVELS, stride=ROWS), :]

    def collect(index, rows, count):
        at_row, at_col = index >> 7, index & (COLS - 1)
        values = [zero] * count
        for r in range(ROWS):
            here = at_row == r
            values = [
                jnp.where(here, lane_take(rows(r, i), at_col), v) for i, v in enumerate(values)
            ]
        return values

    def flow_row(r, i):
        return flow[r, i]

    def copy(k, par, first, side, arriving=False):
        device, facing = sides[side]
        ns = side < 2
        buf, halo = (send_ns, halo_ns) if ns else (send_we, halo_we)
        own, theirs = (side, facing) if ns else (side - 2, facing - 2)
        n = (5 if first else 3) if ns else (2 if first else 1)

        at, seen = (own, side) if arriving else (theirs, facing)
        return pltpu.make_async_remote_copy(
            src_ref=buf.at[k, own, 0:n],
            dst_ref=halo.at[k, at, 0:n],
            send_sem=send_sem.at[par, side],
            recv_sem=recv_sem.at[par, seen],
            device_id=device,
            device_id_type=MESH,
        )

    def on_rim(flag_a, flag_b):
        return pl.when((flag_a == 1) | (flag_b == 1))

    def start(k, par, first, side):
        copy(k, par, first, side).start()

    def wait_all(k, par, first):
        for side in range(4):
            copy(k, par, first, side, arriving=True).wait_recv()

    def wait_sent(k, par, first):
        for side in range(4):
            copy(k, par, first, side).wait_send()

    def pack_all(rows):
        packed = [[zero, zero], [zero, zero]]
        for r in range(ROWS):
            for i in range(3):
                part = shift(jnp.where(on_edge, rows(r, i), 0.0), i * ROWS + r)
                packed[r & 1][(r >> 1) & 1] = packed[r & 1][(r >> 1) & 1] + part
        return packed[0][0] + packed[0][1], packed[1][0] + packed[1][1]

    def find(rows):
        @on_rim(north, south)
        def _():
            for i, v in enumerate(collect(ns_site, rows, 3)):
                found[i] = v

        @on_rim(west, east)
        def _():
            for i, v in enumerate(collect(we_site, rows, 3)):
                found[3 + i] = v

    def rotated(values, angle):
        a, b, d = values
        cos, sin = found[angle], found[angle + 1]
        return a, cos * b + sin * d, cos * d - sin * b

    def send_found(k, par, first, patch):
        @on_rim(north, south)
        def _():
            values = patch([found[i] for i in range(3)], ns_site)
            for i, v in enumerate(rotated(values, 6)):
                send_ns[k, south, i] = v

            @pl.when(north == 1)
            def _():
                start(k, par, first, 0)

            @pl.when(south == 1)
            def _():
                start(k, par, first, 1)

        @on_rim(west, east)
        def _():
            values = patch([found[3 + i] for i in range(3)], we_site)
            a, b, d = rotated(values, 8)
            send_we[k, east, 0] = jnp.where(slot_part == 0, a, jnp.where(slot_part == 1, b, d))

            @pl.when(west == 1)
            def _():
                start(k, par, first, 2)

            @pl.when(east == 1)
            def _():
                start(k, par, first, 3)

    def send_inside(k, par, first):
        for side in (2, 3, 0, 1):

            @pl.when(at_rim[side] == 0)
            def _(side=side):
                start(k, par, first, side)

    def first_row(r, i):
        return flow_in[pl.ds(i * LEVELS * ROWS + r, LEVELS, stride=ROWS), :]

    @on_rim(north, south)
    def _():
        found[6], found[7] = jnp.cos(ns_angle), jnp.sin(ns_angle)

    @on_rim(west, east)
    def _():
        found[8], found[9] = jnp.cos(we_angle), jnp.sin(we_angle)

    inputs[3].wait()
    even, odd = pack_all(first_row)
    inputs[4].wait()
    near_edge = (lane < 2) | (lane >= COLS - 2)
    heat_packed = [zero, zero]
    for r in range(ROWS):
        part = shift(jnp.where(near_edge, heat_row(r), 0.0), 4 * r)
        heat_packed[r & 1] = heat_packed[r & 1] + part
    heat_packed = heat_packed[0] + heat_packed[1]
    for j in range(2):
        send_ns[0, 0, 3 + j] = heat_row(j)
        send_ns[0, 1, 3 + j] = heat_row(ROWS - 2 + j)
        send_we[0, j, 1] = heat_packed
    for i in range(3):
        send_ns[0, 0, i] = first_row(0, i)
        send_ns[0, 1, i] = first_row(ROWS - 1, i)
    send_we[0, 0, 0] = jnp.where(is_even, even, odd)
    send_we[0, 1, 0] = jnp.where(is_even, odd, even)

    pl.semaphore_wait(barrier, 4)
    send_inside(0, 0, True)

    @on_rim(north, south)
    def _():
        for j in range(2):
            send_ns[0, south, 3 + j] = collect(ns_heat[j], lambda r, _: heat_row(r), 1)[0]

    @on_rim(west, east)
    def _():
        send_we[0, east, 1] = collect(we_heat, lambda r, _: heat_row(r), 1)[0]

    find(first_row)
    send_found(0, 0, True, lambda values, index: values)

    def relax(rows, source=None):
        before = [zero] * 3
        now = [rows(0, i) for i in range(3)]
        for r in range(ROWS):
            after = [rows(r + 1, i) for i in range(3)] if r < ROWS - 1 else [zero] * 3
            for i in range(3):
                here = now[i]
                near = (
                    (before[i] + after[i])
                    + jnp.where(lane == 0, 0.0, shift(here, 1))
                    + jnp.where(lane == COLS - 1, 0.0, shift(here, -1))
                )
                value = (
                    coef * near
                    + above_coef * pltpu.roll(here, LEVELS - 1, 0)
                    + below_coef * pltpu.roll(here, 1, 0)
                )
                if i == 0 and source is not None:
                    value = value + source[r]
                flow[r, i] = value
            before, now = now, after

    def completed(k):
        first_cols, last_cols = halo_we[k, 1, 0], shift(halo_we[k, 0, 0], 2)
        pair = (
            coef * jnp.where(is_even, first_cols, last_cols),
            coef * jnp.where(is_even, last_cols, first_cols),
        )

        def rows(r, i):
            value = flow[r, i] + jnp.where(on_edge, shift(pair[r & 1], COLS - 1 - i * ROWS - r), 0.0)
            if r == 0:
                value = value + coef * halo_ns[k, 0, i]
            if r == ROWS - 1:
                value = value + coef * halo_ns[k, 1, i]
            return value

        return rows

    def send_edges(k, par, even, odd, heat=None):
        above = [coef * halo_ns[k, 0, i] for i in range(3)]
        below = [coef * halo_ns[k, 1, i] for i in range(3)]
        last, first = coef * halo_we[k, 0, 0], coef * halo_we[k, 1, 0]
        for i in range(3):
            even = even + shift(jnp.where(on_edge, above[i], 0.0), i * ROWS)
            odd = odd + shift(jnp.where(on_edge, below[i], 0.0), i * ROWS + ROWS - 1)
        to_west, to_east = shift(last, 1), shift(first, -1)
        if heat is not None:
            heat_rows, heat_cols = heat
            for r, value in heat_rows.items():
                part = shift(jnp.where(on_edge, value, 0.0), r)
                even, odd = (even, odd + part) if r & 1 else (even + part, odd)
            at_first = lane_take(heat_cols, (4 * lane) & (COLS - 1))
            at_last = lane_take(heat_cols, (4 * lane + 3) & (COLS - 1))
            to_west = to_west + jnp.where(lane < ROWS, at_first, 0.0)
            to_east = to_east + jnp.where(((lane + 1) & (COLS - 1)) < ROWS, at_last, 0.0)
        send_we[k + 1, 0, 0] = jnp.where(is_even, even, odd) + to_west
        send_we[k + 1, 1, 0] = jnp.where(is_even, odd, even) + to_east
        for own, r, halo in ((0, 0, above), (1, ROWS - 1, below)):
            for i in range(3):
                t = i * ROWS + r
                value = (
                    flow[r, i]
                    + halo[i]
                    + jnp.where(lane == 0, shift(last, 1 - t), 0.0)
                    + jnp.where(lane == COLS - 1, shift(first, COLS - 1 - t), 0.0)
                )
                if i == 0 and heat is not None:
                    cols = jnp.where(near_edge, shift(heat_cols, -4 * r), 0.0)
                    value = value + (heat_rows[r] + cols)
                send_ns[k + 1, own, i] = value
        send_inside(k + 1, par, False)

        def patch(values, index):
            at_row, at_col = index >> 7, index & (COLS - 1)
            for i in range(3):
                slot = i * ROWS + at_row
                add = jnp.where(at_row == 0, lane_take(above[i], at_col), 0.0)
                add = add + jnp.where(at_row == ROWS - 1, lane_take(below[i], at_col), 0.0)
                add = add + jnp.where(at_col == 0, lane_take(last, (slot - 1) & (COLS - 1)), 0.0)
                add = add + jnp.where(at_col == COLS - 1, lane_take(first, slot), 0.0)
                if i == 0 and heat is not None:
                    for r, value in heat_rows.items():
                        add = add + jnp.where(at_row == r, lane_take(value, at_col), 0.0)
                    near = (at_col < 2) | (at_col >= COLS - 2)
                    cols = lane_take(heat_cols, (4 * at_row + at_col) & (COLS - 1))
                    add = add + jnp.where(near, cols, 0.0)
                values[i] = values[i] + add
            return values

        send_found(k + 1, par, False, patch)

    def or_zero(r):
        return heat_row(r) if 0 <= r < ROWS else zero

    for r in range(ROWS):
        up2, up1, here, down1, down2 = (or_zero(r + j) for j in range(-2, 3))
        west1 = jnp.where(lane < 1, 0.0, shift(here, 1))
        west2 = jnp.where(lane < 2, 0.0, shift(here, 2))
        east1 = jnp.where(lane >= COLS - 1, 0.0, shift(here, -1))
        east2 = jnp.where(lane >= COLS - 2, 0.0, shift(here, -2))
        above = jnp.where(level == LEVELS - 1, here, pltpu.roll(here, LEVELS - 1, 0))
        below = jnp.where(level == 0, here, pltpu.roll(here, 1, 0))
        grad_colat = (8.0 * (down1 - up1) - (down2 - up2)) * (1.0 / 12.0)
        grad_lon = (8.0 * (east1 - west1) - (east2 - west2)) * (1.0 / 12.0)
        grad_rad = (above - below) * 0.5
        laplace = down1 + up1 + east1 + west1 + above + below - 6.0 * here
        advect = first_row(r, 0) * grad_rad + first_row(r, 1) * grad_colat + first_row(r, 2) * grad_lon
        stepped = here + TIME_STEP * (laplace - advect)
        heat_out[pl.ds(r, LEVELS, stride=ROWS), :] = stepped
        source[r] = buoyancy * stepped
    relax(first_row, source)
    even, odd = pack_all(flow_row)
    lon_flow = [zero, zero]
    for r in range(ROWS):
        part = shift(jnp.where(near_edge, first_row(r, 2), 0.0), 4 * r)
        lon_flow[r & 1] = lon_flow[r & 1] + part
    lon_flow = (lon_flow[0] + lon_flow[1]) * (1.0 / 12.0)
    find(flow_row)
    wait_all(0, 0, True)

    far, nearby = halo_ns[0, 0, 3], halo_ns[0, 0, 4]
    heat_rows = {
        0: TIME_STEP * (nearby + first_row(0, 1) * ((8.0 * nearby - far) * (1.0 / 12.0))),
        1: (-TIME_STEP / 12.0) * (first_row(1, 1) * nearby),
    }
    nearby, far = halo_ns[0, 1, 3], halo_ns[0, 1, 4]
    heat_rows[ROWS - 2] = (TIME_STEP / 12.0) * (first_row(ROWS - 2, 1) * nearby)
    heat_rows[ROWS - 1] = TIME_STEP * (
        nearby - first_row(ROWS - 1, 1) * ((8.0 * nearby - far) * (1.0 / 12.0))
    )
    west1, west2 = shift(halo_we[0, 0, 1], 1), shift(halo_we[0, 0, 1], 2)
    east1, east2 = shift(halo_we[0, 1, 1], -1), shift(halo_we[0, 1, 1], -2)
    column = lane & 3
    heat_cols = TIME_STEP * jnp.where(
        column == 0,
        west1 + lon_flow * (8.0 * west1 - west2),
        jnp.where(
            column == 1,
            -lon_flow * west2,
            jnp.where(column == 2, lon_flow * east2, east1 - lon_flow * (8.0 * east1 - east2)),
        ),
    )
    scaled_rows = {r: buoyancy * value for r, value in heat_rows.items()}
    send_edges(0, 1, even, odd, (scaled_rows, buoyancy * heat_cols))
    for r in range(ROWS):
        add = jnp.where(near_edge, shift(heat_cols, -4 * r), 0.0)
        if r in heat_rows:
            add = add + heat_rows[r]
        at = pl.ds(r, LEVELS, stride=ROWS)
        heat_out[at, :] = heat_out[at, :] + add
        add = buoyancy * add
        source[r] = source[r] + add
        flow[r, 0] = flow[r, 0] + add
    heat_copy = pltpu.make_async_copy(heat_out, heat_done, out_sem.at[3])
    heat_copy.start()

    def step(k, carry):
        par = k & 1
        relax(completed(k - 1), source)
        even, odd = pack_all(flow_row)
        find(flow_row)
        wait_all(k, par, False)

        @pl.when(k > 1)
        def _():
            wait_sent(k - 1, 1 - par, False)

        send_edges(k, 1 - par, even, odd)
        return carry

    wait_sent(0, 0, True)
    lax.fori_loop(1, ITERS - 1, step, 0)
    relax(completed(ITERS - 2), source)
    last_par = (ITERS - 1) & 1
    wait_all(ITERS - 1, last_par, False)
    rows = completed(ITERS - 1)
    results = []
    for i in range(3):
        for r in range(ROWS):
            flow_out[pl.ds(i * LEVELS * ROWS + r, LEVELS, stride=ROWS), :] = rows(r, i)
        span = pl.ds(i * LEVELS * ROWS, LEVELS * ROWS)
        results.append(pltpu.make_async_copy(flow_out.at[span], flow_done.at[span], out_sem.at[i]))
        results[-1].start()
    wait_sent(ITERS - 2, 1 - last_par, False)
    wait_sent(ITERS - 1, last_par, False)
    heat_copy.wait()
    for result in results:
        result.wait()


def deliver(heat_in, flow_in, heat_out, flow_out, sem):
    copies = [
        pltpu.make_async_copy(heat_in, heat_out, sem.at[0]),
        pltpu.make_async_copy(flow_in, flow_out, sem.at[1]),
    ]
    for copy in copies:
        copy.start()
    for copy in copies:
        copy.wait()


def solution(mesh):
    n_colat, n_lon = mesh.shape["colat"], mesh.shape["lon"]

    block = (LEVELS, COLS)
    heat_shape = jax.ShapeDtypeStruct((LEVELS * ROWS, COLS), jnp.float32)
    flow_shape = jax.ShapeDtypeStruct((3 * LEVELS * ROWS, COLS), jnp.float32)
    anywhere = pl.BlockSpec(memory_space=pl.ANY)
    step = pl.pallas_call(
        lambda *refs: kernel(n_colat, n_lon, *refs),
        out_shape=(heat_shape, flow_shape),
        in_specs=[pl.BlockSpec(memory_space=pltpu.HBM)] * 5,
        out_specs=(anywhere, anywhere),
        scratch_shapes=[
            pltpu.VMEM(heat_shape.shape, jnp.float32),
            pltpu.VMEM(flow_shape.shape, jnp.float32),
            pltpu.SMEM((LEVELS,), jnp.float32),
            pltpu.VMEM((1, 1, 4 * (COLS + ROWS)), jnp.int32),
            pltpu.VMEM((1, 1, 2 * (COLS + ROWS)), jnp.float32),
            pltpu.VMEM(heat_shape.shape, jnp.float32),
            pltpu.VMEM(flow_shape.shape, jnp.float32),
            pltpu.SemaphoreType.DMA((5,)),
            pltpu.SemaphoreType.DMA((4,)),
            pltpu.VMEM((ROWS, 3, *block), jnp.float32),
            pltpu.VMEM((ROWS, *block), jnp.float32),
            pltpu.VMEM((10, *block), jnp.float32),
            pltpu.VMEM((ITERS, 2, 5, *block), jnp.float32),
            pltpu.VMEM((ITERS, 2, 2, *block), jnp.float32),
            pltpu.VMEM((ITERS, 2, 5, *block), jnp.float32),
            pltpu.VMEM((ITERS, 2, 2, *block), jnp.float32),
            pltpu.SemaphoreType.DMA((2, 4)),
            pltpu.SemaphoreType.DMA((2, 4)),
        ],
        compiler_params=pltpu.CompilerParams(collective_id=0, has_side_effects=True, vmem_limit_bytes=8 << 20),
        name="mantle_step",
    )
    place = pl.pallas_call(
        deliver,
        out_shape=(heat_shape, flow_shape),
        in_specs=[anywhere] * 2,
        out_specs=(pl.BlockSpec(memory_space=pltpu.HBM),) * 2,
        scratch_shapes=[pltpu.SemaphoreType.DMA((2,))],
        compiler_params=pltpu.CompilerParams(vmem_limit_bytes=4 << 20),
        name="deliver",
    )

    def pinned(*args):
        return step(*(pltpu.with_memory_space_constraint(a, pltpu.HBM) for a in args))

    def on_device(heat, flow, stiffness, site, phase):
        heat_out, flow_out = place(
            *pinned(
                heat.reshape(heat_shape.shape), flow.reshape(flow_shape.shape), stiffness, site, phase,
            )
        )
        return heat_out.reshape(heat.shape), flow_out.reshape(flow.shape)

    return jax.shard_map(
        on_device,
        mesh=mesh,
        in_specs=(
            P("panel", None, "colat", "lon"),
            P("panel", None, None, "colat", "lon"),
            P(),
            P("panel", "colat", "lon"),
            P("panel", "colat", "lon"),
        ),
        out_specs=(P("panel", None, "colat", "lon"), P("panel", None, None, "colat", "lon")),
        check_vma=False,
    )
```

```python
import jax
import jax.numpy as jnp
from jax import lax
from jax.experimental import pallas as pl
from jax.experimental.pallas import tpu as pltpu
from jax.sharding import PartitionSpec as P

ITERS = 8
TIME_STEP = 0.1
BUOYANCY_FACTOR = 10.0
DRAG_COEF = 1.0
MESH = pl.DeviceIdType.MESH
LEVELS, ROWS, COLS = 8, 32, 128


def lane_take(value, index):
    return jnp.take_along_axis(value, index, axis=1, mode="promise_in_bounds")


def kernel(
    n_colat, n_lon,
    heat_hbm, flow_hbm, stiff_hbm, site_hbm, phase_hbm,
    heat_out, flow_out,
    heat_in, flow_in, stiff_in, site_in, phase_in, in_sem,
    flow, heat, source, found, send_ns, send_we, halo_ns, halo_we, send_sem, recv_sem,
):
    p, c, l = (lax.axis_index(a) for a in ("panel", "colat", "lon"))
    lane = lax.broadcasted_iota(jnp.int32, (LEVELS, COLS), 1)
    level = lax.broadcasted_iota(jnp.int32, (LEVELS, COLS), 0)
    north, south = (c == 0).astype(jnp.int32), (c == n_colat - 1).astype(jnp.int32)
    west, east = (l == 0).astype(jnp.int32), (l == n_lon - 1).astype(jnp.int32)
    at_rim = (north, south, west, east)

    def across(edge):
        return p + edge * (1 - 2 * p)

    sides = (
        ((across(north), c - 1 + north, l), 1 - north),
        ((across(south), c + 1 - south, l), south),
        ((across(west), c, l - 1 + west), 3 - west),
        ((across(east), c, l + 1 - east), 2 + east),
    )
    barrier = pltpu.get_barrier_semaphore()
    for device, _ in sides:
        pl.semaphore_signal(barrier, inc=1, device_id=device, device_id_type=MESH)
    inputs = [
        pltpu.make_async_copy(src, dst, in_sem.at[n])
        for n, (src, dst) in enumerate(
            (
                (stiff_hbm, stiff_in),
                (site_hbm, site_in),
                (phase_hbm, phase_in),
                (flow_hbm, flow_in),
                (heat_hbm, heat_in),
            )
        )
    ]
    for n in (1, 2, 0, 3, 4):
        inputs[n].start()
    for n in (0, 1, 2):
        inputs[n].wait()

    stiff = jnp.zeros((LEVELS, COLS), jnp.float32)
    for k in range(LEVELS):
        stiff = jnp.where(level == k, stiff_in[k], stiff)
    upper = jnp.where(level < LEVELS - 1, 0.5 * (stiff + pltpu.roll(stiff, LEVELS - 1, 0)), 0.0)
    lower = jnp.where(level > 0, 0.5 * (stiff + pltpu.roll(stiff, 1, 0)), 0.0)
    inverse = 1.0 / (DRAG_COEF + 4.0 * stiff + upper + lower)
    coef, above_coef, below_coef = stiff * inverse, upper * inverse, lower * inverse
    buoyancy = BUOYANCY_FACTOR * inverse

    zero = jnp.zeros((LEVELS, COLS), jnp.float32)
    is_even = (lane & 1) == 0
    on_edge = (lane == 0) | (lane == COLS - 1)

    def shift(value, by):
        return pltpu.roll(value, by % COLS, 1)

    def pick(flag, yes, no):
        return jnp.where(flag == 1, yes, no)

    slot = (lane + west) & (COLS - 1)
    slot_row, slot_part = slot & (ROWS - 1), slot >> 5
    heat_slot = (lane + 2 * west) & (COLS - 1)

    def sites(j):
        return jnp.broadcast_to(site_in[0, 0:1, COLS * j : COLS * (j + 1)], (LEVELS, COLS))

    ns_site = pick(north, sites(1), sites(2))
    ns_heat = (pick(north, sites(0), sites(2)), pick(north, sites(1), sites(3)))
    we_base = pick(west, 0, 2 * ROWS)
    we_site = lane_take(sites(4), we_base + west + 2 * slot_row)
    we_heat = lane_take(sites(4), we_base + 2 * (heat_slot >> 2) + (heat_slot & 1))
    ns_angle = jnp.broadcast_to(
        pick(north, phase_in[0, 0:1, 0:COLS], phase_in[0, 0:1, COLS : 2 * COLS]), (LEVELS, COLS)
    )
    tail = phase_in[0, 0:1, 2 * COLS : 2 * COLS + 2 * ROWS]
    tail = jnp.broadcast_to(jnp.concatenate([tail, tail], axis=1), (LEVELS, COLS))
    we_angle = lane_take(tail, pick(west, 0, ROWS) + slot_row)

    def heat_row(r):
        return heat[r]

    def collect(index, rows, count):
        at_row, at_col = index >> 7, index & (COLS - 1)
        values = [zero] * count
        for r in range(ROWS):
            here = at_row == r
            values = [
                jnp.where(here, lane_take(rows(r, i), at_col), v) for i, v in enumerate(values)
            ]
        return values

    def flow_row(r, i):
        return flow[r, i]

    def copy(k, par, first, side, arriving=False):
        device, facing = sides[side]
        ns = side < 2
        buf, halo = (send_ns, halo_ns) if ns else (send_we, halo_we)
        own, theirs = (side, facing) if ns else (side - 2, facing - 2)
        n = (5 if first else 3) if ns else (2 if first else 1)

        at, seen = (own, side) if arriving else (theirs, facing)
        return pltpu.make_async_remote_copy(
            src_ref=buf.at[k, own, 0:n],
            dst_ref=halo.at[k, at, 0:n],
            send_sem=send_sem.at[par, side],
            recv_sem=recv_sem.at[par, seen],
            device_id=device,
            device_id_type=MESH,
        )

    def on_rim(flag_a, flag_b):
        return pl.when((flag_a == 1) | (flag_b == 1))

    def start(k, par, first, side):
        copy(k, par, first, side).start()

    def wait_all(k, par, first):
        for side in range(4):
            copy(k, par, first, side, arriving=True).wait_recv()

    def wait_sent(k, par, first):
        for side in range(4):
            copy(k, par, first, side).wait_send()

    def pack_all(rows):
        packed = [[zero, zero], [zero, zero]]
        for r in range(ROWS):
            for i in range(3):
                part = shift(jnp.where(on_edge, rows(r, i), 0.0), i * ROWS + r)
                packed[r & 1][(r >> 1) & 1] = packed[r & 1][(r >> 1) & 1] + part
        return packed[0][0] + packed[0][1], packed[1][0] + packed[1][1]

    def find(rows):
        @on_rim(north, south)
        def _():
            for i, v in enumerate(collect(ns_site, rows, 3)):
                found[i] = v

        @on_rim(west, east)
        def _():
            for i, v in enumerate(collect(we_site, rows, 3)):
                found[3 + i] = v

    def rotated(values, angle):
        a, b, d = values
        cos, sin = found[angle], found[angle + 1]
        return a, cos * b + sin * d, cos * d - sin * b

    def send_found(k, par, first, patch):
        @on_rim(north, south)
        def _():
            values = patch([found[i] for i in range(3)], ns_site)
            for i, v in enumerate(rotated(values, 6)):
                send_ns[k, south, i] = v

            @pl.when(north == 1)
            def _():
                start(k, par, first, 0)

            @pl.when(south == 1)
            def _():
                start(k, par, first, 1)

        @on_rim(west, east)
        def _():
            values = patch([found[3 + i] for i in range(3)], we_site)
            a, b, d = rotated(values, 8)
            send_we[k, east, 0] = jnp.where(slot_part == 0, a, jnp.where(slot_part == 1, b, d))

            @pl.when(west == 1)
            def _():
                start(k, par, first, 2)

            @pl.when(east == 1)
            def _():
                start(k, par, first, 3)

    def send_inside(k, par, first, which=(2, 3, 0, 1)):
        for side in which:

            @pl.when(at_rim[side] == 0)
            def _(side=side):
                start(k, par, first, side)

    def first_row(r, i):
        return flow_in[pl.ds(i * LEVELS * ROWS + r, LEVELS, stride=ROWS), :]

    @on_rim(north, south)
    def _():
        found[6], found[7] = jnp.cos(ns_angle), jnp.sin(ns_angle)

    @on_rim(west, east)
    def _():
        found[8], found[9] = jnp.cos(we_angle), jnp.sin(we_angle)

    inputs[3].wait()
    for r in range(ROWS):
        for i in range(3):
            flow[r, i] = first_row(r, i)
    even, odd = pack_all(flow_row)
    inputs[4].wait()
    for r in range(ROWS):
        heat[r] = heat_in[pl.ds(r, LEVELS, stride=ROWS), :]
    near_edge = (lane < 2) | (lane >= COLS - 2)
    heat_packed = [zero, zero]
    for r in range(ROWS):
        part = shift(jnp.where(near_edge, heat_row(r), 0.0), 4 * r)
        heat_packed[r & 1] = heat_packed[r & 1] + part
    heat_packed = heat_packed[0] + heat_packed[1]
    for j in range(2):
        send_ns[0, 0, 3 + j] = heat_row(j)
        send_ns[0, 1, 3 + j] = heat_row(ROWS - 2 + j)
        send_we[0, j, 1] = heat_packed
    for i in range(3):
        send_ns[0, 0, i] = flow[0, i]
        send_ns[0, 1, i] = flow[ROWS - 1, i]
    send_we[0, 0, 0] = jnp.where(is_even, even, odd)
    send_we[0, 1, 0] = jnp.where(is_even, odd, even)

    pl.semaphore_wait(barrier, 4)
    send_inside(0, 0, True)

    @on_rim(north, south)
    def _():
        for j in range(2):
            send_ns[0, south, 3 + j] = collect(ns_heat[j], lambda r, _: heat_row(r), 1)[0]

    @on_rim(west, east)
    def _():
        send_we[0, east, 1] = collect(we_heat, lambda r, _: heat_row(r), 1)[0]

    find(flow_row)
    send_found(0, 0, True, lambda values, index: values)

    def relax(rows, source=None):
        before = [zero] * 3
        now = [rows(0, i) for i in range(3)]
        for r in range(ROWS):
            after = [rows(r + 1, i) for i in range(3)] if r < ROWS - 1 else [zero] * 3
            for i in range(3):
                here = now[i]
                near = (
                    (before[i] + after[i])
                    + jnp.where(lane == 0, 0.0, shift(here, 1))
                    + jnp.where(lane == COLS - 1, 0.0, shift(here, -1))
                )
                value = (
                    coef * near
                    + above_coef * pltpu.roll(here, LEVELS - 1, 0)
                    + below_coef * pltpu.roll(here, 1, 0)
                )
                if i == 0 and source is not None:
                    value = value + source[r]
                flow[r, i] = value
            before, now = now, after

    def completed(k):
        first_cols, last_cols = halo_we[k, 1, 0], shift(halo_we[k, 0, 0], 2)
        pair = (
            coef * jnp.where(is_even, first_cols, last_cols),
            coef * jnp.where(is_even, last_cols, first_cols),
        )

        def rows(r, i):
            value = flow[r, i] + jnp.where(on_edge, shift(pair[r & 1], COLS - 1 - i * ROWS - r), 0.0)
            if r == 0:
                value = value + coef * halo_ns[k, 0, i]
            if r == ROWS - 1:
                value = value + coef * halo_ns[k, 1, i]
            return value

        return rows

    def send_edges(k, par, even, odd, heat=None):
        above = [coef * halo_ns[k, 0, i] for i in range(3)]
        below = [coef * halo_ns[k, 1, i] for i in range(3)]
        last, first = coef * halo_we[k, 0, 0], coef * halo_we[k, 1, 0]
        for i in range(3):
            even = even + shift(jnp.where(on_edge, above[i], 0.0), i * ROWS)
            odd = odd + shift(jnp.where(on_edge, below[i], 0.0), i * ROWS + ROWS - 1)
        to_west, to_east = shift(last, 1), shift(first, -1)
        if heat is not None:
            heat_rows, heat_cols = heat
            for r, value in heat_rows.items():
                part = shift(jnp.where(on_edge, value, 0.0), r)
                even, odd = (even, odd + part) if r & 1 else (even + part, odd)
            at_first = lane_take(heat_cols, (4 * lane) & (COLS - 1))
            at_last = lane_take(heat_cols, (4 * lane + 3) & (COLS - 1))
            to_west = to_west + jnp.where(lane < ROWS, at_first, 0.0)
            to_east = to_east + jnp.where(((lane + 1) & (COLS - 1)) < ROWS, at_last, 0.0)
        send_we[k + 1, 0, 0] = jnp.where(is_even, even, odd) + to_west
        send_we[k + 1, 1, 0] = jnp.where(is_even, odd, even) + to_east
        send_inside(k + 1, par, False, (2, 3))
        for own, r, halo in ((0, 0, above), (1, ROWS - 1, below)):
            for i in range(3):
                t = i * ROWS + r
                value = (
                    flow[r, i]
                    + halo[i]
                    + jnp.where(lane == 0, shift(last, 1 - t), 0.0)
                    + jnp.where(lane == COLS - 1, shift(first, COLS - 1 - t), 0.0)
                )
                if i == 0 and heat is not None:
                    cols = jnp.where(near_edge, shift(heat_cols, -4 * r), 0.0)
                    value = value + (heat_rows[r] + cols)
                send_ns[k + 1, own, i] = value
        send_inside(k + 1, par, False, (0, 1))

        def patch(values, index):
            at_row, at_col = index >> 7, index & (COLS - 1)
            for i in range(3):
                slot = i * ROWS + at_row
                add = jnp.where(at_row == 0, lane_take(above[i], at_col), 0.0)
                add = add + jnp.where(at_row == ROWS - 1, lane_take(below[i], at_col), 0.0)
                add = add + jnp.where(at_col == 0, lane_take(last, (slot - 1) & (COLS - 1)), 0.0)
                add = add + jnp.where(at_col == COLS - 1, lane_take(first, slot), 0.0)
                if i == 0 and heat is not None:
                    for r, value in heat_rows.items():
                        add = add + jnp.where(at_row == r, lane_take(value, at_col), 0.0)
                    near = (at_col < 2) | (at_col >= COLS - 2)
                    cols = lane_take(heat_cols, (4 * at_row + at_col) & (COLS - 1))
                    add = add + jnp.where(near, cols, 0.0)
                values[i] = values[i] + add
            return values

        send_found(k + 1, par, False, patch)

    def or_zero(r):
        return heat_row(r) if 0 <= r < ROWS else zero

    for r in range(ROWS):
        up2, up1, here, down1, down2 = (or_zero(r + j) for j in range(-2, 3))
        west1 = jnp.where(lane < 1, 0.0, shift(here, 1))
        west2 = jnp.where(lane < 2, 0.0, shift(here, 2))
        east1 = jnp.where(lane >= COLS - 1, 0.0, shift(here, -1))
        east2 = jnp.where(lane >= COLS - 2, 0.0, shift(here, -2))
        above = jnp.where(level == LEVELS - 1, here, pltpu.roll(here, LEVELS - 1, 0))
        below = jnp.where(level == 0, here, pltpu.roll(here, 1, 0))
        grad_colat = (8.0 * (down1 - up1) - (down2 - up2)) * (1.0 / 12.0)
        grad_lon = (8.0 * (east1 - west1) - (east2 - west2)) * (1.0 / 12.0)
        grad_rad = (above - below) * 0.5
        laplace = down1 + up1 + east1 + west1 + above + below - 6.0 * here
        advect = flow[r, 0] * grad_rad + flow[r, 1] * grad_colat + flow[r, 2] * grad_lon
        stepped = here + TIME_STEP * (laplace - advect)
        heat_out[pl.ds(r, LEVELS, stride=ROWS), :] = stepped
        source[r] = buoyancy * stepped
    lon_flow = [zero, zero]
    for r in range(ROWS):
        part = shift(jnp.where(near_edge, flow[r, 2], 0.0), 4 * r)
        lon_flow[r & 1] = lon_flow[r & 1] + part
    lon_flow = (lon_flow[0] + lon_flow[1]) * (1.0 / 12.0)
    relax(flow_row, source)
    even, odd = pack_all(flow_row)
    find(flow_row)
    wait_all(0, 0, True)

    far, nearby = halo_ns[0, 0, 3], halo_ns[0, 0, 4]
    heat_rows = {
        0: TIME_STEP * (nearby + first_row(0, 1) * ((8.0 * nearby - far) * (1.0 / 12.0))),
        1: (-TIME_STEP / 12.0) * (first_row(1, 1) * nearby),
    }
    nearby, far = halo_ns[0, 1, 3], halo_ns[0, 1, 4]
    heat_rows[ROWS - 2] = (TIME_STEP / 12.0) * (first_row(ROWS - 2, 1) * nearby)
    heat_rows[ROWS - 1] = TIME_STEP * (
        nearby - first_row(ROWS - 1, 1) * ((8.0 * nearby - far) * (1.0 / 12.0))
    )
    west1, west2 = shift(halo_we[0, 0, 1], 1), shift(halo_we[0, 0, 1], 2)
    east1, east2 = shift(halo_we[0, 1, 1], -1), shift(halo_we[0, 1, 1], -2)
    column = lane & 3
    heat_cols = TIME_STEP * jnp.where(
        column == 0,
        west1 + lon_flow * (8.0 * west1 - west2),
        jnp.where(
            column == 1,
            -lon_flow * west2,
            jnp.where(column == 2, lon_flow * east2, east1 - lon_flow * (8.0 * east1 - east2)),
        ),
    )
    scaled_rows = {r: buoyancy * value for r, value in heat_rows.items()}
    send_edges(0, 1, even, odd, (scaled_rows, buoyancy * heat_cols))
    for r in range(ROWS):
        add = jnp.where(near_edge, shift(heat_cols, -4 * r), 0.0)
        if r in heat_rows:
            add = add + heat_rows[r]
        at = pl.ds(r, LEVELS, stride=ROWS)
        heat_out[at, :] = heat_out[at, :] + add
        add = buoyancy * add
        source[r] = source[r] + add
        flow[r, 0] = flow[r, 0] + add

    def step(k, carry):
        par = k & 1
        relax(completed(k - 1), source)
        even, odd = pack_all(flow_row)
        find(flow_row)

        @pl.when(k > 1)
        def _():
            wait_sent(k - 1, 1 - par, False)

        wait_all(k, par, False)
        send_edges(k, 1 - par, even, odd)
        return carry

    wait_sent(0, 0, True)
    lax.fori_loop(1, ITERS - 1, step, 0)
    relax(completed(ITERS - 2), source)
    last_par = (ITERS - 1) & 1
    wait_all(ITERS - 1, last_par, False)
    rows = completed(ITERS - 1)
    for r in range(ROWS):
        for i in range(3):
            flow_out[pl.ds(i * LEVELS * ROWS + r, LEVELS, stride=ROWS), :] = rows(r, i)
    wait_sent(ITERS - 2, 1 - last_par, False)
    wait_sent(ITERS - 1, last_par, False)


def deliver(heat_in, flow_in, heat_out, flow_out, sem):
    copies = [
        pltpu.make_async_copy(heat_in, heat_out, sem.at[0]),
        pltpu.make_async_copy(flow_in, flow_out, sem.at[1]),
    ]
    for copy in copies:
        copy.start()
    for copy in copies:
        copy.wait()


def solution(mesh):
    n_colat, n_lon = mesh.shape["colat"], mesh.shape["lon"]

    block = (LEVELS, COLS)
    heat_shape = jax.ShapeDtypeStruct((LEVELS * ROWS, COLS), jnp.float32)
    flow_shape = jax.ShapeDtypeStruct((3 * LEVELS * ROWS, COLS), jnp.float32)
    anywhere = pl.BlockSpec(memory_space=pl.ANY)
    step = pl.pallas_call(
        lambda *refs: kernel(n_colat, n_lon, *refs),
        out_shape=(heat_shape, flow_shape),
        in_specs=[pl.BlockSpec(memory_space=pltpu.HBM)] * 5,
        out_specs=(pl.BlockSpec(memory_space=pltpu.VMEM),) * 2,
        scratch_shapes=[
            pltpu.VMEM(heat_shape.shape, jnp.float32),
            pltpu.VMEM(flow_shape.shape, jnp.float32),
            pltpu.SMEM((LEVELS,), jnp.float32),
            pltpu.VMEM((1, 1, 4 * (COLS + ROWS)), jnp.int32),
            pltpu.VMEM((1, 1, 2 * (COLS + ROWS)), jnp.float32),
            pltpu.SemaphoreType.DMA((5,)),
            pltpu.VMEM((ROWS, 3, *block), jnp.float32),
            pltpu.VMEM((ROWS, *block), jnp.float32),
            pltpu.VMEM((ROWS, *block), jnp.float32),
            pltpu.VMEM((10, *block), jnp.float32),
            pltpu.VMEM((ITERS, 2, 5, *block), jnp.float32),
            pltpu.VMEM((ITERS, 2, 2, *block), jnp.float32),
            pltpu.VMEM((ITERS, 2, 5, *block), jnp.float32),
            pltpu.VMEM((ITERS, 2, 2, *block), jnp.float32),
            pltpu.SemaphoreType.DMA((2, 4)),
            pltpu.SemaphoreType.DMA((2, 4)),
        ],
        compiler_params=pltpu.CompilerParams(collective_id=0, has_side_effects=True, vmem_limit_bytes=8 << 20),
        name="mantle_step",
    )
    place = pl.pallas_call(
        deliver,
        out_shape=(heat_shape, flow_shape),
        in_specs=[anywhere] * 2,
        out_specs=(pl.BlockSpec(memory_space=pltpu.HBM),) * 2,
        scratch_shapes=[pltpu.SemaphoreType.DMA((2,))],
        compiler_params=pltpu.CompilerParams(vmem_limit_bytes=4 << 20),
        name="deliver",
    )

    def pinned(*args):
        return step(*(pltpu.with_memory_space_constraint(a, pltpu.HBM) for a in args))

    def on_device(heat, flow, stiffness, site, phase):
        heat_out, flow_out = place(
            *pinned(
                heat.reshape(heat_shape.shape), flow.reshape(flow_shape.shape), stiffness, site, phase,
            )
        )
        return heat_out.reshape(heat.shape), flow_out.reshape(flow.shape)

    return jax.shard_map(
        on_device,
        mesh=mesh,
        in_specs=(
            P("panel", None, "colat", "lon"),
            P("panel", None, None, "colat", "lon"),
            P(),
            P("panel", "colat", "lon"),
            P("panel", "colat", "lon"),
        ),
        out_specs=(P("panel", None, "colat", "lon"), P("panel", None, None, "colat", "lon")),
        check_vma=False,
    )
```

```python
import jax
import jax.numpy as jnp
from jax import lax
from jax.experimental import pallas as pl
from jax.experimental.pallas import tpu as pltpu
from jax.sharding import PartitionSpec as P

ITERS = 8
TIME_STEP = 0.1
BUOYANCY_FACTOR = 10.0
DRAG_COEF = 1.0
MESH = pl.DeviceIdType.MESH
LEVELS, ROWS, COLS = 8, 32, 128


def lane_take(value, index):
    return jnp.take_along_axis(value, index, axis=1, mode="promise_in_bounds")


def kernel(
    n_colat, n_lon,
    heat_hbm, flow_hbm, stiff_hbm, site_hbm, phase_hbm,
    heat_out, flow_out,
    stiff_in, site_in, phase_in, in_sem,
    flow, heat, source, found, send_ns, send_we, halo_ns, halo_we, send_sem, recv_sem,
):
    p, c, l = (lax.axis_index(a) for a in ("panel", "colat", "lon"))
    lane = lax.broadcasted_iota(jnp.int32, (LEVELS, COLS), 1)
    level = lax.broadcasted_iota(jnp.int32, (LEVELS, COLS), 0)
    north, south = (c == 0).astype(jnp.int32), (c == n_colat - 1).astype(jnp.int32)
    west, east = (l == 0).astype(jnp.int32), (l == n_lon - 1).astype(jnp.int32)
    at_rim = (north, south, west, east)

    def across(edge):
        return p + edge * (1 - 2 * p)

    sides = (
        ((across(north), c - 1 + north, l), 1 - north),
        ((across(south), c + 1 - south, l), south),
        ((across(west), c, l - 1 + west), 3 - west),
        ((across(east), c, l + 1 - east), 2 + east),
    )
    barrier = pltpu.get_barrier_semaphore()
    for device, _ in sides:
        pl.semaphore_signal(barrier, inc=1, device_id=device, device_id_type=MESH)
    small = [
        pltpu.make_async_copy(src, dst, in_sem.at[n])
        for n, (src, dst) in enumerate(
            ((site_hbm, site_in), (phase_hbm, phase_in), (stiff_hbm, stiff_in))
        )
    ]
    for copy in small:
        copy.start()
    for i in range(3):
        for k in range(LEVELS):
            pltpu.make_async_copy(flow_hbm.at[i, k], flow.at[:, i, k, :], in_sem.at[3]).start()
    for k in range(LEVELS):
        pltpu.make_async_copy(heat_hbm.at[k], heat.at[:, k, :], in_sem.at[4]).start()
    for copy in small:
        copy.wait()

    stiff = jnp.zeros((LEVELS, COLS), jnp.float32)
    for k in range(LEVELS):
        stiff = jnp.where(level == k, stiff_in[k], stiff)
    upper = jnp.where(level < LEVELS - 1, 0.5 * (stiff + pltpu.roll(stiff, LEVELS - 1, 0)), 0.0)
    lower = jnp.where(level > 0, 0.5 * (stiff + pltpu.roll(stiff, 1, 0)), 0.0)
    inverse = 1.0 / (DRAG_COEF + 4.0 * stiff + upper + lower)
    coef, above_coef, below_coef = stiff * inverse, upper * inverse, lower * inverse
    buoyancy = BUOYANCY_FACTOR * inverse

    zero = jnp.zeros((LEVELS, COLS), jnp.float32)
    is_even = (lane & 1) == 0
    on_edge = (lane == 0) | (lane == COLS - 1)

    def shift(value, by):
        return pltpu.roll(value, by % COLS, 1)

    def pick(flag, yes, no):
        return jnp.where(flag == 1, yes, no)

    slot = (lane + west) & (COLS - 1)
    slot_row, slot_part = slot & (ROWS - 1), slot >> 5
    heat_slot = (lane + 2 * west) & (COLS - 1)

    def sites(j):
        return jnp.broadcast_to(site_in[0, 0:1, COLS * j : COLS * (j + 1)], (LEVELS, COLS))

    ns_site = pick(north, sites(1), sites(2))
    ns_heat = (pick(north, sites(0), sites(2)), pick(north, sites(1), sites(3)))
    we_base = pick(west, 0, 2 * ROWS)
    we_site = lane_take(sites(4), we_base + west + 2 * slot_row)
    we_heat = lane_take(sites(4), we_base + 2 * (heat_slot >> 2) + (heat_slot & 1))
    ns_angle = jnp.broadcast_to(
        pick(north, phase_in[0, 0:1, 0:COLS], phase_in[0, 0:1, COLS : 2 * COLS]), (LEVELS, COLS)
    )
    tail = phase_in[0, 0:1, 2 * COLS : 2 * COLS + 2 * ROWS]
    tail = jnp.broadcast_to(jnp.concatenate([tail, tail], axis=1), (LEVELS, COLS))
    we_angle = lane_take(tail, pick(west, 0, ROWS) + slot_row)

    def heat_row(r):
        return heat[r]

    def collect(index, rows, count):
        at_row, at_col = index >> 7, index & (COLS - 1)
        values = [zero] * count
        for r in range(ROWS):
            here = at_row == r
            values = [
                jnp.where(here, lane_take(rows(r, i), at_col), v) for i, v in enumerate(values)
            ]
        return values

    def flow_row(r, i):
        return flow[r, i]

    def copy(k, par, first, side, arriving=False):
        device, facing = sides[side]
        ns = side < 2
        buf, halo = (send_ns, halo_ns) if ns else (send_we, halo_we)
        own, theirs = (side, facing) if ns else (side - 2, facing - 2)
        n = (5 if first else 3) if ns else (2 if first else 1)

        at, seen = (own, side) if arriving else (theirs, facing)
        return pltpu.make_async_remote_copy(
            src_ref=buf.at[k, own, 0:n],
            dst_ref=halo.at[k, at, 0:n],
            send_sem=send_sem.at[par, side],
            recv_sem=recv_sem.at[par, seen],
            device_id=device,
            device_id_type=MESH,
        )

    def on_rim(flag_a, flag_b):
        return pl.when((flag_a == 1) | (flag_b == 1))

    def start(k, par, first, side):
        copy(k, par, first, side).start()

    def wait_all(k, par, first):
        for side in range(4):
            copy(k, par, first, side, arriving=True).wait_recv()

    def wait_sent(k, par, first):
        for side in range(4):
            copy(k, par, first, side).wait_send()

    def pack_all(rows):
        packed = [[zero, zero], [zero, zero]]
        for r in range(ROWS):
            for i in range(3):
                part = shift(jnp.where(on_edge, rows(r, i), 0.0), i * ROWS + r)
                packed[r & 1][(r >> 1) & 1] = packed[r & 1][(r >> 1) & 1] + part
        return packed[0][0] + packed[0][1], packed[1][0] + packed[1][1]

    def find(rows):
        @on_rim(north, south)
        def _():
            for i, v in enumerate(collect(ns_site, rows, 3)):
                found[i] = v

        @on_rim(west, east)
        def _():
            for i, v in enumerate(collect(we_site, rows, 3)):
                found[3 + i] = v

    def rotated(values, angle):
        a, b, d = values
        cos, sin = found[angle], found[angle + 1]
        return a, cos * b + sin * d, cos * d - sin * b

    def send_found(k, par, first, patch):
        @on_rim(north, south)
        def _():
            values = patch([found[i] for i in range(3)], ns_site)
            for i, v in enumerate(rotated(values, 6)):
                send_ns[k, south, i] = v

            @pl.when(north == 1)
            def _():
                start(k, par, first, 0)

            @pl.when(south == 1)
            def _():
                start(k, par, first, 1)

        @on_rim(west, east)
        def _():
            values = patch([found[3 + i] for i in range(3)], we_site)
            a, b, d = rotated(values, 8)
            send_we[k, east, 0] = jnp.where(slot_part == 0, a, jnp.where(slot_part == 1, b, d))

            @pl.when(west == 1)
            def _():
                start(k, par, first, 2)

            @pl.when(east == 1)
            def _():
                start(k, par, first, 3)

    def send_inside(k, par, first, which=(2, 3, 0, 1)):
        for side in which:

            @pl.when(at_rim[side] == 0)
            def _(side=side):
                start(k, par, first, side)

    @on_rim(north, south)
    def _():
        found[6], found[7] = jnp.cos(ns_angle), jnp.sin(ns_angle)

    @on_rim(west, east)
    def _():
        found[8], found[9] = jnp.cos(we_angle), jnp.sin(we_angle)

    pltpu.make_async_copy(flow, flow, in_sem.at[3]).wait()
    even, odd = pack_all(flow_row)
    pltpu.make_async_copy(heat, heat, in_sem.at[4]).wait()
    near_edge = (lane < 2) | (lane >= COLS - 2)
    heat_packed = [zero, zero]
    for r in range(ROWS):
        part = shift(jnp.where(near_edge, heat_row(r), 0.0), 4 * r)
        heat_packed[r & 1] = heat_packed[r & 1] + part
    heat_packed = heat_packed[0] + heat_packed[1]
    for j in range(2):
        send_ns[0, 0, 3 + j] = heat_row(j)
        send_ns[0, 1, 3 + j] = heat_row(ROWS - 2 + j)
        send_we[0, j, 1] = heat_packed
    for i in range(3):
        send_ns[0, 0, i] = flow[0, i]
        send_ns[0, 1, i] = flow[ROWS - 1, i]
    send_we[0, 0, 0] = jnp.where(is_even, even, odd)
    send_we[0, 1, 0] = jnp.where(is_even, odd, even)

    pl.semaphore_wait(barrier, 4)
    send_inside(0, 0, True)

    @on_rim(north, south)
    def _():
        for j in range(2):
            send_ns[0, south, 3 + j] = collect(ns_heat[j], lambda r, _: heat_row(r), 1)[0]

    @on_rim(west, east)
    def _():
        send_we[0, east, 1] = collect(we_heat, lambda r, _: heat_row(r), 1)[0]

    find(flow_row)
    send_found(0, 0, True, lambda values, index: values)

    def relax(rows, source=None):
        before = [zero] * 3
        now = [rows(0, i) for i in range(3)]
        for r in range(ROWS):
            after = [rows(r + 1, i) for i in range(3)] if r < ROWS - 1 else [zero] * 3
            for i in range(3):
                here = now[i]
                near = (
                    (before[i] + after[i])
                    + jnp.where(lane == 0, 0.0, shift(here, 1))
                    + jnp.where(lane == COLS - 1, 0.0, shift(here, -1))
                )
                value = (
                    coef * near
                    + above_coef * pltpu.roll(here, LEVELS - 1, 0)
                    + below_coef * pltpu.roll(here, 1, 0)
                )
                if i == 0 and source is not None:
                    value = value + source[r]
                flow[r, i] = value
            before, now = now, after

    def completed(k):
        first_cols, last_cols = halo_we[k, 1, 0], shift(halo_we[k, 0, 0], 2)
        pair = (
            coef * jnp.where(is_even, first_cols, last_cols),
            coef * jnp.where(is_even, last_cols, first_cols),
        )

        def rows(r, i):
            value = flow[r, i] + jnp.where(on_edge, shift(pair[r & 1], COLS - 1 - i * ROWS - r), 0.0)
            if r == 0:
                value = value + coef * halo_ns[k, 0, i]
            if r == ROWS - 1:
                value = value + coef * halo_ns[k, 1, i]
            return value

        return rows

    def send_edges(k, par, even, odd, heat=None):
        above = [coef * halo_ns[k, 0, i] for i in range(3)]
        below = [coef * halo_ns[k, 1, i] for i in range(3)]
        last, first = coef * halo_we[k, 0, 0], coef * halo_we[k, 1, 0]
        for i in range(3):
            even = even + shift(jnp.where(on_edge, above[i], 0.0), i * ROWS)
            odd = odd + shift(jnp.where(on_edge, below[i], 0.0), i * ROWS + ROWS - 1)
        to_west, to_east = shift(last, 1), shift(first, -1)
        if heat is not None:
            heat_rows, heat_cols = heat
            for r, value in heat_rows.items():
                part = shift(jnp.where(on_edge, value, 0.0), r)
                even, odd = (even, odd + part) if r & 1 else (even + part, odd)
            at_first = lane_take(heat_cols, (4 * lane) & (COLS - 1))
            at_last = lane_take(heat_cols, (4 * lane + 3) & (COLS - 1))
            to_west = to_west + jnp.where(lane < ROWS, at_first, 0.0)
            to_east = to_east + jnp.where(((lane + 1) & (COLS - 1)) < ROWS, at_last, 0.0)
        send_we[k + 1, 0, 0] = jnp.where(is_even, even, odd) + to_west
        send_we[k + 1, 1, 0] = jnp.where(is_even, odd, even) + to_east
        send_inside(k + 1, par, False, (2, 3))
        for own, r, halo in ((0, 0, above), (1, ROWS - 1, below)):
            for i in range(3):
                t = i * ROWS + r
                value = (
                    flow[r, i]
                    + halo[i]
                    + jnp.where(lane == 0, shift(last, 1 - t), 0.0)
                    + jnp.where(lane == COLS - 1, shift(first, COLS - 1 - t), 0.0)
                )
                if i == 0 and heat is not None:
                    cols = jnp.where(near_edge, shift(heat_cols, -4 * r), 0.0)
                    value = value + (heat_rows[r] + cols)
                send_ns[k + 1, own, i] = value
        send_inside(k + 1, par, False, (0, 1))

        def patch(values, index):
            at_row, at_col = index >> 7, index & (COLS - 1)
            for i in range(3):
                slot = i * ROWS + at_row
                add = jnp.where(at_row == 0, lane_take(above[i], at_col), 0.0)
                add = add + jnp.where(at_row == ROWS - 1, lane_take(below[i], at_col), 0.0)
                add = add + jnp.where(at_col == 0, lane_take(last, (slot - 1) & (COLS - 1)), 0.0)
                add = add + jnp.where(at_col == COLS - 1, lane_take(first, slot), 0.0)
                if i == 0 and heat is not None:
                    for r, value in heat_rows.items():
                        add = add + jnp.where(at_row == r, lane_take(value, at_col), 0.0)
                    near = (at_col < 2) | (at_col >= COLS - 2)
                    cols = lane_take(heat_cols, (4 * at_row + at_col) & (COLS - 1))
                    add = add + jnp.where(near, cols, 0.0)
                values[i] = values[i] + add
            return values

        send_found(k + 1, par, False, patch)

    def or_zero(r):
        return heat_row(r) if 0 <= r < ROWS else zero

    for r in range(ROWS):
        up2, up1, here, down1, down2 = (or_zero(r + j) for j in range(-2, 3))
        west1 = jnp.where(lane < 1, 0.0, shift(here, 1))
        west2 = jnp.where(lane < 2, 0.0, shift(here, 2))
        east1 = jnp.where(lane >= COLS - 1, 0.0, shift(here, -1))
        east2 = jnp.where(lane >= COLS - 2, 0.0, shift(here, -2))
        above = jnp.where(level == LEVELS - 1, here, pltpu.roll(here, LEVELS - 1, 0))
        below = jnp.where(level == 0, here, pltpu.roll(here, 1, 0))
        grad_colat = (8.0 * (down1 - up1) - (down2 - up2)) * (1.0 / 12.0)
        grad_lon = (8.0 * (east1 - west1) - (east2 - west2)) * (1.0 / 12.0)
        grad_rad = (above - below) * 0.5
        laplace = down1 + up1 + east1 + west1 + above + below - 6.0 * here
        advect = flow[r, 0] * grad_rad + flow[r, 1] * grad_colat + flow[r, 2] * grad_lon
        stepped = here + TIME_STEP * (laplace - advect)
        heat_out[r] = stepped
        source[r] = buoyancy * stepped
    outer_flow = {r: flow[r, 1] for r in (0, 1, ROWS - 2, ROWS - 1)}
    lon_flow = [zero, zero]
    for r in range(ROWS):
        part = shift(jnp.where(near_edge, flow[r, 2], 0.0), 4 * r)
        lon_flow[r & 1] = lon_flow[r & 1] + part
    lon_flow = (lon_flow[0] + lon_flow[1]) * (1.0 / 12.0)
    relax(flow_row, source)
    even, odd = pack_all(flow_row)
    find(flow_row)
    wait_all(0, 0, True)

    far, nearby = halo_ns[0, 0, 3], halo_ns[0, 0, 4]
    heat_rows = {
        0: TIME_STEP * (nearby + outer_flow[0] * ((8.0 * nearby - far) * (1.0 / 12.0))),
        1: (-TIME_STEP / 12.0) * (outer_flow[1] * nearby),
    }
    nearby, far = halo_ns[0, 1, 3], halo_ns[0, 1, 4]
    heat_rows[ROWS - 2] = (TIME_STEP / 12.0) * (outer_flow[ROWS - 2] * nearby)
    heat_rows[ROWS - 1] = TIME_STEP * (
        nearby - outer_flow[ROWS - 1] * ((8.0 * nearby - far) * (1.0 / 12.0))
    )
    west1, west2 = shift(halo_we[0, 0, 1], 1), shift(halo_we[0, 0, 1], 2)
    east1, east2 = shift(halo_we[0, 1, 1], -1), shift(halo_we[0, 1, 1], -2)
    column = lane & 3
    heat_cols = TIME_STEP * jnp.where(
        column == 0,
        west1 + lon_flow * (8.0 * west1 - west2),
        jnp.where(
            column == 1,
            -lon_flow * west2,
            jnp.where(column == 2, lon_flow * east2, east1 - lon_flow * (8.0 * east1 - east2)),
        ),
    )
    scaled_rows = {r: buoyancy * value for r, value in heat_rows.items()}
    send_edges(0, 1, even, odd, (scaled_rows, buoyancy * heat_cols))
    for r in range(ROWS):
        add = jnp.where(near_edge, shift(heat_cols, -4 * r), 0.0)
        if r in heat_rows:
            add = add + heat_rows[r]
        heat_out[r] = heat_out[r] + add
        add = buoyancy * add
        source[r] = source[r] + add
        flow[r, 0] = flow[r, 0] + add

    def step(k, carry):
        par = k & 1
        relax(completed(k - 1), source)
        even, odd = pack_all(flow_row)
        find(flow_row)

        @pl.when(k > 1)
        def _():
            wait_sent(k - 1, 1 - par, False)

        wait_all(k, par, False)
        send_edges(k, 1 - par, even, odd)
        return carry

    wait_sent(0, 0, True)
    lax.fori_loop(1, ITERS - 1, step, 0)
    relax(completed(ITERS - 2), source)
    last_par = (ITERS - 1) & 1
    wait_all(ITERS - 1, last_par, False)
    rows = completed(ITERS - 1)
    for r in range(ROWS):
        for i in range(3):
            flow_out[r, i] = rows(r, i)
    wait_sent(ITERS - 2, 1 - last_par, False)
    wait_sent(ITERS - 1, last_par, False)


def deliver(heat_in, flow_in, heat_out, flow_out, sem):
    for i in range(3):
        for k in range(LEVELS):
            pltpu.make_async_copy(flow_in.at[:, i, k, :], flow_out.at[i, k], sem.at[0]).start()
    for k in range(LEVELS):
        pltpu.make_async_copy(heat_in.at[:, k, :], heat_out.at[k], sem.at[1]).start()
    pltpu.make_async_copy(flow_out, flow_out, sem.at[0]).wait()
    pltpu.make_async_copy(heat_out, heat_out, sem.at[1]).wait()


def solution(mesh):
    n_colat, n_lon = mesh.shape["colat"], mesh.shape["lon"]

    block = (LEVELS, COLS)
    heat_shape = jax.ShapeDtypeStruct((LEVELS, ROWS, COLS), jnp.float32)
    flow_shape = jax.ShapeDtypeStruct((3, LEVELS, ROWS, COLS), jnp.float32)
    heat_by_row = jax.ShapeDtypeStruct((ROWS, *block), jnp.float32)
    flow_by_row = jax.ShapeDtypeStruct((ROWS, 3, *block), jnp.float32)
    anywhere = pl.BlockSpec(memory_space=pl.ANY)
    step = pl.pallas_call(
        lambda *refs: kernel(n_colat, n_lon, *refs),
        out_shape=(heat_by_row, flow_by_row),
        in_specs=[pl.BlockSpec(memory_space=pltpu.HBM)] * 5,
        out_specs=(pl.BlockSpec(memory_space=pltpu.VMEM),) * 2,
        scratch_shapes=[
            pltpu.SMEM((LEVELS,), jnp.float32),
            pltpu.VMEM((1, 1, 4 * (COLS + ROWS)), jnp.int32),
            pltpu.VMEM((1, 1, 2 * (COLS + ROWS)), jnp.float32),
            pltpu.SemaphoreType.DMA((5,)),
            pltpu.VMEM((ROWS, 3, *block), jnp.float32),
            pltpu.VMEM((ROWS, *block), jnp.float32),
            pltpu.VMEM((ROWS, *block), jnp.float32),
            pltpu.VMEM((10, *block), jnp.float32),
            pltpu.VMEM((ITERS, 2, 5, *block), jnp.float32),
            pltpu.VMEM((ITERS, 2, 2, *block), jnp.float32),
            pltpu.VMEM((ITERS, 2, 5, *block), jnp.float32),
            pltpu.VMEM((ITERS, 2, 2, *block), jnp.float32),
            pltpu.SemaphoreType.DMA((2, 4)),
            pltpu.SemaphoreType.DMA((2, 4)),
        ],
        compiler_params=pltpu.CompilerParams(collective_id=0, has_side_effects=True, vmem_limit_bytes=8 << 20),
        name="mantle_step",
    )
    place = pl.pallas_call(
        deliver,
        out_shape=(heat_shape, flow_shape),
        in_specs=[anywhere] * 2,
        out_specs=(pl.BlockSpec(memory_space=pltpu.HBM),) * 2,
        scratch_shapes=[pltpu.SemaphoreType.DMA((2,))],
        compiler_params=pltpu.CompilerParams(vmem_limit_bytes=4 << 20),
        name="deliver",
    )

    def pinned(*args):
        return step(*(pltpu.with_memory_space_constraint(a, pltpu.HBM) for a in args))

    def on_device(heat, flow, stiffness, site, phase):
        heat_out, flow_out = place(
            *pinned(
                heat.reshape(heat_shape.shape), flow.reshape(flow_shape.shape), stiffness, site, phase,
            )
        )
        return heat_out.reshape(heat.shape), flow_out.reshape(flow.shape)

    return jax.shard_map(
        on_device,
        mesh=mesh,
        in_specs=(
            P("panel", None, "colat", "lon"),
            P("panel", None, None, "colat", "lon"),
            P(),
            P("panel", "colat", "lon"),
            P("panel", "colat", "lon"),
        ),
        out_specs=(P("panel", None, "colat", "lon"), P("panel", None, None, "colat", "lon")),
        check_vma=False,
    )
```

```python
import jax
import jax.numpy as jnp
from jax import lax
from jax.experimental import pallas as pl
from jax.experimental.pallas import tpu as pltpu
from jax.sharding import PartitionSpec as P

ITERS = 8
TIME_STEP = 0.1
BUOYANCY_FACTOR = 10.0
DRAG_COEF = 1.0
MESH = pl.DeviceIdType.MESH
LEVELS, ROWS, COLS = 8, 32, 128


def lane_take(value, index):
    return jnp.take_along_axis(value, index, axis=1, mode="promise_in_bounds")


def with_halo(rows, share, on_edge):
    def complete(r, i):
        by = (COLS - 1 - i * ROWS - r) % COLS
        value = rows(r, i) + jnp.where(on_edge, pltpu.roll(share[6 + (r & 1)], by, 1), 0.0)
        if r == 0:
            value = value + share[i]
        if r == ROWS - 1:
            value = value + share[3 + i]
        return value

    return complete


def kernel(
    n_colat, n_lon,
    heat_hbm, flow_hbm, stiff_hbm, site_hbm, phase_hbm,
    heat_out, flow_out, halo_out,
    stiff_in, site_in, phase_in, in_sem,
    flow, heat, source, found, send_ns, send_we, halo_ns, halo_we, send_sem, recv_sem,
):
    p, c, l = (lax.axis_index(a) for a in ("panel", "colat", "lon"))
    lane = lax.broadcasted_iota(jnp.int32, (LEVELS, COLS), 1)
    level = lax.broadcasted_iota(jnp.int32, (LEVELS, COLS), 0)
    north, south = (c == 0).astype(jnp.int32), (c == n_colat - 1).astype(jnp.int32)
    west, east = (l == 0).astype(jnp.int32), (l == n_lon - 1).astype(jnp.int32)
    at_rim = (north, south, west, east)

    def across(edge):
        return p + edge * (1 - 2 * p)

    sides = (
        ((across(north), c - 1 + north, l), 1 - north),
        ((across(south), c + 1 - south, l), south),
        ((across(west), c, l - 1 + west), 3 - west),
        ((across(east), c, l + 1 - east), 2 + east),
    )
    barrier = pltpu.get_barrier_semaphore()
    for device, _ in sides:
        pl.semaphore_signal(barrier, inc=1, device_id=device, device_id_type=MESH)
    small = [
        pltpu.make_async_copy(src, dst, in_sem.at[n])
        for n, (src, dst) in enumerate(
            ((site_hbm, site_in), (phase_hbm, phase_in), (stiff_hbm, stiff_in))
        )
    ]
    for copy in small:
        copy.start()
    for i in range(3):
        for k in range(LEVELS):
            pltpu.make_async_copy(flow_hbm.at[i, k], flow.at[:, i, k, :], in_sem.at[3]).start()
    for k in range(LEVELS):
        pltpu.make_async_copy(heat_hbm.at[k], heat.at[:, k, :], in_sem.at[4]).start()
    for copy in small:
        copy.wait()

    stiff = jnp.zeros((LEVELS, COLS), jnp.float32)
    for k in range(LEVELS):
        stiff = jnp.where(level == k, stiff_in[k], stiff)
    upper = jnp.where(level < LEVELS - 1, 0.5 * (stiff + pltpu.roll(stiff, LEVELS - 1, 0)), 0.0)
    lower = jnp.where(level > 0, 0.5 * (stiff + pltpu.roll(stiff, 1, 0)), 0.0)
    inverse = 1.0 / (DRAG_COEF + 4.0 * stiff + upper + lower)
    coef, above_coef, below_coef = stiff * inverse, upper * inverse, lower * inverse
    buoyancy = BUOYANCY_FACTOR * inverse

    zero = jnp.zeros((LEVELS, COLS), jnp.float32)
    is_even = (lane & 1) == 0
    on_edge = (lane == 0) | (lane == COLS - 1)

    def shift(value, by):
        return pltpu.roll(value, by % COLS, 1)

    def pick(flag, yes, no):
        return jnp.where(flag == 1, yes, no)

    slot = (lane + west) & (COLS - 1)
    slot_row, slot_part = slot & (ROWS - 1), slot >> 5
    heat_slot = (lane + 2 * west) & (COLS - 1)

    def sites(j):
        return jnp.broadcast_to(site_in[0, 0:1, COLS * j : COLS * (j + 1)], (LEVELS, COLS))

    ns_site = pick(north, sites(1), sites(2))
    ns_heat = (pick(north, sites(0), sites(2)), pick(north, sites(1), sites(3)))
    we_base = pick(west, 0, 2 * ROWS)
    we_site = lane_take(sites(4), we_base + west + 2 * slot_row)
    we_heat = lane_take(sites(4), we_base + 2 * (heat_slot >> 2) + (heat_slot & 1))
    ns_angle = jnp.broadcast_to(
        pick(north, phase_in[0, 0:1, 0:COLS], phase_in[0, 0:1, COLS : 2 * COLS]), (LEVELS, COLS)
    )
    tail = phase_in[0, 0:1, 2 * COLS : 2 * COLS + 2 * ROWS]
    tail = jnp.broadcast_to(jnp.concatenate([tail, tail], axis=1), (LEVELS, COLS))
    we_angle = lane_take(tail, pick(west, 0, ROWS) + slot_row)

    def heat_row(r):
        return heat[r]

    def collect(index, rows, count):
        at_row, at_col = index >> 7, index & (COLS - 1)
        values = [zero] * count
        for r in range(ROWS):
            here = at_row == r
            values = [
                jnp.where(here, lane_take(rows(r, i), at_col), v) for i, v in enumerate(values)
            ]
        return values

    def flow_row(r, i):
        return flow[r, i]

    def copy(k, par, first, side, arriving=False):
        device, facing = sides[side]
        ns = side < 2
        buf, halo = (send_ns, halo_ns) if ns else (send_we, halo_we)
        own, theirs = (side, facing) if ns else (side - 2, facing - 2)
        n = (5 if first else 3) if ns else (2 if first else 1)

        at, seen = (own, side) if arriving else (theirs, facing)
        return pltpu.make_async_remote_copy(
            src_ref=buf.at[k, own, 0:n],
            dst_ref=halo.at[k, at, 0:n],
            send_sem=send_sem.at[par, side],
            recv_sem=recv_sem.at[par, seen],
            device_id=device,
            device_id_type=MESH,
        )

    def on_rim(flag_a, flag_b):
        return pl.when((flag_a == 1) | (flag_b == 1))

    def start(k, par, first, side):
        copy(k, par, first, side).start()

    def wait_all(k, par, first):
        for side in range(4):
            copy(k, par, first, side, arriving=True).wait_recv()

    def wait_sent(k, par, first):
        for side in range(4):
            copy(k, par, first, side).wait_send()

    def pack_all(rows):
        packed = [[zero, zero], [zero, zero]]
        for r in range(ROWS):
            for i in range(3):
                part = shift(jnp.where(on_edge, rows(r, i), 0.0), i * ROWS + r)
                packed[r & 1][(r >> 1) & 1] = packed[r & 1][(r >> 1) & 1] + part
        return packed[0][0] + packed[0][1], packed[1][0] + packed[1][1]

    def find(rows):
        @on_rim(north, south)
        def _():
            for i, v in enumerate(collect(ns_site, rows, 3)):
                found[i] = v

        @on_rim(west, east)
        def _():
            for i, v in enumerate(collect(we_site, rows, 3)):
                found[3 + i] = v

    def rotated(values, angle):
        a, b, d = values
        cos, sin = found[angle], found[angle + 1]
        return a, cos * b + sin * d, cos * d - sin * b

    def send_found(k, par, first, patch):
        @on_rim(north, south)
        def _():
            values = patch([found[i] for i in range(3)], ns_site)
            for i, v in enumerate(rotated(values, 6)):
                send_ns[k, south, i] = v

            @pl.when(north == 1)
            def _():
                start(k, par, first, 0)

            @pl.when(south == 1)
            def _():
                start(k, par, first, 1)

        @on_rim(west, east)
        def _():
            values = patch([found[3 + i] for i in range(3)], we_site)
            a, b, d = rotated(values, 8)
            send_we[k, east, 0] = jnp.where(slot_part == 0, a, jnp.where(slot_part == 1, b, d))

            @pl.when(west == 1)
            def _():
                start(k, par, first, 2)

            @pl.when(east == 1)
            def _():
                start(k, par, first, 3)

    def send_inside(k, par, first, which=(2, 3, 0, 1)):
        for side in which:

            @pl.when(at_rim[side] == 0)
            def _(side=side):
                start(k, par, first, side)

    @on_rim(north, south)
    def _():
        found[6], found[7] = jnp.cos(ns_angle), jnp.sin(ns_angle)

    @on_rim(west, east)
    def _():
        found[8], found[9] = jnp.cos(we_angle), jnp.sin(we_angle)

    pltpu.make_async_copy(flow, flow, in_sem.at[3]).wait()
    even, odd = pack_all(flow_row)
    pltpu.make_async_copy(heat, heat, in_sem.at[4]).wait()
    near_edge = (lane < 2) | (lane >= COLS - 2)
    heat_packed = [zero, zero]
    for r in range(ROWS):
        part = shift(jnp.where(near_edge, heat_row(r), 0.0), 4 * r)
        heat_packed[r & 1] = heat_packed[r & 1] + part
    heat_packed = heat_packed[0] + heat_packed[1]
    for j in range(2):
        send_ns[0, 0, 3 + j] = heat_row(j)
        send_ns[0, 1, 3 + j] = heat_row(ROWS - 2 + j)
        send_we[0, j, 1] = heat_packed
    for i in range(3):
        send_ns[0, 0, i] = flow[0, i]
        send_ns[0, 1, i] = flow[ROWS - 1, i]
    send_we[0, 0, 0] = jnp.where(is_even, even, odd)
    send_we[0, 1, 0] = jnp.where(is_even, odd, even)

    pl.semaphore_wait(barrier, 4)
    send_inside(0, 0, True)

    @on_rim(north, south)
    def _():
        for j in range(2):
            send_ns[0, south, 3 + j] = collect(ns_heat[j], lambda r, _: heat_row(r), 1)[0]

    @on_rim(west, east)
    def _():
        send_we[0, east, 1] = collect(we_heat, lambda r, _: heat_row(r), 1)[0]

    find(flow_row)
    send_found(0, 0, True, lambda values, index: values)

    def relax(rows, source=None, result=flow):
        before = [zero] * 3
        now = [rows(0, i) for i in range(3)]
        for r in range(ROWS):
            after = [rows(r + 1, i) for i in range(3)] if r < ROWS - 1 else [zero] * 3
            for i in range(3):
                here = now[i]
                near = (
                    (before[i] + after[i])
                    + jnp.where(lane == 0, 0.0, shift(here, 1))
                    + jnp.where(lane == COLS - 1, 0.0, shift(here, -1))
                )
                value = (
                    coef * near
                    + above_coef * pltpu.roll(here, LEVELS - 1, 0)
                    + below_coef * pltpu.roll(here, 1, 0)
                )
                if i == 0 and source is not None:
                    value = value + source[r]
                result[r, i] = value
            before, now = now, after

    def halo_share(k):
        first_cols, last_cols = halo_we[k, 1, 0], shift(halo_we[k, 0, 0], 2)
        share = [coef * halo_ns[k, side, i] for side in range(2) for i in range(3)]
        share.append(coef * jnp.where(is_even, first_cols, last_cols))
        share.append(coef * jnp.where(is_even, last_cols, first_cols))
        return share

    def completed(k):
        return with_halo(lambda r, i: flow[r, i], halo_share(k), on_edge)

    def send_edges(k, par, even, odd, heat=None):
        above = [coef * halo_ns[k, 0, i] for i in range(3)]
        below = [coef * halo_ns[k, 1, i] for i in range(3)]
        last, first = coef * halo_we[k, 0, 0], coef * halo_we[k, 1, 0]
        for i in range(3):
            even = even + shift(jnp.where(on_edge, above[i], 0.0), i * ROWS)
            odd = odd + shift(jnp.where(on_edge, below[i], 0.0), i * ROWS + ROWS - 1)
        to_west, to_east = shift(last, 1), shift(first, -1)
        if heat is not None:
            heat_rows, heat_cols = heat
            for r, value in heat_rows.items():
                part = shift(jnp.where(on_edge, value, 0.0), r)
                even, odd = (even, odd + part) if r & 1 else (even + part, odd)
            at_first = lane_take(heat_cols, (4 * lane) & (COLS - 1))
            at_last = lane_take(heat_cols, (4 * lane + 3) & (COLS - 1))
            to_west = to_west + jnp.where(lane < ROWS, at_first, 0.0)
            to_east = to_east + jnp.where(((lane + 1) & (COLS - 1)) < ROWS, at_last, 0.0)
        send_we[k + 1, 0, 0] = jnp.where(is_even, even, odd) + to_west
        send_we[k + 1, 1, 0] = jnp.where(is_even, odd, even) + to_east
        send_inside(k + 1, par, False, (2, 3))
        for own, r, halo in ((0, 0, above), (1, ROWS - 1, below)):
            for i in range(3):
                t = i * ROWS + r
                value = (
                    flow[r, i]
                    + halo[i]
                    + jnp.where(lane == 0, shift(last, 1 - t), 0.0)
                    + jnp.where(lane == COLS - 1, shift(first, COLS - 1 - t), 0.0)
                )
                if i == 0 and heat is not None:
                    cols = jnp.where(near_edge, shift(heat_cols, -4 * r), 0.0)
                    value = value + (heat_rows[r] + cols)
                send_ns[k + 1, own, i] = value
        send_inside(k + 1, par, False, (0, 1))

        def patch(values, index):
            at_row, at_col = index >> 7, index & (COLS - 1)
            for i in range(3):
                slot = i * ROWS + at_row
                add = jnp.where(at_row == 0, lane_take(above[i], at_col), 0.0)
                add = add + jnp.where(at_row == ROWS - 1, lane_take(below[i], at_col), 0.0)
                add = add + jnp.where(at_col == 0, lane_take(last, (slot - 1) & (COLS - 1)), 0.0)
                add = add + jnp.where(at_col == COLS - 1, lane_take(first, slot), 0.0)
                if i == 0 and heat is not None:
                    for r, value in heat_rows.items():
                        add = add + jnp.where(at_row == r, lane_take(value, at_col), 0.0)
                    near = (at_col < 2) | (at_col >= COLS - 2)
                    cols = lane_take(heat_cols, (4 * at_row + at_col) & (COLS - 1))
                    add = add + jnp.where(near, cols, 0.0)
                values[i] = values[i] + add
            return values

        send_found(k + 1, par, False, patch)

    def or_zero(r):
        return heat_row(r) if 0 <= r < ROWS else zero

    for r in range(ROWS):
        up2, up1, here, down1, down2 = (or_zero(r + j) for j in range(-2, 3))
        west1 = jnp.where(lane < 1, 0.0, shift(here, 1))
        west2 = jnp.where(lane < 2, 0.0, shift(here, 2))
        east1 = jnp.where(lane >= COLS - 1, 0.0, shift(here, -1))
        east2 = jnp.where(lane >= COLS - 2, 0.0, shift(here, -2))
        above = jnp.where(level == LEVELS - 1, here, pltpu.roll(here, LEVELS - 1, 0))
        below = jnp.where(level == 0, here, pltpu.roll(here, 1, 0))
        grad_colat = (8.0 * (down1 - up1) - (down2 - up2)) * (1.0 / 12.0)
        grad_lon = (8.0 * (east1 - west1) - (east2 - west2)) * (1.0 / 12.0)
        grad_rad = (above - below) * 0.5
        laplace = down1 + up1 + east1 + west1 + above + below - 6.0 * here
        advect = flow[r, 0] * grad_rad + flow[r, 1] * grad_colat + flow[r, 2] * grad_lon
        stepped = here + TIME_STEP * (laplace - advect)
        heat_out[r] = stepped
        source[r] = buoyancy * stepped
    outer_flow = {r: flow[r, 1] for r in (0, 1, ROWS - 2, ROWS - 1)}
    lon_flow = [zero, zero]
    for r in range(ROWS):
        part = shift(jnp.where(near_edge, flow[r, 2], 0.0), 4 * r)
        lon_flow[r & 1] = lon_flow[r & 1] + part
    lon_flow = (lon_flow[0] + lon_flow[1]) * (1.0 / 12.0)
    relax(flow_row, source)
    even, odd = pack_all(flow_row)
    find(flow_row)
    wait_all(0, 0, True)

    far, nearby = halo_ns[0, 0, 3], halo_ns[0, 0, 4]
    heat_rows = {
        0: TIME_STEP * (nearby + outer_flow[0] * ((8.0 * nearby - far) * (1.0 / 12.0))),
        1: (-TIME_STEP / 12.0) * (outer_flow[1] * nearby),
    }
    nearby, far = halo_ns[0, 1, 3], halo_ns[0, 1, 4]
    heat_rows[ROWS - 2] = (TIME_STEP / 12.0) * (outer_flow[ROWS - 2] * nearby)
    heat_rows[ROWS - 1] = TIME_STEP * (
        nearby - outer_flow[ROWS - 1] * ((8.0 * nearby - far) * (1.0 / 12.0))
    )
    west1, west2 = shift(halo_we[0, 0, 1], 1), shift(halo_we[0, 0, 1], 2)
    east1, east2 = shift(halo_we[0, 1, 1], -1), shift(halo_we[0, 1, 1], -2)
    column = lane & 3
    heat_cols = TIME_STEP * jnp.where(
        column == 0,
        west1 + lon_flow * (8.0 * west1 - west2),
        jnp.where(
            column == 1,
            -lon_flow * west2,
            jnp.where(column == 2, lon_flow * east2, east1 - lon_flow * (8.0 * east1 - east2)),
        ),
    )
    scaled_rows = {r: buoyancy * value for r, value in heat_rows.items()}
    send_edges(0, 1, even, odd, (scaled_rows, buoyancy * heat_cols))
    for r in range(ROWS):
        add = jnp.where(near_edge, shift(heat_cols, -4 * r), 0.0)
        if r in heat_rows:
            add = add + heat_rows[r]
        heat_out[r] = heat_out[r] + add
        add = buoyancy * add
        source[r] = source[r] + add
        flow[r, 0] = flow[r, 0] + add

    def step(k, carry):
        par = k & 1
        relax(completed(k - 1), source)
        even, odd = pack_all(flow_row)
        find(flow_row)

        @pl.when(k > 1)
        def _():
            wait_sent(k - 1, 1 - par, False)

        wait_all(k, par, False)
        send_edges(k, 1 - par, even, odd)
        return carry

    wait_sent(0, 0, True)
    lax.fori_loop(1, ITERS - 1, step, 0)
    relax(completed(ITERS - 2), source, flow_out)
    last_par = (ITERS - 1) & 1
    wait_sent(ITERS - 2, 1 - last_par, False)
    wait_sent(ITERS - 1, last_par, False)
    wait_all(ITERS - 1, last_par, False)
    for n, value in enumerate(halo_share(ITERS - 1)):
        halo_out[n] = value


def deliver(heat_in, flow_in, halo_in, heat_out, flow_out, done, sem):
    for k in range(LEVELS):
        pltpu.make_async_copy(heat_in.at[:, k, :], heat_out.at[k], sem.at[0]).start()
    lane = lax.broadcasted_iota(jnp.int32, (LEVELS, COLS), 1)
    on_edge = (lane == 0) | (lane == COLS - 1)
    rows = with_halo(lambda r, i: flow_in[r, i], [halo_in[n] for n in range(8)], on_edge)

    def send(r):
        pltpu.make_async_copy(done.at[r], flow_out.at[:, :, r, :], sem.at[1]).start()

    lag = 4
    for r in range(ROWS):
        for i in range(3):
            done[r, i] = rows(r, i)
        if r >= lag:
            send(r - lag)
    for r in range(ROWS - lag, ROWS):
        send(r)
    pltpu.make_async_copy(heat_out, heat_out, sem.at[0]).wait()
    pltpu.make_async_copy(flow_out, flow_out, sem.at[1]).wait()


def solution(mesh):
    n_colat, n_lon = mesh.shape["colat"], mesh.shape["lon"]

    block = (LEVELS, COLS)
    heat_shape = jax.ShapeDtypeStruct((LEVELS, ROWS, COLS), jnp.float32)
    flow_shape = jax.ShapeDtypeStruct((3, LEVELS, ROWS, COLS), jnp.float32)
    heat_by_row = jax.ShapeDtypeStruct((ROWS, *block), jnp.float32)
    halo_shape = jax.ShapeDtypeStruct((8, *block), jnp.float32)
    vmem = pl.BlockSpec(memory_space=pltpu.VMEM)
    flow_by_row = jax.ShapeDtypeStruct((ROWS, 3, *block), jnp.float32)
    step = pl.pallas_call(
        lambda *refs: kernel(n_colat, n_lon, *refs),
        out_shape=(heat_by_row, flow_by_row, halo_shape),
        in_specs=[pl.BlockSpec(memory_space=pltpu.HBM)] * 5,
        out_specs=(vmem,) * 3,
        scratch_shapes=[
            pltpu.SMEM((LEVELS,), jnp.float32),
            pltpu.VMEM((1, 1, 4 * (COLS + ROWS)), jnp.int32),
            pltpu.VMEM((1, 1, 2 * (COLS + ROWS)), jnp.float32),
            pltpu.SemaphoreType.DMA((5,)),
            pltpu.VMEM((ROWS, 3, *block), jnp.float32),
            pltpu.VMEM((ROWS, *block), jnp.float32),
            pltpu.VMEM((ROWS, *block), jnp.float32),
            pltpu.VMEM((10, *block), jnp.float32),
            pltpu.VMEM((ITERS, 2, 5, *block), jnp.float32),
            pltpu.VMEM((ITERS, 2, 2, *block), jnp.float32),
            pltpu.VMEM((ITERS, 2, 5, *block), jnp.float32),
            pltpu.VMEM((ITERS, 2, 2, *block), jnp.float32),
            pltpu.SemaphoreType.DMA((2, 4)),
            pltpu.SemaphoreType.DMA((2, 4)),
        ],
        compiler_params=pltpu.CompilerParams(collective_id=0, has_side_effects=True, vmem_limit_bytes=8 << 20),
        name="mantle_step",
    )
    place = pl.pallas_call(
        deliver,
        out_shape=(heat_shape, flow_shape),
        in_specs=[vmem] * 3,
        out_specs=(pl.BlockSpec(memory_space=pltpu.HBM),) * 2,
        scratch_shapes=[
            pltpu.VMEM(flow_by_row.shape, jnp.float32),
            pltpu.SemaphoreType.DMA((2,)),
        ],
        compiler_params=pltpu.CompilerParams(vmem_limit_bytes=4 << 20),
        name="deliver",
    )

    def pinned(*args):
        return step(*(pltpu.with_memory_space_constraint(a, pltpu.HBM) for a in args))

    def on_device(heat, flow, stiffness, site, phase):
        heat_out, flow_out = place(
            *pinned(
                heat.reshape(heat_shape.shape), flow.reshape(flow_shape.shape), stiffness, site, phase,
            )
        )
        return heat_out.reshape(heat.shape), flow_out.reshape(flow.shape)

    return jax.shard_map(
        on_device,
        mesh=mesh,
        in_specs=(
            P("panel", None, "colat", "lon"),
            P("panel", None, None, "colat", "lon"),
            P(),
            P("panel", "colat", "lon"),
            P("panel", "colat", "lon"),
        ),
        out_specs=(P("panel", None, "colat", "lon"), P("panel", None, None, "colat", "lon")),
        check_vma=False,
    )
```

```python
import jax
import jax.numpy as jnp
from jax import lax
from jax.experimental import pallas as pl
from jax.experimental.pallas import tpu as pltpu
from jax.sharding import PartitionSpec as P

ITERS = 8
TIME_STEP = 0.1
BUOYANCY_FACTOR = 10.0
DRAG_COEF = 1.0
MESH = pl.DeviceIdType.MESH
LEVELS, ROWS, COLS = 8, 32, 128


def lane_take(value, index):
    return jnp.take_along_axis(value, index, axis=1, mode="promise_in_bounds")


def with_halo(rows, share, on_edge):
    def complete(r, i):
        by = (COLS - 1 - i * ROWS - r) % COLS
        value = rows(r, i) + jnp.where(on_edge, pltpu.roll(share[6 + (r & 1)], by, 1), 0.0)
        if r == 0:
            value = value + share[i]
        if r == ROWS - 1:
            value = value + share[3 + i]
        return value

    return complete


def kernel(
    n_colat, n_lon,
    heat_hbm, flow_hbm, stiff_hbm, site_hbm, phase_hbm,
    heat_out, flow_out, halo_out,
    stiff_in, site_in, phase_in, in_sem,
    flow, heat, source, found, send_ns, send_we, halo_ns, halo_we, send_sem, recv_sem,
):
    p, c, l = (lax.axis_index(a) for a in ("panel", "colat", "lon"))
    lane = lax.broadcasted_iota(jnp.int32, (LEVELS, COLS), 1)
    level = lax.broadcasted_iota(jnp.int32, (LEVELS, COLS), 0)
    north, south = (c == 0).astype(jnp.int32), (c == n_colat - 1).astype(jnp.int32)
    west, east = (l == 0).astype(jnp.int32), (l == n_lon - 1).astype(jnp.int32)
    at_rim = (north, south, west, east)

    def across(edge):
        return p + edge * (1 - 2 * p)

    sides = (
        ((across(north), c - 1 + north, l), 1 - north),
        ((across(south), c + 1 - south, l), south),
        ((across(west), c, l - 1 + west), 3 - west),
        ((across(east), c, l + 1 - east), 2 + east),
    )
    barrier = pltpu.get_barrier_semaphore()
    for device, _ in sides:
        pl.semaphore_signal(barrier, inc=1, device_id=device, device_id_type=MESH)
    small = [
        pltpu.make_async_copy(src, dst, in_sem.at[n])
        for n, (src, dst) in enumerate(
            ((site_hbm, site_in), (phase_hbm, phase_in), (stiff_hbm, stiff_in))
        )
    ]
    for copy in small:
        copy.start()
    for i in range(3):
        for k in range(LEVELS):
            pltpu.make_async_copy(flow_hbm.at[i, k], flow.at[:, i, k, :], in_sem.at[3]).start()
    for k in range(LEVELS):
        pltpu.make_async_copy(heat_hbm.at[k], heat.at[:, k, :], in_sem.at[4]).start()
    for copy in small:
        copy.wait()

    stiff = jnp.zeros((LEVELS, COLS), jnp.float32)
    for k in range(LEVELS):
        stiff = jnp.where(level == k, stiff_in[k], stiff)
    upper = jnp.where(level < LEVELS - 1, 0.5 * (stiff + pltpu.roll(stiff, LEVELS - 1, 0)), 0.0)
    lower = jnp.where(level > 0, 0.5 * (stiff + pltpu.roll(stiff, 1, 0)), 0.0)
    inverse = 1.0 / (DRAG_COEF + 4.0 * stiff + upper + lower)
    coef, above_coef, below_coef = stiff * inverse, upper * inverse, lower * inverse
    buoyancy = BUOYANCY_FACTOR * inverse

    zero = jnp.zeros((LEVELS, COLS), jnp.float32)
    is_even = (lane & 1) == 0
    on_edge = (lane == 0) | (lane == COLS - 1)

    def shift(value, by):
        return pltpu.roll(value, by % COLS, 1)

    def pick(flag, yes, no):
        return jnp.where(flag == 1, yes, no)

    slot_row, slot_part = lane & (ROWS - 1), lane >> 5
    heat_slot = (lane + 2 * west) & (COLS - 1)

    def sites(j):
        return jnp.broadcast_to(site_in[0, 0:1, COLS * j : COLS * (j + 1)], (LEVELS, COLS))

    ns_site = pick(north, sites(1), sites(2))
    ns_heat = (pick(north, sites(0), sites(2)), pick(north, sites(1), sites(3)))
    we_base = pick(west, 0, 2 * ROWS)
    we_site = lane_take(sites(4), we_base + west + 2 * slot_row)
    we_heat = lane_take(sites(4), we_base + 2 * (heat_slot >> 2) + (heat_slot & 1))
    ns_angle = jnp.broadcast_to(
        pick(north, phase_in[0, 0:1, 0:COLS], phase_in[0, 0:1, COLS : 2 * COLS]), (LEVELS, COLS)
    )
    tail = phase_in[0, 0:1, 2 * COLS : 2 * COLS + 2 * ROWS]
    tail = jnp.broadcast_to(jnp.concatenate([tail, tail], axis=1), (LEVELS, COLS))
    we_angle = lane_take(tail, pick(west, 0, ROWS) + slot_row)

    def heat_row(r):
        return heat[r]

    def collect(index, rows, count):
        at_row, at_col = index >> 7, index & (COLS - 1)
        values = [zero] * count
        for r in range(ROWS):
            here = at_row == r
            values = [
                jnp.where(here, lane_take(rows(r, i), at_col), v) for i, v in enumerate(values)
            ]
        return values

    def flow_row(r, i):
        return flow[r, i]

    def copy(k, par, first, side, arriving=False):
        device, facing = sides[side]
        ns = side < 2
        buf, halo = (send_ns, halo_ns) if ns else (send_we, halo_we)
        own, theirs = (side, facing) if ns else (side - 2, facing - 2)
        n = (5 if first else 3) if ns else (2 if first else 1)

        at, seen = (own, side) if arriving else (theirs, facing)
        return pltpu.make_async_remote_copy(
            src_ref=buf.at[k, own, 0:n],
            dst_ref=halo.at[k, at, 0:n],
            send_sem=send_sem.at[par, side],
            recv_sem=recv_sem.at[par, seen],
            device_id=device,
            device_id_type=MESH,
        )

    def on_rim(flag_a, flag_b):
        return pl.when((flag_a == 1) | (flag_b == 1))

    def start(k, par, first, side):
        copy(k, par, first, side).start()

    def wait_all(k, par, first, which=(0, 1, 2, 3)):
        for side in which:
            copy(k, par, first, side, arriving=True).wait_recv()

    def wait_sent(k, par, first):
        for side in range(4):
            copy(k, par, first, side).wait_send()

    def pack_all(rows):
        packed = [[zero, zero], [zero, zero]]
        for r in range(ROWS):
            for i in range(3):
                part = shift(jnp.where(on_edge, rows(r, i), 0.0), i * ROWS + r)
                packed[r & 1][(r >> 1) & 1] = packed[r & 1][(r >> 1) & 1] + part
        return packed[0][0] + packed[0][1], packed[1][0] + packed[1][1]

    def find(rows):
        @on_rim(north, south)
        def _():
            for i, v in enumerate(collect(ns_site, rows, 3)):
                found[i] = v

        @on_rim(west, east)
        def _():
            for i, v in enumerate(collect(we_site, rows, 3)):
                found[3 + i] = v

    def rotated(values, angle):
        a, b, d = values
        cos, sin = found[angle], found[angle + 1]
        return a, cos * b + sin * d, cos * d - sin * b

    def send_found(k, par, first, patch):
        @on_rim(north, south)
        def _():
            values = patch([found[i] for i in range(3)], ns_site)
            for i, v in enumerate(rotated(values, 6)):
                send_ns[k, south, i] = v

            @pl.when(north == 1)
            def _():
                start(k, par, first, 0)

            @pl.when(south == 1)
            def _():
                start(k, par, first, 1)

        @on_rim(west, east)
        def _():
            values = patch([found[3 + i] for i in range(3)], we_site)
            a, b, d = rotated(values, 8)
            send_we[k, east, 0] = jnp.where(slot_part == 0, a, jnp.where(slot_part == 1, b, d))

            @pl.when(west == 1)
            def _():
                start(k, par, first, 2)

            @pl.when(east == 1)
            def _():
                start(k, par, first, 3)

    def send_inside(k, par, first, which=(2, 3, 0, 1)):
        for side in which:

            @pl.when(at_rim[side] == 0)
            def _(side=side):
                start(k, par, first, side)

    @on_rim(north, south)
    def _():
        found[6], found[7] = jnp.cos(ns_angle), jnp.sin(ns_angle)

    @on_rim(west, east)
    def _():
        found[8], found[9] = jnp.cos(we_angle), jnp.sin(we_angle)

    pltpu.make_async_copy(flow, flow, in_sem.at[3]).wait()
    even, odd = pack_all(flow_row)
    pltpu.make_async_copy(heat, heat, in_sem.at[4]).wait()
    near_edge = (lane < 2) | (lane >= COLS - 2)
    heat_packed = [zero, zero]
    for r in range(ROWS):
        part = shift(jnp.where(near_edge, heat_row(r), 0.0), 4 * r)
        heat_packed[r & 1] = heat_packed[r & 1] + part
    heat_packed = heat_packed[0] + heat_packed[1]
    for j in range(2):
        send_ns[0, 0, 3 + j] = heat_row(j)
        send_ns[0, 1, 3 + j] = heat_row(ROWS - 2 + j)
        send_we[0, j, 1] = heat_packed
    for i in range(3):
        send_ns[0, 0, i] = flow[0, i]
        send_ns[0, 1, i] = flow[ROWS - 1, i]
    send_we[0, 0, 0] = jnp.where(is_even, even, odd)
    send_we[0, 1, 0] = shift(jnp.where(is_even, odd, even), 1)


    @on_rim(north, south)
    def _():
        for j in range(2):
            send_ns[0, south, 3 + j] = collect(ns_heat[j], lambda r, _: heat_row(r), 1)[0]

    @on_rim(west, east)
    def _():
        send_we[0, east, 1] = collect(we_heat, lambda r, _: heat_row(r), 1)[0]

    find(flow_row)
    pl.semaphore_wait(barrier, 4)
    send_inside(0, 0, True)
    send_found(0, 0, True, lambda values, index: values)

    def relax(rows, source=None, result=flow):
        before = [zero] * 3
        now = [rows(0, i) for i in range(3)]
        for r in range(ROWS):
            after = [rows(r + 1, i) for i in range(3)] if r < ROWS - 1 else [zero] * 3
            for i in range(3):
                here = now[i]
                near = (
                    (before[i] + after[i])
                    + jnp.where(lane == 0, 0.0, shift(here, 1))
                    + jnp.where(lane == COLS - 1, 0.0, shift(here, -1))
                )
                value = (
                    coef * near
                    + above_coef * pltpu.roll(here, LEVELS - 1, 0)
                    + below_coef * pltpu.roll(here, 1, 0)
                )
                if i == 0 and source is not None:
                    value = value + source[r]
                result[r, i] = value
            before, now = now, after

    def halo_share(k):
        first_cols, last_cols = halo_we[k, 1, 0], shift(halo_we[k, 0, 0], 1)
        share = [coef * halo_ns[k, side, i] for side in range(2) for i in range(3)]
        share.append(coef * jnp.where(is_even, first_cols, last_cols))
        share.append(coef * jnp.where(is_even, last_cols, first_cols))
        return share

    def completed(k):
        return with_halo(lambda r, i: flow[r, i], halo_share(k), on_edge)

    def send_edges(k, par, even, odd, heat=None):
        above = [coef * halo_ns[k, 0, i] for i in range(3)]
        below = [coef * halo_ns[k, 1, i] for i in range(3)]
        for i in range(3):
            even = even + shift(jnp.where(on_edge, above[i], 0.0), i * ROWS)
            odd = odd + shift(jnp.where(on_edge, below[i], 0.0), i * ROWS + ROWS - 1)
        if heat is not None:
            heat_rows, heat_cols = heat
            for r, value in heat_rows.items():
                part = shift(jnp.where(on_edge, value, 0.0), r)
                even, odd = (even, odd + part) if r & 1 else (even + part, odd)
        west_edge, east_edge = jnp.where(is_even, even, odd), shift(jnp.where(is_even, odd, even), 1)
        outer = [[flow[0, i] + above[i] for i in range(3)], [flow[ROWS - 1, i] + below[i] for i in range(3)]]
        if heat is None:
            wait_all(k, 1 - par, False, (2, 3))
        last, first = coef * halo_we[k, 0, 0], coef * halo_we[k, 1, 0]
        to_west, to_east = last, first
        if heat is not None:
            at_first = lane_take(heat_cols, (4 * lane) & (COLS - 1))
            at_last = lane_take(heat_cols, (4 * lane - 1) & (COLS - 1))
            to_west = to_west + jnp.where(lane < ROWS, at_first, 0.0)
            to_east = to_east + jnp.where(lane < ROWS, at_last, 0.0)
        send_we[k + 1, 0, 0] = west_edge + to_west
        send_we[k + 1, 1, 0] = east_edge + to_east
        send_inside(k + 1, par, False, (2, 3))
        for own, r in ((0, 0), (1, ROWS - 1)):
            for i in range(3):
                t = i * ROWS + r
                value = (
                    outer[own][i]
                    + jnp.where(lane == 0, shift(last, -t), 0.0)
                    + jnp.where(lane == COLS - 1, shift(first, COLS - 1 - t), 0.0)
                )
                if i == 0 and heat is not None:
                    cols = jnp.where(near_edge, shift(heat_cols, -4 * r), 0.0)
                    value = value + (heat_rows[r] + cols)
                send_ns[k + 1, own, i] = value
        send_inside(k + 1, par, False, (0, 1))

        def patch(values, index):
            at_row, at_col = index >> 7, index & (COLS - 1)
            for i in range(3):
                slot = i * ROWS + at_row
                add = jnp.where(at_row == 0, lane_take(above[i], at_col), 0.0)
                add = add + jnp.where(at_row == ROWS - 1, lane_take(below[i], at_col), 0.0)
                add = add + jnp.where(at_col == 0, lane_take(last, slot), 0.0)
                add = add + jnp.where(at_col == COLS - 1, lane_take(first, slot), 0.0)
                if i == 0 and heat is not None:
                    for r, value in heat_rows.items():
                        add = add + jnp.where(at_row == r, lane_take(value, at_col), 0.0)
                    near = (at_col < 2) | (at_col >= COLS - 2)
                    cols = lane_take(heat_cols, (4 * at_row + at_col) & (COLS - 1))
                    add = add + jnp.where(near, cols, 0.0)
                values[i] = values[i] + add
            return values

        send_found(k + 1, par, False, patch)

    def or_zero(r):
        return heat_row(r) if 0 <= r < ROWS else zero

    for r in range(ROWS):
        up2, up1, here, down1, down2 = (or_zero(r + j) for j in range(-2, 3))
        west1 = jnp.where(lane < 1, 0.0, shift(here, 1))
        west2 = jnp.where(lane < 2, 0.0, shift(here, 2))
        east1 = jnp.where(lane >= COLS - 1, 0.0, shift(here, -1))
        east2 = jnp.where(lane >= COLS - 2, 0.0, shift(here, -2))
        above = jnp.where(level == LEVELS - 1, here, pltpu.roll(here, LEVELS - 1, 0))
        below = jnp.where(level == 0, here, pltpu.roll(here, 1, 0))
        grad_colat = (8.0 * (down1 - up1) - (down2 - up2)) * (1.0 / 12.0)
        grad_lon = (8.0 * (east1 - west1) - (east2 - west2)) * (1.0 / 12.0)
        grad_rad = (above - below) * 0.5
        laplace = down1 + up1 + east1 + west1 + above + below - 6.0 * here
        advect = flow[r, 0] * grad_rad + flow[r, 1] * grad_colat + flow[r, 2] * grad_lon
        stepped = here + TIME_STEP * (laplace - advect)
        heat_out[r] = stepped
        source[r] = buoyancy * stepped
    outer_flow = {r: flow[r, 1] for r in (0, 1, ROWS - 2, ROWS - 1)}
    lon_flow = [zero, zero]
    for r in range(ROWS):
        part = shift(jnp.where(near_edge, flow[r, 2], 0.0), 4 * r)
        lon_flow[r & 1] = lon_flow[r & 1] + part
    lon_flow = (lon_flow[0] + lon_flow[1]) * (1.0 / 12.0)
    relax(flow_row, source)
    even, odd = pack_all(flow_row)
    find(flow_row)
    wait_all(0, 0, True)

    far, nearby = halo_ns[0, 0, 3], halo_ns[0, 0, 4]
    heat_rows = {
        0: TIME_STEP * (nearby + outer_flow[0] * ((8.0 * nearby - far) * (1.0 / 12.0))),
        1: (-TIME_STEP / 12.0) * (outer_flow[1] * nearby),
    }
    nearby, far = halo_ns[0, 1, 3], halo_ns[0, 1, 4]
    heat_rows[ROWS - 2] = (TIME_STEP / 12.0) * (outer_flow[ROWS - 2] * nearby)
    heat_rows[ROWS - 1] = TIME_STEP * (
        nearby - outer_flow[ROWS - 1] * ((8.0 * nearby - far) * (1.0 / 12.0))
    )
    west1, west2 = shift(halo_we[0, 0, 1], 1), shift(halo_we[0, 0, 1], 2)
    east1, east2 = shift(halo_we[0, 1, 1], -1), shift(halo_we[0, 1, 1], -2)
    column = lane & 3
    heat_cols = TIME_STEP * jnp.where(
        column == 0,
        west1 + lon_flow * (8.0 * west1 - west2),
        jnp.where(
            column == 1,
            -lon_flow * west2,
            jnp.where(column == 2, lon_flow * east2, east1 - lon_flow * (8.0 * east1 - east2)),
        ),
    )
    scaled_rows = {r: buoyancy * value for r, value in heat_rows.items()}
    send_edges(0, 1, even, odd, (scaled_rows, buoyancy * heat_cols))
    for r in range(ROWS):
        add = jnp.where(near_edge, shift(heat_cols, -4 * r), 0.0)
        if r in heat_rows:
            add = add + heat_rows[r]
        heat_out[r] = heat_out[r] + add
        add = buoyancy * add
        source[r] = source[r] + add
        flow[r, 0] = flow[r, 0] + add

    def step(k, carry):
        par = k & 1
        relax(completed(k - 1), source)
        even, odd = pack_all(flow_row)
        find(flow_row)

        @pl.when(k > 1)
        def _():
            wait_sent(k - 1, 1 - par, False)

        wait_all(k, par, False, (0, 1))
        send_edges(k, 1 - par, even, odd)
        return carry

    wait_sent(0, 0, True)
    lax.fori_loop(1, ITERS - 1, step, 0)
    relax(completed(ITERS - 2), source, flow_out)
    last_par = (ITERS - 1) & 1
    wait_sent(ITERS - 2, 1 - last_par, False)
    wait_sent(ITERS - 1, last_par, False)
    wait_all(ITERS - 1, last_par, False)
    for n, value in enumerate(halo_share(ITERS - 1)):
        halo_out[n] = value


def deliver(heat_in, flow_in, halo_in, heat_out, flow_out, done, sem):
    for k in range(LEVELS):
        pltpu.make_async_copy(heat_in.at[:, k, :], heat_out.at[k], sem.at[0]).start()
    lane = lax.broadcasted_iota(jnp.int32, (LEVELS, COLS), 1)
    on_edge = (lane == 0) | (lane == COLS - 1)
    rows = with_halo(lambda r, i: flow_in[r, i], [halo_in[n] for n in range(8)], on_edge)

    def send(r):
        pltpu.make_async_copy(done.at[r], flow_out.at[:, :, r, :], sem.at[1]).start()

    lag = 4
    for r in range(ROWS):
        for i in range(3):
            done[r, i] = rows(r, i)
        if r >= lag:
            send(r - lag)
    for r in range(ROWS - lag, ROWS):
        send(r)
    pltpu.make_async_copy(heat_out, heat_out, sem.at[0]).wait()
    pltpu.make_async_copy(flow_out, flow_out, sem.at[1]).wait()


def solution(mesh):
    n_colat, n_lon = mesh.shape["colat"], mesh.shape["lon"]

    block = (LEVELS, COLS)
    heat_shape = jax.ShapeDtypeStruct((LEVELS, ROWS, COLS), jnp.float32)
    flow_shape = jax.ShapeDtypeStruct((3, LEVELS, ROWS, COLS), jnp.float32)
    heat_by_row = jax.ShapeDtypeStruct((ROWS, *block), jnp.float32)
    halo_shape = jax.ShapeDtypeStruct((8, *block), jnp.float32)
    vmem = pl.BlockSpec(memory_space=pltpu.VMEM)
    flow_by_row = jax.ShapeDtypeStruct((ROWS, 3, *block), jnp.float32)
    step = pl.pallas_call(
        lambda *refs: kernel(n_colat, n_lon, *refs),
        out_shape=(heat_by_row, flow_by_row, halo_shape),
        in_specs=[pl.BlockSpec(memory_space=pltpu.HBM)] * 5,
        out_specs=(vmem,) * 3,
        scratch_shapes=[
            pltpu.SMEM((LEVELS,), jnp.float32),
            pltpu.VMEM((1, 1, 4 * (COLS + ROWS)), jnp.int32),
            pltpu.VMEM((1, 1, 2 * (COLS + ROWS)), jnp.float32),
            pltpu.SemaphoreType.DMA((5,)),
            pltpu.VMEM((ROWS, 3, *block), jnp.float32),
            pltpu.VMEM((ROWS, *block), jnp.float32),
            pltpu.VMEM((ROWS, *block), jnp.float32),
            pltpu.VMEM((10, *block), jnp.float32),
            pltpu.VMEM((ITERS, 2, 5, *block), jnp.float32),
            pltpu.VMEM((ITERS, 2, 2, *block), jnp.float32),
            pltpu.VMEM((ITERS, 2, 5, *block), jnp.float32),
            pltpu.VMEM((ITERS, 2, 2, *block), jnp.float32),
            pltpu.SemaphoreType.DMA((2, 4)),
            pltpu.SemaphoreType.DMA((2, 4)),
        ],
        compiler_params=pltpu.CompilerParams(collective_id=0, has_side_effects=True, vmem_limit_bytes=8 << 20),
        name="mantle_step",
    )
    place = pl.pallas_call(
        deliver,
        out_shape=(heat_shape, flow_shape),
        in_specs=[vmem] * 3,
        out_specs=(pl.BlockSpec(memory_space=pltpu.HBM),) * 2,
        scratch_shapes=[
            pltpu.VMEM(flow_by_row.shape, jnp.float32),
            pltpu.SemaphoreType.DMA((2,)),
        ],
        compiler_params=pltpu.CompilerParams(vmem_limit_bytes=4 << 20),
        name="deliver",
    )

    def pinned(*args):
        return step(*(pltpu.with_memory_space_constraint(a, pltpu.HBM) for a in args))

    def on_device(heat, flow, stiffness, site, phase):
        heat_out, flow_out = place(
            *pinned(
                heat.reshape(heat_shape.shape), flow.reshape(flow_shape.shape), stiffness, site, phase,
            )
        )
        return heat_out.reshape(heat.shape), flow_out.reshape(flow.shape)

    return jax.shard_map(
        on_device,
        mesh=mesh,
        in_specs=(
            P("panel", None, "colat", "lon"),
            P("panel", None, None, "colat", "lon"),
            P(),
            P("panel", "colat", "lon"),
            P("panel", "colat", "lon"),
        ),
        out_specs=(P("panel", None, "colat", "lon"), P("panel", None, None, "colat", "lon")),
        check_vma=False,
    )
```

```python
import jax
import jax.numpy as jnp
from jax import lax
from jax.experimental import pallas as pl
from jax.experimental.pallas import tpu as pltpu
from jax.sharding import PartitionSpec as P

ITERS = 8
TIME_STEP = 0.1
BUOYANCY_FACTOR = 10.0
DRAG_COEF = 1.0
MESH = pl.DeviceIdType.MESH
LEVELS, ROWS, COLS = 8, 32, 128


def lane_take(value, index):
    return jnp.take_along_axis(value, index, axis=1, mode="promise_in_bounds")


def with_halo(rows, share, on_edge):
    def complete(r, i):
        by = (COLS - 1 - i * ROWS - r) % COLS
        value = rows(r, i) + jnp.where(on_edge, pltpu.roll(share[6 + (r & 1)], by, 1), 0.0)
        if r == 0:
            value = value + share[i]
        if r == ROWS - 1:
            value = value + share[3 + i]
        return value

    return complete


def kernel(
    n_colat, n_lon,
    heat_hbm, flow_hbm, stiff_hbm, site_hbm, phase_hbm,
    heat_out, flow_out, halo_out,
    stiff_in, site_in, phase_in, in_sem,
    flow, heat, source, found, send_ns, send_we, halo_ns, halo_we, send_sem, recv_sem,
):
    p, c, l = (lax.axis_index(a) for a in ("panel", "colat", "lon"))
    lane = lax.broadcasted_iota(jnp.int32, (LEVELS, COLS), 1)
    level = lax.broadcasted_iota(jnp.int32, (LEVELS, COLS), 0)
    north, south = (c == 0).astype(jnp.int32), (c == n_colat - 1).astype(jnp.int32)
    west, east = (l == 0).astype(jnp.int32), (l == n_lon - 1).astype(jnp.int32)
    at_rim = (north, south, west, east)

    def across(edge):
        return p + edge * (1 - 2 * p)

    sides = (
        ((across(north), c - 1 + north, l), 1 - north),
        ((across(south), c + 1 - south, l), south),
        ((across(west), c, l - 1 + west), 3 - west),
        ((across(east), c, l + 1 - east), 2 + east),
    )
    barrier = pltpu.get_barrier_semaphore()
    for device, _ in sides:
        pl.semaphore_signal(barrier, inc=1, device_id=device, device_id_type=MESH)
    small = [
        pltpu.make_async_copy(src, dst, in_sem.at[n])
        for n, (src, dst) in enumerate(
            ((site_hbm, site_in), (phase_hbm, phase_in), (stiff_hbm, stiff_in))
        )
    ]
    for copy in small:
        copy.start()
    for i in range(3):
        for k in range(LEVELS):
            pltpu.make_async_copy(flow_hbm.at[i, k], flow.at[:, i, k, :], in_sem.at[3]).start()
    for k in range(LEVELS):
        pltpu.make_async_copy(heat_hbm.at[k], heat.at[:, k, :], in_sem.at[4]).start()
    for copy in small:
        copy.wait()

    stiff = jnp.zeros((LEVELS, COLS), jnp.float32)
    for k in range(LEVELS):
        stiff = jnp.where(level == k, stiff_in[k], stiff)
    upper = jnp.where(level < LEVELS - 1, 0.5 * (stiff + pltpu.roll(stiff, LEVELS - 1, 0)), 0.0)
    lower = jnp.where(level > 0, 0.5 * (stiff + pltpu.roll(stiff, 1, 0)), 0.0)
    inverse = 1.0 / (DRAG_COEF + 4.0 * stiff + upper + lower)
    coef, above_coef, below_coef = stiff * inverse, upper * inverse, lower * inverse
    buoyancy = BUOYANCY_FACTOR * inverse

    zero = jnp.zeros((LEVELS, COLS), jnp.float32)
    is_even = (lane & 1) == 0
    on_edge = (lane == 0) | (lane == COLS - 1)

    def shift(value, by):
        return pltpu.roll(value, by % COLS, 1)

    def pick(flag, yes, no):
        return jnp.where(flag == 1, yes, no)

    slot_row, slot_part = lane & (ROWS - 1), lane >> 5
    heat_slot = (lane + 2 * west) & (COLS - 1)

    def sites(j):
        return jnp.broadcast_to(site_in[0, 0:1, COLS * j : COLS * (j + 1)], (LEVELS, COLS))

    ns_site = pick(north, sites(1), sites(2))
    ns_heat = (pick(north, sites(0), sites(2)), pick(north, sites(1), sites(3)))
    we_base = pick(west, 0, 2 * ROWS)
    we_site = lane_take(sites(4), we_base + west + 2 * slot_row)
    we_heat = lane_take(sites(4), we_base + 2 * (heat_slot >> 2) + (heat_slot & 1))
    ns_angle = jnp.broadcast_to(
        pick(north, phase_in[0, 0:1, 0:COLS], phase_in[0, 0:1, COLS : 2 * COLS]), (LEVELS, COLS)
    )
    tail = phase_in[0, 0:1, 2 * COLS : 2 * COLS + 2 * ROWS]
    tail = jnp.broadcast_to(jnp.concatenate([tail, tail], axis=1), (LEVELS, COLS))
    we_angle = lane_take(tail, pick(west, 0, ROWS) + slot_row)

    def heat_row(r):
        return heat[r]

    def collect(index, rows, count):
        at_row, at_col = index >> 7, index & (COLS - 1)
        values = [zero] * count
        for r in range(ROWS):
            here = at_row == r
            values = [
                jnp.where(here, lane_take(rows(r, i), at_col), v) for i, v in enumerate(values)
            ]
        return values

    def flow_row(r, i):
        return flow[r, i]

    def copy(k, par, first, side, arriving=False):
        device, facing = sides[side]
        ns = side < 2
        buf, halo = (send_ns, halo_ns) if ns else (send_we, halo_we)
        own, theirs = (side, facing) if ns else (side - 2, facing - 2)
        n = (5 if first else 3) if ns else (2 if first else 1)

        at, seen = (own, side) if arriving else (theirs, facing)
        return pltpu.make_async_remote_copy(
            src_ref=buf.at[k, own, 0:n],
            dst_ref=halo.at[k, at, 0:n],
            send_sem=send_sem.at[par, side],
            recv_sem=recv_sem.at[par, seen],
            device_id=device,
            device_id_type=MESH,
        )

    def on_rim(flag_a, flag_b):
        return pl.when((flag_a == 1) | (flag_b == 1))

    def start(k, par, first, side):
        copy(k, par, first, side).start()

    def wait_all(k, par, first, which=(0, 1, 2, 3)):
        for side in which:
            copy(k, par, first, side, arriving=True).wait_recv()

    def wait_sent(k, par, first):
        for side in range(4):
            copy(k, par, first, side).wait_send()

    def pack_all(rows):
        packed = [[zero, zero], [zero, zero]]
        for r in range(ROWS):
            for i in range(3):
                part = shift(jnp.where(on_edge, rows(r, i), 0.0), i * ROWS + r)
                packed[r & 1][(r >> 1) & 1] = packed[r & 1][(r >> 1) & 1] + part
        return packed[0][0] + packed[0][1], packed[1][0] + packed[1][1]

    def find(rows):
        @on_rim(north, south)
        def _():
            for i, v in enumerate(collect(ns_site, rows, 3)):
                found[i] = v

        @on_rim(west, east)
        def _():
            for i, v in enumerate(collect(we_site, rows, 3)):
                found[3 + i] = v

    def rotated(values, angle):
        a, b, d = values
        cos, sin = found[angle], found[angle + 1]
        return a, cos * b + sin * d, cos * d - sin * b

    def send_found_rows(k, par, first, patch):
        @on_rim(north, south)
        def _():
            values = patch([found[i] for i in range(3)], ns_site)
            for i, v in enumerate(rotated(values, 6)):
                send_ns[k, south, i] = v

            @pl.when(north == 1)
            def _():
                start(k, par, first, 0)

            @pl.when(south == 1)
            def _():
                start(k, par, first, 1)

    def send_found_cols(k, par, first, patch):
        @on_rim(west, east)
        def _():
            values = patch([found[3 + i] for i in range(3)], we_site)
            a, b, d = rotated(values, 8)
            send_we[k, east, 0] = jnp.where(slot_part == 0, a, jnp.where(slot_part == 1, b, d))

            @pl.when(west == 1)
            def _():
                start(k, par, first, 2)

            @pl.when(east == 1)
            def _():
                start(k, par, first, 3)

    def send_inside(k, par, first, which=(2, 3, 0, 1)):
        for side in which:

            @pl.when(at_rim[side] == 0)
            def _(side=side):
                start(k, par, first, side)

    @on_rim(north, south)
    def _():
        found[6], found[7] = jnp.cos(ns_angle), jnp.sin(ns_angle)

    @on_rim(west, east)
    def _():
        found[8], found[9] = jnp.cos(we_angle), jnp.sin(we_angle)

    pltpu.make_async_copy(flow, flow, in_sem.at[3]).wait()
    even, odd = pack_all(flow_row)
    pltpu.make_async_copy(heat, heat, in_sem.at[4]).wait()
    near_edge = (lane < 2) | (lane >= COLS - 2)
    heat_packed = [zero, zero]
    for r in range(ROWS):
        part = shift(jnp.where(near_edge, heat_row(r), 0.0), 4 * r)
        heat_packed[r & 1] = heat_packed[r & 1] + part
    heat_packed = heat_packed[0] + heat_packed[1]
    for j in range(2):
        send_ns[0, 0, 3 + j] = heat_row(j)
        send_ns[0, 1, 3 + j] = heat_row(ROWS - 2 + j)
        send_we[0, j, 1] = heat_packed
    for i in range(3):
        send_ns[0, 0, i] = flow[0, i]
        send_ns[0, 1, i] = flow[ROWS - 1, i]
    send_we[0, 0, 0] = jnp.where(is_even, even, odd)
    send_we[0, 1, 0] = shift(jnp.where(is_even, odd, even), 1)


    @on_rim(north, south)
    def _():
        for j in range(2):
            send_ns[0, south, 3 + j] = collect(ns_heat[j], lambda r, _: heat_row(r), 1)[0]

    @on_rim(west, east)
    def _():
        send_we[0, east, 1] = collect(we_heat, lambda r, _: heat_row(r), 1)[0]

    find(flow_row)
    pl.semaphore_wait(barrier, 4)
    send_inside(0, 0, True)
    send_found_rows(0, 0, True, lambda values, index: values)
    send_found_cols(0, 0, True, lambda values, index: values)

    def relax(rows, source=None, result=flow):
        before = [zero] * 3
        now = [rows(0, i) for i in range(3)]
        for r in range(ROWS):
            after = [rows(r + 1, i) for i in range(3)] if r < ROWS - 1 else [zero] * 3
            for i in range(3):
                here = now[i]
                near = (
                    (before[i] + after[i])
                    + jnp.where(lane == 0, 0.0, shift(here, 1))
                    + jnp.where(lane == COLS - 1, 0.0, shift(here, -1))
                )
                value = (
                    coef * near
                    + above_coef * pltpu.roll(here, LEVELS - 1, 0)
                    + below_coef * pltpu.roll(here, 1, 0)
                )
                if i == 0 and source is not None:
                    value = value + source[r]
                result[r, i] = value
            before, now = now, after

    def halo_share(k):
        first_cols, last_cols = halo_we[k, 1, 0], shift(halo_we[k, 0, 0], 1)
        share = [coef * halo_ns[k, side, i] for side in range(2) for i in range(3)]
        share.append(coef * jnp.where(is_even, first_cols, last_cols))
        share.append(coef * jnp.where(is_even, last_cols, first_cols))
        return share

    def completed(k):
        return with_halo(lambda r, i: flow[r, i], halo_share(k), on_edge)

    def send_edges(k, par, even, odd, heat=None):
        above = [coef * halo_ns[k, 0, i] for i in range(3)]
        below = [coef * halo_ns[k, 1, i] for i in range(3)]
        for i in range(3):
            even = even + shift(jnp.where(on_edge, above[i], 0.0), i * ROWS)
            odd = odd + shift(jnp.where(on_edge, below[i], 0.0), i * ROWS + ROWS - 1)
        if heat is not None:
            heat_rows, heat_cols = heat
            for r, value in heat_rows.items():
                part = shift(jnp.where(on_edge, value, 0.0), r)
                even, odd = (even, odd + part) if r & 1 else (even + part, odd)
        west_edge, east_edge = jnp.where(is_even, even, odd), shift(jnp.where(is_even, odd, even), 1)
        outer = [[flow[0, i] + above[i] for i in range(3)], [flow[ROWS - 1, i] + below[i] for i in range(3)]]
        if heat is None:
            wait_all(k, 1 - par, False, (2, 3))
        last, first = coef * halo_we[k, 0, 0], coef * halo_we[k, 1, 0]
        to_west, to_east = last, first
        if heat is not None:
            at_first = lane_take(heat_cols, (4 * lane) & (COLS - 1))
            at_last = lane_take(heat_cols, (4 * lane - 1) & (COLS - 1))
            to_west = to_west + jnp.where(lane < ROWS, at_first, 0.0)
            to_east = to_east + jnp.where(lane < ROWS, at_last, 0.0)
        send_we[k + 1, 0, 0] = west_edge + to_west
        send_we[k + 1, 1, 0] = east_edge + to_east
        send_inside(k + 1, par, False, (2, 3))

        def patch(values, index):
            at_row, at_col = index >> 7, index & (COLS - 1)
            for i in range(3):
                slot = i * ROWS + at_row
                add = jnp.where(at_row == 0, lane_take(above[i], at_col), 0.0)
                add = add + jnp.where(at_row == ROWS - 1, lane_take(below[i], at_col), 0.0)
                add = add + jnp.where(at_col == 0, lane_take(last, slot), 0.0)
                add = add + jnp.where(at_col == COLS - 1, lane_take(first, slot), 0.0)
                if i == 0 and heat is not None:
                    for r, value in heat_rows.items():
                        add = add + jnp.where(at_row == r, lane_take(value, at_col), 0.0)
                    near = (at_col < 2) | (at_col >= COLS - 2)
                    cols = lane_take(heat_cols, (4 * at_row + at_col) & (COLS - 1))
                    add = add + jnp.where(near, cols, 0.0)
                values[i] = values[i] + add
            return values

        send_found_rows(k + 1, par, False, patch)
        values = ([], [])
        for own, r in ((0, 0), (1, ROWS - 1)):
            for i in range(3):
                t = i * ROWS + r
                value = (
                    outer[own][i]
                    + jnp.where(lane == 0, shift(last, -t), 0.0)
                    + jnp.where(lane == COLS - 1, shift(first, COLS - 1 - t), 0.0)
                )
                if i == 0 and heat is not None:
                    cols = jnp.where(near_edge, shift(heat_cols, -4 * r), 0.0)
                    value = value + (heat_rows[r] + cols)
                values[own].append(value)
        for own in range(2):

            @pl.when(at_rim[own] == 0)
            def _(own=own):
                for i in range(3):
                    send_ns[k + 1, own, i] = values[own][i]
                start(k + 1, par, False, own)

        send_found_cols(k + 1, par, False, patch)

    def or_zero(r):
        return heat_row(r) if 0 <= r < ROWS else zero

    for r in range(ROWS):
        up2, up1, here, down1, down2 = (or_zero(r + j) for j in range(-2, 3))
        west1 = jnp.where(lane < 1, 0.0, shift(here, 1))
        west2 = jnp.where(lane < 2, 0.0, shift(here, 2))
        east1 = jnp.where(lane >= COLS - 1, 0.0, shift(here, -1))
        east2 = jnp.where(lane >= COLS - 2, 0.0, shift(here, -2))
        above = jnp.where(level == LEVELS - 1, here, pltpu.roll(here, LEVELS - 1, 0))
        below = jnp.where(level == 0, here, pltpu.roll(here, 1, 0))
        grad_colat = (8.0 * (down1 - up1) - (down2 - up2)) * (1.0 / 12.0)
        grad_lon = (8.0 * (east1 - west1) - (east2 - west2)) * (1.0 / 12.0)
        grad_rad = (above - below) * 0.5
        laplace = down1 + up1 + east1 + west1 + above + below - 6.0 * here
        advect = flow[r, 0] * grad_rad + flow[r, 1] * grad_colat + flow[r, 2] * grad_lon
        stepped = here + TIME_STEP * (laplace - advect)
        heat_out[r] = stepped
        source[r] = buoyancy * stepped
    outer_flow = {r: flow[r, 1] for r in (0, 1, ROWS - 2, ROWS - 1)}
    lon_flow = [zero, zero]
    for r in range(ROWS):
        part = shift(jnp.where(near_edge, flow[r, 2], 0.0), 4 * r)
        lon_flow[r & 1] = lon_flow[r & 1] + part
    lon_flow = (lon_flow[0] + lon_flow[1]) * (1.0 / 12.0)
    relax(flow_row, source)
    even, odd = pack_all(flow_row)
    find(flow_row)
    wait_all(0, 0, True)

    far, nearby = halo_ns[0, 0, 3], halo_ns[0, 0, 4]
    heat_rows = {
        0: TIME_STEP * (nearby + outer_flow[0] * ((8.0 * nearby - far) * (1.0 / 12.0))),
        1: (-TIME_STEP / 12.0) * (outer_flow[1] * nearby),
    }
    nearby, far = halo_ns[0, 1, 3], halo_ns[0, 1, 4]
    heat_rows[ROWS - 2] = (TIME_STEP / 12.0) * (outer_flow[ROWS - 2] * nearby)
    heat_rows[ROWS - 1] = TIME_STEP * (
        nearby - outer_flow[ROWS - 1] * ((8.0 * nearby - far) * (1.0 / 12.0))
    )
    west1, west2 = shift(halo_we[0, 0, 1], 1), shift(halo_we[0, 0, 1], 2)
    east1, east2 = shift(halo_we[0, 1, 1], -1), shift(halo_we[0, 1, 1], -2)
    column = lane & 3
    heat_cols = TIME_STEP * jnp.where(
        column == 0,
        west1 + lon_flow * (8.0 * west1 - west2),
        jnp.where(
            column == 1,
            -lon_flow * west2,
            jnp.where(column == 2, lon_flow * east2, east1 - lon_flow * (8.0 * east1 - east2)),
        ),
    )
    scaled_rows = {r: buoyancy * value for r, value in heat_rows.items()}
    send_edges(0, 1, even, odd, (scaled_rows, buoyancy * heat_cols))
    for r in range(ROWS):
        add = jnp.where(near_edge, shift(heat_cols, -4 * r), 0.0)
        if r in heat_rows:
            add = add + heat_rows[r]
        heat_out[r] = heat_out[r] + add
        add = buoyancy * add
        source[r] = source[r] + add
        flow[r, 0] = flow[r, 0] + add

    def step(k, carry):
        par = k & 1
        relax(completed(k - 1), source)
        even, odd = pack_all(flow_row)
        find(flow_row)

        @pl.when(k > 1)
        def _():
            wait_sent(k - 1, 1 - par, False)

        wait_all(k, par, False, (0, 1))
        send_edges(k, 1 - par, even, odd)
        return carry

    wait_sent(0, 0, True)
    lax.fori_loop(1, ITERS - 1, step, 0)
    relax(completed(ITERS - 2), source, flow_out)
    last_par = (ITERS - 1) & 1
    wait_sent(ITERS - 2, 1 - last_par, False)
    wait_sent(ITERS - 1, last_par, False)
    wait_all(ITERS - 1, last_par, False)
    for n, value in enumerate(halo_share(ITERS - 1)):
        halo_out[n] = value


def deliver(heat_in, flow_in, halo_in, heat_out, flow_out, done, sem):
    for k in range(LEVELS):
        pltpu.make_async_copy(heat_in.at[:, k, :], heat_out.at[k], sem.at[0]).start()
    lane = lax.broadcasted_iota(jnp.int32, (LEVELS, COLS), 1)
    on_edge = (lane == 0) | (lane == COLS - 1)
    rows = with_halo(lambda r, i: flow_in[r, i], [halo_in[n] for n in range(8)], on_edge)

    def send(r):
        pltpu.make_async_copy(done.at[r], flow_out.at[:, :, r, :], sem.at[1]).start()

    lag = 4
    for r in range(ROWS):
        for i in range(3):
            done[r, i] = rows(r, i)
        if r >= lag:
            send(r - lag)
    for r in range(ROWS - lag, ROWS):
        send(r)
    pltpu.make_async_copy(heat_out, heat_out, sem.at[0]).wait()
    pltpu.make_async_copy(flow_out, flow_out, sem.at[1]).wait()


def solution(mesh):
    n_colat, n_lon = mesh.shape["colat"], mesh.shape["lon"]

    block = (LEVELS, COLS)
    heat_shape = jax.ShapeDtypeStruct((LEVELS, ROWS, COLS), jnp.float32)
    flow_shape = jax.ShapeDtypeStruct((3, LEVELS, ROWS, COLS), jnp.float32)
    heat_by_row = jax.ShapeDtypeStruct((ROWS, *block), jnp.float32)
    halo_shape = jax.ShapeDtypeStruct((8, *block), jnp.float32)
    vmem = pl.BlockSpec(memory_space=pltpu.VMEM)
    flow_by_row = jax.ShapeDtypeStruct((ROWS, 3, *block), jnp.float32)
    step = pl.pallas_call(
        lambda *refs: kernel(n_colat, n_lon, *refs),
        out_shape=(heat_by_row, flow_by_row, halo_shape),
        in_specs=[pl.BlockSpec(memory_space=pltpu.HBM)] * 5,
        out_specs=(vmem,) * 3,
        scratch_shapes=[
            pltpu.SMEM((LEVELS,), jnp.float32),
            pltpu.VMEM((1, 1, 4 * (COLS + ROWS)), jnp.int32),
            pltpu.VMEM((1, 1, 2 * (COLS + ROWS)), jnp.float32),
            pltpu.SemaphoreType.DMA((5,)),
            pltpu.VMEM((ROWS, 3, *block), jnp.float32),
            pltpu.VMEM((ROWS, *block), jnp.float32),
            pltpu.VMEM((ROWS, *block), jnp.float32),
            pltpu.VMEM((10, *block), jnp.float32),
            pltpu.VMEM((ITERS, 2, 5, *block), jnp.float32),
            pltpu.VMEM((ITERS, 2, 2, *block), jnp.float32),
            pltpu.VMEM((ITERS, 2, 5, *block), jnp.float32),
            pltpu.VMEM((ITERS, 2, 2, *block), jnp.float32),
            pltpu.SemaphoreType.DMA((2, 4)),
            pltpu.SemaphoreType.DMA((2, 4)),
        ],
        compiler_params=pltpu.CompilerParams(collective_id=0, has_side_effects=True, vmem_limit_bytes=8 << 20),
        name="mantle_step",
    )
    place = pl.pallas_call(
        deliver,
        out_shape=(heat_shape, flow_shape),
        in_specs=[vmem] * 3,
        out_specs=(pl.BlockSpec(memory_space=pltpu.HBM),) * 2,
        scratch_shapes=[
            pltpu.VMEM(flow_by_row.shape, jnp.float32),
            pltpu.SemaphoreType.DMA((2,)),
        ],
        compiler_params=pltpu.CompilerParams(vmem_limit_bytes=4 << 20),
        name="deliver",
    )

    def pinned(*args):
        return step(*(pltpu.with_memory_space_constraint(a, pltpu.HBM) for a in args))

    def on_device(heat, flow, stiffness, site, phase):
        heat_out, flow_out = place(
            *pinned(
                heat.reshape(heat_shape.shape), flow.reshape(flow_shape.shape), stiffness, site, phase,
            )
        )
        return heat_out.reshape(heat.shape), flow_out.reshape(flow.shape)

    return jax.shard_map(
        on_device,
        mesh=mesh,
        in_specs=(
            P("panel", None, "colat", "lon"),
            P("panel", None, None, "colat", "lon"),
            P(),
            P("panel", "colat", "lon"),
            P("panel", "colat", "lon"),
        ),
        out_specs=(P("panel", None, "colat", "lon"), P("panel", None, None, "colat", "lon")),
        check_vma=False,
    )
```

```python
import jax
import jax.numpy as jnp
from jax import lax
from jax.experimental import pallas as pl
from jax.experimental.pallas import tpu as pltpu
from jax.sharding import PartitionSpec as P

ITERS = 8
TIME_STEP = 0.1
BUOYANCY_FACTOR = 10.0
DRAG_COEF = 1.0
MESH = pl.DeviceIdType.MESH
LEVELS, ROWS, COLS = 8, 32, 128


def lane_take(value, index):
    return jnp.take_along_axis(value, index, axis=1, mode="promise_in_bounds")


def with_halo(rows, share, on_edge):
    def complete(r, i):
        by = (COLS - 1 - i * ROWS - r) % COLS
        value = rows(r, i) + jnp.where(on_edge, pltpu.roll(share[6 + (r & 1)], by, 1), 0.0)
        if r == 0:
            value = value + share[i]
        if r == ROWS - 1:
            value = value + share[3 + i]
        return value

    return complete


def kernel(
    n_colat, n_lon,
    heat_hbm, flow_hbm, stiff_hbm, site_hbm, phase_hbm,
    heat_out, flow_out, halo_out,
    stiff_in, site_in, phase_in, in_sem,
    flow, heat, source, found, send_ns, send_we, halo_ns, halo_we, send_sem, recv_sem,
):
    p, c, l = (lax.axis_index(a) for a in ("panel", "colat", "lon"))
    lane = lax.broadcasted_iota(jnp.int32, (LEVELS, COLS), 1)
    level = lax.broadcasted_iota(jnp.int32, (LEVELS, COLS), 0)
    north, south = (c == 0).astype(jnp.int32), (c == n_colat - 1).astype(jnp.int32)
    west, east = (l == 0).astype(jnp.int32), (l == n_lon - 1).astype(jnp.int32)
    at_rim = (north, south, west, east)

    def across(edge):
        return p + edge * (1 - 2 * p)

    sides = (
        ((across(north), c - 1 + north, l), 1 - north),
        ((across(south), c + 1 - south, l), south),
        ((across(west), c, l - 1 + west), 3 - west),
        ((across(east), c, l + 1 - east), 2 + east),
    )
    barrier = pltpu.get_barrier_semaphore()
    for device, _ in sides:
        pl.semaphore_signal(barrier, inc=1, device_id=device, device_id_type=MESH)
    small = [
        pltpu.make_async_copy(src, dst, in_sem.at[n])
        for n, (src, dst) in enumerate(
            ((site_hbm, site_in), (phase_hbm, phase_in), (stiff_hbm, stiff_in))
        )
    ]
    for copy in small:
        copy.start()
    for i in range(3):
        for k in range(LEVELS):
            pltpu.make_async_copy(flow_hbm.at[i, k], flow.at[:, i, k, :], in_sem.at[3]).start()
    for k in range(LEVELS):
        pltpu.make_async_copy(heat_hbm.at[k], heat.at[:, k, :], in_sem.at[4]).start()
    for copy in small:
        copy.wait()

    stiff = jnp.zeros((LEVELS, COLS), jnp.float32)
    for k in range(LEVELS):
        stiff = jnp.where(level == k, stiff_in[k], stiff)
    upper = jnp.where(level < LEVELS - 1, 0.5 * (stiff + pltpu.roll(stiff, LEVELS - 1, 0)), 0.0)
    lower = jnp.where(level > 0, 0.5 * (stiff + pltpu.roll(stiff, 1, 0)), 0.0)
    inverse = 1.0 / (DRAG_COEF + 4.0 * stiff + upper + lower)
    coef, above_coef, below_coef = stiff * inverse, upper * inverse, lower * inverse
    buoyancy = BUOYANCY_FACTOR * inverse

    zero = jnp.zeros((LEVELS, COLS), jnp.float32)
    is_even = (lane & 1) == 0
    on_edge = (lane == 0) | (lane == COLS - 1)

    def shift(value, by):
        return pltpu.roll(value, by % COLS, 1)

    def pick(flag, yes, no):
        return jnp.where(flag == 1, yes, no)

    slot_row, slot_part = lane & (ROWS - 1), lane >> 5
    heat_slot = (lane + 2 * west) & (COLS - 1)

    def sites(j):
        return jnp.broadcast_to(site_in[0, 0:1, COLS * j : COLS * (j + 1)], (LEVELS, COLS))

    ns_site = pick(north, sites(1), sites(2))
    ns_heat = (pick(north, sites(0), sites(2)), pick(north, sites(1), sites(3)))
    we_base = pick(west, 0, 2 * ROWS)
    we_site = lane_take(sites(4), we_base + west + 2 * slot_row)
    we_heat = lane_take(sites(4), we_base + 2 * (heat_slot >> 2) + (heat_slot & 1))
    ns_angle = jnp.broadcast_to(
        pick(north, phase_in[0, 0:1, 0:COLS], phase_in[0, 0:1, COLS : 2 * COLS]), (LEVELS, COLS)
    )
    tail = phase_in[0, 0:1, 2 * COLS : 2 * COLS + 2 * ROWS]
    tail = jnp.broadcast_to(jnp.concatenate([tail, tail], axis=1), (LEVELS, COLS))
    we_angle = lane_take(tail, pick(west, 0, ROWS) + slot_row)

    def heat_row(r):
        return heat[r]

    def collect(index, rows, count):
        at_row, at_col = index >> 7, index & (COLS - 1)
        values = [zero] * count
        for r in range(ROWS):
            here = at_row == r
            values = [
                jnp.where(here, lane_take(rows(r, i), at_col), v) for i, v in enumerate(values)
            ]
        return values

    def flow_row(r, i):
        return flow[r, i]

    def copy(k, par, first, side, arriving=False):
        device, facing = sides[side]
        ns = side < 2
        buf, halo = (send_ns, halo_ns) if ns else (send_we, halo_we)
        own, theirs = (side, facing) if ns else (side - 2, facing - 2)
        n = (5 if first else 3) if ns else (2 if first else 1)

        at, seen = (own, side) if arriving else (theirs, facing)
        return pltpu.make_async_remote_copy(
            src_ref=buf.at[k, own, 0:n],
            dst_ref=halo.at[k, at, 0:n],
            send_sem=send_sem.at[par, side],
            recv_sem=recv_sem.at[par, seen],
            device_id=device,
            device_id_type=MESH,
        )

    def start_rim(k, par, first, ns):
        side = south if ns else east
        buf, halo = (send_ns, halo_ns) if ns else (send_we, halo_we)
        n = (5 if first else 3) if ns else (2 if first else 1)
        at = side if ns else side + 2
        pltpu.make_async_remote_copy(
            src_ref=buf.at[k, side, 0:n],
            dst_ref=halo.at[k, side, 0:n],
            send_sem=send_sem.at[par, at],
            recv_sem=recv_sem.at[par, at],
            device_id=(1 - p, c, l),
            device_id_type=MESH,
        ).start()

    def on_rim(flag_a, flag_b):
        return pl.when((flag_a == 1) | (flag_b == 1))

    def start(k, par, first, side):
        copy(k, par, first, side).start()

    def wait_all(k, par, first, which=(0, 1, 2, 3)):
        for side in which:
            copy(k, par, first, side, arriving=True).wait_recv()

    def wait_sent(k, par, first):
        for side in range(4):
            copy(k, par, first, side).wait_send()

    def pack_all(rows):
        packed = [[zero, zero], [zero, zero]]
        for r in range(ROWS):
            for i in range(3):
                part = shift(jnp.where(on_edge, rows(r, i), 0.0), i * ROWS + r)
                packed[r & 1][(r >> 1) & 1] = packed[r & 1][(r >> 1) & 1] + part
        return packed[0][0] + packed[0][1], packed[1][0] + packed[1][1]

    def find(rows):
        @on_rim(north, south)
        def _():
            for i, v in enumerate(collect(ns_site, rows, 3)):
                found[i] = v

        @on_rim(west, east)
        def _():
            for i, v in enumerate(collect(we_site, rows, 3)):
                found[3 + i] = v

    def rotated(values, angle):
        a, b, d = values
        cos, sin = found[angle], found[angle + 1]
        return a, cos * b + sin * d, cos * d - sin * b

    def send_found_rows(k, par, first, patch):
        values = patch([found[i] for i in range(3)])
        for i, v in enumerate(rotated(values, 6)):
            send_ns[k, south, i] = v
        start_rim(k, par, first, True)

    def send_found_cols(k, par, first, patch):
        @on_rim(west, east)
        def _():
            a, b, d = rotated(patch([found[3 + i] for i in range(3)]), 8)
            send_we[k, east, 0] = jnp.where(slot_part == 0, a, jnp.where(slot_part == 1, b, d))
            start_rim(k, par, first, False)

    def send_inside(k, par, first, which=(2, 3, 0, 1)):
        for side in which:

            @pl.when(at_rim[side] == 0)
            def _(side=side):
                start(k, par, first, side)

    @on_rim(north, south)
    def _():
        found[6], found[7] = jnp.cos(ns_angle), jnp.sin(ns_angle)

    @on_rim(west, east)
    def _():
        found[8], found[9] = jnp.cos(we_angle), jnp.sin(we_angle)

    pltpu.make_async_copy(flow, flow, in_sem.at[3]).wait()
    even, odd = pack_all(flow_row)
    pltpu.make_async_copy(heat, heat, in_sem.at[4]).wait()
    near_edge = (lane < 2) | (lane >= COLS - 2)
    heat_packed = [zero, zero]
    for r in range(ROWS):
        part = shift(jnp.where(near_edge, heat_row(r), 0.0), 4 * r)
        heat_packed[r & 1] = heat_packed[r & 1] + part
    heat_packed = heat_packed[0] + heat_packed[1]
    for j in range(2):
        send_ns[0, 0, 3 + j] = heat_row(j)
        send_ns[0, 1, 3 + j] = heat_row(ROWS - 2 + j)
        send_we[0, j, 1] = heat_packed
    for i in range(3):
        send_ns[0, 0, i] = flow[0, i]
        send_ns[0, 1, i] = flow[ROWS - 1, i]
    send_we[0, 0, 0] = jnp.where(is_even, even, odd)
    send_we[0, 1, 0] = shift(jnp.where(is_even, odd, even), 1)


    @on_rim(north, south)
    def _():
        for j in range(2):
            send_ns[0, south, 3 + j] = collect(ns_heat[j], lambda r, _: heat_row(r), 1)[0]

    @on_rim(west, east)
    def _():
        send_we[0, east, 1] = collect(we_heat, lambda r, _: heat_row(r), 1)[0]

    find(flow_row)
    pl.semaphore_wait(barrier, 4)
    send_inside(0, 0, True)

    @on_rim(north, south)
    def _():
        send_found_rows(0, 0, True, lambda values: values)

    send_found_cols(0, 0, True, lambda values: values)

    def relax(rows, source=None, result=flow):
        before = [zero] * 3
        now = [rows(0, i) for i in range(3)]
        for r in range(ROWS):
            after = [rows(r + 1, i) for i in range(3)] if r < ROWS - 1 else [zero] * 3
            for i in range(3):
                here = now[i]
                near = (
                    (before[i] + after[i])
                    + jnp.where(lane == 0, 0.0, shift(here, 1))
                    + jnp.where(lane == COLS - 1, 0.0, shift(here, -1))
                )
                value = (
                    coef * near
                    + above_coef * pltpu.roll(here, LEVELS - 1, 0)
                    + below_coef * pltpu.roll(here, 1, 0)
                )
                if i == 0 and source is not None:
                    value = value + source[r]
                result[r, i] = value
            before, now = now, after

    def halo_share(k):
        first_cols, last_cols = halo_we[k, 1, 0], shift(halo_we[k, 0, 0], 1)
        share = [coef * halo_ns[k, side, i] for side in range(2) for i in range(3)]
        share.append(coef * jnp.where(is_even, first_cols, last_cols))
        share.append(coef * jnp.where(is_even, last_cols, first_cols))
        return share

    def completed(k):
        return with_halo(lambda r, i: flow[r, i], halo_share(k), on_edge)

    def send_edges(k, par, even, odd, heat=None):
        on_side = north + south

        @pl.when(on_side == 1)
        def _():
            send_edges_as(True, k, par, even, odd, heat)

        @pl.when(on_side == 0)
        def _():
            send_edges_as(False, k, par, even, odd, heat)

    def send_edges_as(rim, k, par, even, odd, heat):
        if heat is None:
            wait_all(k, 1 - par, False, (0, 1))
        above = [coef * halo_ns[k, 0, i] for i in range(3)]
        below = [coef * halo_ns[k, 1, i] for i in range(3)]
        for i in range(3):
            even = even + shift(jnp.where(on_edge, above[i], 0.0), i * ROWS)
            odd = odd + shift(jnp.where(on_edge, below[i], 0.0), i * ROWS + ROWS - 1)
        if heat is not None:
            heat_rows, heat_cols = heat
            for r, value in heat_rows.items():
                part = shift(jnp.where(on_edge, value, 0.0), r)
                even, odd = (even, odd + part) if r & 1 else (even + part, odd)
        def patch_rows(index):
            at_row, at_col = index >> 7, index & (COLS - 1)
            adds = []
            for i in range(3):
                add = jnp.where(at_row == 0, lane_take(above[i], at_col), 0.0)
                add = add + jnp.where(at_row == ROWS - 1, lane_take(below[i], at_col), 0.0)
                if i == 0 and heat is not None:
                    for r, value in heat_rows.items():
                        add = add + jnp.where(at_row == r, lane_take(value, at_col), 0.0)
                    near = (at_col < 2) | (at_col >= COLS - 2)
                    cols = lane_take(heat_cols, (4 * at_row + at_col) & (COLS - 1))
                    add = add + jnp.where(near, cols, 0.0)
                adds.append(add)
            return adds

        def patch_cols(index, adds):
            at_row, at_col = index >> 7, index & (COLS - 1)
            adds = list(adds)
            for i in range(3):
                slot = i * ROWS + at_row
                add = jnp.where(at_col == 0, lane_take(last, slot), 0.0)
                add = add + jnp.where(at_col == COLS - 1, lane_take(first, slot), 0.0)
                adds[i] = adds[i] + add
            return adds

        west_edge, east_edge = jnp.where(is_even, even, odd), shift(jnp.where(is_even, odd, even), 1)
        outer = [[flow[0, i] + above[i] for i in range(3)], [flow[ROWS - 1, i] + below[i] for i in range(3)]]
        if rim:
            adds = patch_rows(ns_site)
        if heat is None:
            wait_all(k, 1 - par, False, (2, 3))
        last, first = coef * halo_we[k, 0, 0], coef * halo_we[k, 1, 0]
        to_west, to_east = last, first
        if heat is not None:
            at_first = lane_take(heat_cols, (4 * lane) & (COLS - 1))
            at_last = lane_take(heat_cols, (4 * lane - 1) & (COLS - 1))
            to_west = to_west + jnp.where(lane < ROWS, at_first, 0.0)
            to_east = to_east + jnp.where(lane < ROWS, at_last, 0.0)
        send_we[k + 1, 0, 0] = west_edge + to_west
        send_we[k + 1, 1, 0] = east_edge + to_east
        send_inside(k + 1, par, False, (2, 3))

        if rim:
            adds = patch_cols(ns_site, adds)
            send_found_rows(k + 1, par, False, lambda found: [f + add for f, add in zip(found, adds)])
        values = ([], [])
        for own, r in ((0, 0), (1, ROWS - 1)):
            for i in range(3):
                t = i * ROWS + r
                value = (
                    outer[own][i]
                    + jnp.where(lane == 0, shift(last, -t), 0.0)
                    + jnp.where(lane == COLS - 1, shift(first, COLS - 1 - t), 0.0)
                )
                if i == 0 and heat is not None:
                    cols = jnp.where(near_edge, shift(heat_cols, -4 * r), 0.0)
                    value = value + (heat_rows[r] + cols)
                values[own].append(value)
        for own in range(2):

            @pl.when(at_rim[own] == 0)
            def _(own=own):
                for i in range(3):
                    send_ns[k + 1, own, i] = values[own][i]
                start(k + 1, par, False, own)


        def patch(found):
            adds = patch_cols(we_site, patch_rows(we_site))
            return [f + add for f, add in zip(found, adds)]

        send_found_cols(k + 1, par, False, patch)

    def or_zero(r):
        return heat_row(r) if 0 <= r < ROWS else zero

    for r in range(ROWS):
        up2, up1, here, down1, down2 = (or_zero(r + j) for j in range(-2, 3))
        west1 = jnp.where(lane < 1, 0.0, shift(here, 1))
        west2 = jnp.where(lane < 2, 0.0, shift(here, 2))
        east1 = jnp.where(lane >= COLS - 1, 0.0, shift(here, -1))
        east2 = jnp.where(lane >= COLS - 2, 0.0, shift(here, -2))
        above = jnp.where(level == LEVELS - 1, here, pltpu.roll(here, LEVELS - 1, 0))
        below = jnp.where(level == 0, here, pltpu.roll(here, 1, 0))
        grad_colat = (8.0 * (down1 - up1) - (down2 - up2)) * (1.0 / 12.0)
        grad_lon = (8.0 * (east1 - west1) - (east2 - west2)) * (1.0 / 12.0)
        grad_rad = (above - below) * 0.5
        laplace = down1 + up1 + east1 + west1 + above + below - 6.0 * here
        advect = flow[r, 0] * grad_rad + flow[r, 1] * grad_colat + flow[r, 2] * grad_lon
        stepped = here + TIME_STEP * (laplace - advect)
        heat_out[r] = stepped
        source[r] = buoyancy * stepped
    outer_flow = {r: flow[r, 1] for r in (0, 1, ROWS - 2, ROWS - 1)}
    lon_flow = [zero, zero]
    for r in range(ROWS):
        part = shift(jnp.where(near_edge, flow[r, 2], 0.0), 4 * r)
        lon_flow[r & 1] = lon_flow[r & 1] + part
    lon_flow = (lon_flow[0] + lon_flow[1]) * (1.0 / 12.0)
    relax(flow_row, source)
    even, odd = pack_all(flow_row)
    find(flow_row)
    wait_all(0, 0, True)

    far, nearby = halo_ns[0, 0, 3], halo_ns[0, 0, 4]
    heat_rows = {
        0: TIME_STEP * (nearby + outer_flow[0] * ((8.0 * nearby - far) * (1.0 / 12.0))),
        1: (-TIME_STEP / 12.0) * (outer_flow[1] * nearby),
    }
    nearby, far = halo_ns[0, 1, 3], halo_ns[0, 1, 4]
    heat_rows[ROWS - 2] = (TIME_STEP / 12.0) * (outer_flow[ROWS - 2] * nearby)
    heat_rows[ROWS - 1] = TIME_STEP * (
        nearby - outer_flow[ROWS - 1] * ((8.0 * nearby - far) * (1.0 / 12.0))
    )
    west1, west2 = shift(halo_we[0, 0, 1], 1), shift(halo_we[0, 0, 1], 2)
    east1, east2 = shift(halo_we[0, 1, 1], -1), shift(halo_we[0, 1, 1], -2)
    column = lane & 3
    heat_cols = TIME_STEP * jnp.where(
        column == 0,
        west1 + lon_flow * (8.0 * west1 - west2),
        jnp.where(
            column == 1,
            -lon_flow * west2,
            jnp.where(column == 2, lon_flow * east2, east1 - lon_flow * (8.0 * east1 - east2)),
        ),
    )
    scaled_rows = {r: buoyancy * value for r, value in heat_rows.items()}
    send_edges(0, 1, even, odd, (scaled_rows, buoyancy * heat_cols))
    for r in range(ROWS):
        add = jnp.where(near_edge, shift(heat_cols, -4 * r), 0.0)
        if r in heat_rows:
            add = add + heat_rows[r]
        heat_out[r] = heat_out[r] + add
        add = buoyancy * add
        source[r] = source[r] + add
        flow[r, 0] = flow[r, 0] + add

    def step(k, carry):
        par = k & 1
        relax(completed(k - 1), source)
        even, odd = pack_all(flow_row)
        find(flow_row)

        @pl.when(k > 1)
        def _():
            wait_sent(k - 1, 1 - par, False)

        send_edges(k, 1 - par, even, odd)
        return carry

    wait_sent(0, 0, True)
    lax.fori_loop(1, ITERS - 1, step, 0)
    relax(completed(ITERS - 2), source, flow_out)
    last_par = (ITERS - 1) & 1
    wait_sent(ITERS - 2, 1 - last_par, False)
    wait_sent(ITERS - 1, last_par, False)
    wait_all(ITERS - 1, last_par, False)
    for n, value in enumerate(halo_share(ITERS - 1)):
        halo_out[n] = value


def deliver(heat_in, flow_in, halo_in, heat_out, flow_out, done, sem):
    for k in range(LEVELS):
        pltpu.make_async_copy(heat_in.at[:, k, :], heat_out.at[k], sem.at[0]).start()
    lane = lax.broadcasted_iota(jnp.int32, (LEVELS, COLS), 1)
    on_edge = (lane == 0) | (lane == COLS - 1)
    rows = with_halo(lambda r, i: flow_in[r, i], [halo_in[n] for n in range(8)], on_edge)

    def send(r):
        pltpu.make_async_copy(done.at[r], flow_out.at[:, :, r, :], sem.at[1]).start()

    lag = 4
    for r in range(ROWS):
        for i in range(3):
            done[r, i] = rows(r, i)
        if r >= lag:
            send(r - lag)
    for r in range(ROWS - lag, ROWS):
        send(r)
    pltpu.make_async_copy(heat_out, heat_out, sem.at[0]).wait()
    pltpu.make_async_copy(flow_out, flow_out, sem.at[1]).wait()


def solution(mesh):
    n_colat, n_lon = mesh.shape["colat"], mesh.shape["lon"]

    block = (LEVELS, COLS)
    heat_shape = jax.ShapeDtypeStruct((LEVELS, ROWS, COLS), jnp.float32)
    flow_shape = jax.ShapeDtypeStruct((3, LEVELS, ROWS, COLS), jnp.float32)
    heat_by_row = jax.ShapeDtypeStruct((ROWS, *block), jnp.float32)
    halo_shape = jax.ShapeDtypeStruct((8, *block), jnp.float32)
    vmem = pl.BlockSpec(memory_space=pltpu.VMEM)
    flow_by_row = jax.ShapeDtypeStruct((ROWS, 3, *block), jnp.float32)
    step = pl.pallas_call(
        lambda *refs: kernel(n_colat, n_lon, *refs),
        out_shape=(heat_by_row, flow_by_row, halo_shape),
        in_specs=[pl.BlockSpec(memory_space=pltpu.HBM)] * 5,
        out_specs=(vmem,) * 3,
        scratch_shapes=[
            pltpu.SMEM((LEVELS,), jnp.float32),
            pltpu.VMEM((1, 1, 4 * (COLS + ROWS)), jnp.int32),
            pltpu.VMEM((1, 1, 2 * (COLS + ROWS)), jnp.float32),
            pltpu.SemaphoreType.DMA((5,)),
            pltpu.VMEM((ROWS, 3, *block), jnp.float32),
            pltpu.VMEM((ROWS, *block), jnp.float32),
            pltpu.VMEM((ROWS, *block), jnp.float32),
            pltpu.VMEM((10, *block), jnp.float32),
            pltpu.VMEM((ITERS, 2, 5, *block), jnp.float32),
            pltpu.VMEM((ITERS, 2, 2, *block), jnp.float32),
            pltpu.VMEM((ITERS, 2, 5, *block), jnp.float32),
            pltpu.VMEM((ITERS, 2, 2, *block), jnp.float32),
            pltpu.SemaphoreType.DMA((2, 4)),
            pltpu.SemaphoreType.DMA((2, 4)),
        ],
        compiler_params=pltpu.CompilerParams(collective_id=0, has_side_effects=True, vmem_limit_bytes=8 << 20),
        name="mantle_step",
    )
    place = pl.pallas_call(
        deliver,
        out_shape=(heat_shape, flow_shape),
        in_specs=[vmem] * 3,
        out_specs=(pl.BlockSpec(memory_space=pltpu.HBM),) * 2,
        scratch_shapes=[
            pltpu.VMEM(flow_by_row.shape, jnp.float32),
            pltpu.SemaphoreType.DMA((2,)),
        ],
        compiler_params=pltpu.CompilerParams(vmem_limit_bytes=4 << 20),
        name="deliver",
    )

    def pinned(*args):
        return step(*(pltpu.with_memory_space_constraint(a, pltpu.HBM) for a in args))

    def on_device(heat, flow, stiffness, site, phase):
        heat_out, flow_out = place(
            *pinned(
                heat.reshape(heat_shape.shape), flow.reshape(flow_shape.shape), stiffness, site, phase,
            )
        )
        return heat_out.reshape(heat.shape), flow_out.reshape(flow.shape)

    return jax.shard_map(
        on_device,
        mesh=mesh,
        in_specs=(
            P("panel", None, "colat", "lon"),
            P("panel", None, None, "colat", "lon"),
            P(),
            P("panel", "colat", "lon"),
            P("panel", "colat", "lon"),
        ),
        out_specs=(P("panel", None, "colat", "lon"), P("panel", None, None, "colat", "lon")),
        check_vma=False,
    )
```

```python
import jax
import jax.numpy as jnp
from jax import lax
from jax.experimental import pallas as pl
from jax.experimental.pallas import tpu as pltpu
from jax.sharding import PartitionSpec as P

ITERS = 8
TIME_STEP = 0.1
BUOYANCY_FACTOR = 10.0
DRAG_COEF = 1.0
MESH = pl.DeviceIdType.MESH
LEVELS, ROWS, COLS = 8, 32, 128


def lane_take(value, index):
    return jnp.take_along_axis(value, index, axis=1, mode="promise_in_bounds")


def with_halo(rows, share, on_edge):
    def complete(r, i):
        by = (COLS - 1 - i * ROWS - r) % COLS
        value = rows(r, i) + jnp.where(on_edge, pltpu.roll(share[6 + (r & 1)], by, 1), 0.0)
        if r == 0:
            value = value + share[i]
        if r == ROWS - 1:
            value = value + share[3 + i]
        return value

    return complete


def kernel(
    n_colat, n_lon,
    heat_hbm, flow_hbm, stiff_hbm, site_hbm, phase_hbm,
    heat_out, flow_out, halo_out,
    stiff_in, site_in, phase_in, in_sem,
    flow, heat, source, found, send_ns, send_we, halo_ns, halo_we, send_sem, recv_sem,
):
    p, c, l = (lax.axis_index(a) for a in ("panel", "colat", "lon"))
    lane = lax.broadcasted_iota(jnp.int32, (LEVELS, COLS), 1)
    level = lax.broadcasted_iota(jnp.int32, (LEVELS, COLS), 0)
    north, south = (c == 0).astype(jnp.int32), (c == n_colat - 1).astype(jnp.int32)
    west, east = (l == 0).astype(jnp.int32), (l == n_lon - 1).astype(jnp.int32)
    at_rim = (north, south, west, east)

    def across(edge):
        return p + edge * (1 - 2 * p)

    sides = (
        ((across(north), c - 1 + north, l), 1 - north),
        ((across(south), c + 1 - south, l), south),
        ((across(west), c, l - 1 + west), 3 - west),
        ((across(east), c, l + 1 - east), 2 + east),
    )
    barrier = pltpu.get_barrier_semaphore()
    for device, _ in sides:
        pl.semaphore_signal(barrier, inc=1, device_id=device, device_id_type=MESH)
    small = [
        pltpu.make_async_copy(src, dst, in_sem.at[n])
        for n, (src, dst) in enumerate(
            ((site_hbm, site_in), (phase_hbm, phase_in), (stiff_hbm, stiff_in))
        )
    ]
    for copy in small:
        copy.start()
    for i in range(3):
        for k in range(LEVELS):
            pltpu.make_async_copy(flow_hbm.at[i, k], flow.at[:, i, k, :], in_sem.at[3]).start()
    for k in range(LEVELS):
        pltpu.make_async_copy(heat_hbm.at[k], heat.at[:, k, :], in_sem.at[4]).start()
    for copy in small:
        copy.wait()

    stiff = jnp.zeros((LEVELS, COLS), jnp.float32)
    for k in range(LEVELS):
        stiff = jnp.where(level == k, stiff_in[k], stiff)
    upper = jnp.where(level < LEVELS - 1, 0.5 * (stiff + pltpu.roll(stiff, LEVELS - 1, 0)), 0.0)
    lower = jnp.where(level > 0, 0.5 * (stiff + pltpu.roll(stiff, 1, 0)), 0.0)
    inverse = 1.0 / (DRAG_COEF + 4.0 * stiff + upper + lower)
    coef, above_coef, below_coef = stiff * inverse, upper * inverse, lower * inverse
    buoyancy = BUOYANCY_FACTOR * inverse

    zero = jnp.zeros((LEVELS, COLS), jnp.float32)
    is_even = (lane & 1) == 0
    on_edge = (lane == 0) | (lane == COLS - 1)

    def shift(value, by):
        return pltpu.roll(value, by % COLS, 1)

    def pick(flag, yes, no):
        return jnp.where(flag == 1, yes, no)

    slot_row, slot_part = lane & (ROWS - 1), lane >> 5
    heat_slot = (lane + 2 * west) & (COLS - 1)

    def sites(j):
        return jnp.broadcast_to(site_in[0, 0:1, COLS * j : COLS * (j + 1)], (LEVELS, COLS))

    ns_site = pick(north, sites(1), sites(2))
    ns_heat = (pick(north, sites(0), sites(2)), pick(north, sites(1), sites(3)))
    we_base = pick(west, 0, 2 * ROWS)
    we_site = lane_take(sites(4), we_base + west + 2 * slot_row)
    we_heat = lane_take(sites(4), we_base + 2 * (heat_slot >> 2) + (heat_slot & 1))
    ns_angle = jnp.broadcast_to(
        pick(north, phase_in[0, 0:1, 0:COLS], phase_in[0, 0:1, COLS : 2 * COLS]), (LEVELS, COLS)
    )
    tail = phase_in[0, 0:1, 2 * COLS : 2 * COLS + 2 * ROWS]
    tail = jnp.broadcast_to(jnp.concatenate([tail, tail], axis=1), (LEVELS, COLS))
    we_angle = lane_take(tail, pick(west, 0, ROWS) + slot_row)

    def heat_row(r):
        return heat[r]

    def collect(index, rows, count):
        at_row, at_col = index >> 7, index & (COLS - 1)
        values = [zero] * count
        for r in range(ROWS):
            here = at_row == r
            values = [
                jnp.where(here, lane_take(rows(r, i), at_col), v) for i, v in enumerate(values)
            ]
        return values

    def flow_row(r, i):
        return flow[r, i]

    def copy(k, par, first, side, arriving=False):
        device, facing = sides[side]
        ns = side < 2
        buf, halo = (send_ns, halo_ns) if ns else (send_we, halo_we)
        own, theirs = (side, facing) if ns else (side - 2, facing - 2)
        n = (5 if first else 3) if ns else (2 if first else 1)

        at, seen = (own, side) if arriving else (theirs, facing)
        return pltpu.make_async_remote_copy(
            src_ref=buf.at[k, own, 0:n],
            dst_ref=halo.at[k, at, 0:n],
            send_sem=send_sem.at[par, side],
            recv_sem=recv_sem.at[par, seen],
            device_id=device,
            device_id_type=MESH,
        )

    def start_columns(k, par, first):
        n = 2 if first else 1
        far = (lax.rem(l, 8) == 7).astype(jnp.int32)
        for own in (far, 1 - far):

            @pl.when(west + own * (east - west) == 0)
            def _(own=own):
                pltpu.make_async_remote_copy(
                    src_ref=send_we.at[k, own, 0:n],
                    dst_ref=halo_we.at[k, 1 - own, 0:n],
                    send_sem=send_sem.at[par, 2 + own],
                    recv_sem=recv_sem.at[par, 3 - own],
                    device_id=(p, c, l - 1 + 2 * own),
                    device_id_type=MESH,
                ).start()

    def start_rim(k, par, first, ns):
        side = south if ns else east
        buf, halo = (send_ns, halo_ns) if ns else (send_we, halo_we)
        n = (5 if first else 3) if ns else (2 if first else 1)
        at = side if ns else side + 2
        pltpu.make_async_remote_copy(
            src_ref=buf.at[k, side, 0:n],
            dst_ref=halo.at[k, side, 0:n],
            send_sem=send_sem.at[par, at],
            recv_sem=recv_sem.at[par, at],
            device_id=(1 - p, c, l),
            device_id_type=MESH,
        ).start()

    def on_rim(flag_a, flag_b):
        return pl.when((flag_a == 1) | (flag_b == 1))

    def start(k, par, first, side):
        copy(k, par, first, side).start()

    def wait_all(k, par, first, which=(0, 1, 2, 3)):
        for side in which:
            copy(k, par, first, side, arriving=True).wait_recv()

    def wait_sent(k, par, first):
        for side in range(4):
            copy(k, par, first, side).wait_send()

    def pack_all(rows):
        packed = [[zero, zero], [zero, zero]]
        for r in range(ROWS):
            for i in range(3):
                part = shift(jnp.where(on_edge, rows(r, i), 0.0), i * ROWS + r)
                packed[r & 1][(r >> 1) & 1] = packed[r & 1][(r >> 1) & 1] + part
        return packed[0][0] + packed[0][1], packed[1][0] + packed[1][1]

    def find(rows):
        @on_rim(north, south)
        def _():
            for i, v in enumerate(collect(ns_site, rows, 3)):
                found[i] = v

        @on_rim(west, east)
        def _():
            for i, v in enumerate(collect(we_site, rows, 3)):
                found[3 + i] = v

    def rotated(values, angle):
        a, b, d = values
        cos, sin = found[angle], found[angle + 1]
        return a, cos * b + sin * d, cos * d - sin * b

    def send_found_rows(k, par, first, patch):
        values = patch([found[i] for i in range(3)])
        for i, v in enumerate(rotated(values, 6)):
            send_ns[k, south, i] = v
        start_rim(k, par, first, True)

    def send_found_cols(k, par, first, patch):
        @on_rim(west, east)
        def _():
            a, b, d = rotated(patch([found[3 + i] for i in range(3)]), 8)
            send_we[k, east, 0] = jnp.where(slot_part == 0, a, jnp.where(slot_part == 1, b, d))
            start_rim(k, par, first, False)

    def send_inside(k, par, first, which=(2, 3, 0, 1)):
        for side in which:

            @pl.when(at_rim[side] == 0)
            def _(side=side):
                start(k, par, first, side)

    @on_rim(north, south)
    def _():
        found[6], found[7] = jnp.cos(ns_angle), jnp.sin(ns_angle)

    @on_rim(west, east)
    def _():
        found[8], found[9] = jnp.cos(we_angle), jnp.sin(we_angle)

    pltpu.make_async_copy(flow, flow, in_sem.at[3]).wait()
    even, odd = pack_all(flow_row)
    pltpu.make_async_copy(heat, heat, in_sem.at[4]).wait()
    near_edge = (lane < 2) | (lane >= COLS - 2)
    heat_packed = [zero, zero]
    for r in range(ROWS):
        part = shift(jnp.where(near_edge, heat_row(r), 0.0), 4 * r)
        heat_packed[r & 1] = heat_packed[r & 1] + part
    heat_packed = heat_packed[0] + heat_packed[1]
    for j in range(2):
        send_ns[0, 0, 3 + j] = heat_row(j)
        send_ns[0, 1, 3 + j] = heat_row(ROWS - 2 + j)
        send_we[0, j, 1] = heat_packed
    for i in range(3):
        send_ns[0, 0, i] = flow[0, i]
        send_ns[0, 1, i] = flow[ROWS - 1, i]
    send_we[0, 0, 0] = jnp.where(is_even, even, odd)
    send_we[0, 1, 0] = shift(jnp.where(is_even, odd, even), 1)


    @on_rim(north, south)
    def _():
        for j in range(2):
            send_ns[0, south, 3 + j] = collect(ns_heat[j], lambda r, _: heat_row(r), 1)[0]

    @on_rim(west, east)
    def _():
        send_we[0, east, 1] = collect(we_heat, lambda r, _: heat_row(r), 1)[0]

    find(flow_row)

    @on_rim(north, south)
    def _():
        for i, v in enumerate(rotated([found[i] for i in range(3)], 6)):
            send_ns[0, south, i] = v

    pl.semaphore_wait(barrier, 4)

    @on_rim(north, south)
    def _():
        start_rim(0, 0, True, True)

    start_columns(0, 0, True)
    send_inside(0, 0, True, (0, 1))

    send_found_cols(0, 0, True, lambda values: values)

    def relax(rows, source=None, result=flow):
        before = [zero] * 3
        now = [rows(0, i) for i in range(3)]
        for r in range(ROWS):
            after = [rows(r + 1, i) for i in range(3)] if r < ROWS - 1 else [zero] * 3
            for i in range(3):
                here = now[i]
                near = (
                    (before[i] + after[i])
                    + jnp.where(lane == 0, 0.0, shift(here, 1))
                    + jnp.where(lane == COLS - 1, 0.0, shift(here, -1))
                )
                value = (
                    coef * near
                    + above_coef * pltpu.roll(here, LEVELS - 1, 0)
                    + below_coef * pltpu.roll(here, 1, 0)
                )
                if i == 0 and source is not None:
                    value = value + source[r]
                result[r, i] = value
            before, now = now, after

    def halo_share(k):
        first_cols, last_cols = halo_we[k, 1, 0], shift(halo_we[k, 0, 0], 1)
        share = [coef * halo_ns[k, side, i] for side in range(2) for i in range(3)]
        share.append(coef * jnp.where(is_even, first_cols, last_cols))
        share.append(coef * jnp.where(is_even, last_cols, first_cols))
        return share

    def completed(k):
        return with_halo(lambda r, i: flow[r, i], halo_share(k), on_edge)

    def send_edges(k, par, even, odd, heat=None):
        on_side = north + south

        @pl.when(on_side == 1)
        def _():
            send_edges_as(True, k, par, even, odd, heat)

        @pl.when(on_side == 0)
        def _():
            send_edges_as(False, k, par, even, odd, heat)

    def send_edges_as(rim, k, par, even, odd, heat):
        if heat is None:
            wait_all(k, 1 - par, False, (0, 1))
        above = [coef * halo_ns[k, 0, i] for i in range(3)]
        below = [coef * halo_ns[k, 1, i] for i in range(3)]
        for i in range(3):
            even = even + shift(jnp.where(on_edge, above[i], 0.0), i * ROWS)
            odd = odd + shift(jnp.where(on_edge, below[i], 0.0), i * ROWS + ROWS - 1)
        if heat is not None:
            heat_rows, heat_cols = heat
            for r, value in heat_rows.items():
                part = shift(jnp.where(on_edge, value, 0.0), r)
                even, odd = (even, odd + part) if r & 1 else (even + part, odd)
        def patch_rows(index):
            at_row, at_col = index >> 7, index & (COLS - 1)
            adds = []
            for i in range(3):
                add = jnp.where(at_row == 0, lane_take(above[i], at_col), 0.0)
                add = add + jnp.where(at_row == ROWS - 1, lane_take(below[i], at_col), 0.0)
                if i == 0 and heat is not None:
                    for r, value in heat_rows.items():
                        add = add + jnp.where(at_row == r, lane_take(value, at_col), 0.0)
                    near = (at_col < 2) | (at_col >= COLS - 2)
                    cols = lane_take(heat_cols, (4 * at_row + at_col) & (COLS - 1))
                    add = add + jnp.where(near, cols, 0.0)
                adds.append(add)
            return adds

        def patch_cols(index, adds):
            at_row, at_col = index >> 7, index & (COLS - 1)
            adds = list(adds)
            for i in range(3):
                slot = i * ROWS + at_row
                add = jnp.where(at_col == 0, lane_take(last, slot), 0.0)
                add = add + jnp.where(at_col == COLS - 1, lane_take(first, slot), 0.0)
                adds[i] = adds[i] + add
            return adds

        west_edge, east_edge = jnp.where(is_even, even, odd), shift(jnp.where(is_even, odd, even), 1)
        outer = [[flow[0, i] + above[i] for i in range(3)], [flow[ROWS - 1, i] + below[i] for i in range(3)]]
        if rim:
            adds = patch_rows(ns_site)
        if heat is None:
            wait_all(k, 1 - par, False, (2, 3))
        last, first = coef * halo_we[k, 0, 0], coef * halo_we[k, 1, 0]
        to_west, to_east = last, first
        if heat is not None:
            at_first = lane_take(heat_cols, (4 * lane) & (COLS - 1))
            at_last = lane_take(heat_cols, (4 * lane - 1) & (COLS - 1))
            to_west = to_west + jnp.where(lane < ROWS, at_first, 0.0)
            to_east = to_east + jnp.where(lane < ROWS, at_last, 0.0)
        send_we[k + 1, 0, 0] = west_edge + to_west
        send_we[k + 1, 1, 0] = east_edge + to_east
        start_columns(k + 1, par, False)

        if rim:
            adds = patch_cols(ns_site, adds)
            send_found_rows(k + 1, par, False, lambda found: [f + add for f, add in zip(found, adds)])
        values = ([], [])
        for own, r in ((0, 0), (1, ROWS - 1)):
            for i in range(3):
                t = i * ROWS + r
                value = (
                    outer[own][i]
                    + jnp.where(lane == 0, shift(last, -t), 0.0)
                    + jnp.where(lane == COLS - 1, shift(first, COLS - 1 - t), 0.0)
                )
                if i == 0 and heat is not None:
                    cols = jnp.where(near_edge, shift(heat_cols, -4 * r), 0.0)
                    value = value + (heat_rows[r] + cols)
                values[own].append(value)
        for own in range(2):

            @pl.when(at_rim[own] == 0)
            def _(own=own):
                for i in range(3):
                    send_ns[k + 1, own, i] = values[own][i]
                start(k + 1, par, False, own)


        def patch(found):
            adds = patch_cols(we_site, patch_rows(we_site))
            return [f + add for f, add in zip(found, adds)]

        send_found_cols(k + 1, par, False, patch)

    def or_zero(r):
        return heat_row(r) if 0 <= r < ROWS else zero

    for r in range(ROWS):
        up2, up1, here, down1, down2 = (or_zero(r + j) for j in range(-2, 3))
        west1 = jnp.where(lane < 1, 0.0, shift(here, 1))
        west2 = jnp.where(lane < 2, 0.0, shift(here, 2))
        east1 = jnp.where(lane >= COLS - 1, 0.0, shift(here, -1))
        east2 = jnp.where(lane >= COLS - 2, 0.0, shift(here, -2))
        above = jnp.where(level == LEVELS - 1, here, pltpu.roll(here, LEVELS - 1, 0))
        below = jnp.where(level == 0, here, pltpu.roll(here, 1, 0))
        grad_colat = (8.0 * (down1 - up1) - (down2 - up2)) * (1.0 / 12.0)
        grad_lon = (8.0 * (east1 - west1) - (east2 - west2)) * (1.0 / 12.0)
        grad_rad = (above - below) * 0.5
        laplace = down1 + up1 + east1 + west1 + above + below - 6.0 * here
        advect = flow[r, 0] * grad_rad + flow[r, 1] * grad_colat + flow[r, 2] * grad_lon
        stepped = here + TIME_STEP * (laplace - advect)
        heat_out[r] = stepped
        source[r] = buoyancy * stepped
    outer_flow = {r: flow[r, 1] for r in (0, 1, ROWS - 2, ROWS - 1)}
    lon_flow = [zero, zero]
    for r in range(ROWS):
        part = shift(jnp.where(near_edge, flow[r, 2], 0.0), 4 * r)
        lon_flow[r & 1] = lon_flow[r & 1] + part
    lon_flow = (lon_flow[0] + lon_flow[1]) * (1.0 / 12.0)
    relax(flow_row, source)
    even, odd = pack_all(flow_row)
    find(flow_row)
    wait_all(0, 0, True)

    far, nearby = halo_ns[0, 0, 3], halo_ns[0, 0, 4]
    heat_rows = {
        0: TIME_STEP * (nearby + outer_flow[0] * ((8.0 * nearby - far) * (1.0 / 12.0))),
        1: (-TIME_STEP / 12.0) * (outer_flow[1] * nearby),
    }
    nearby, far = halo_ns[0, 1, 3], halo_ns[0, 1, 4]
    heat_rows[ROWS - 2] = (TIME_STEP / 12.0) * (outer_flow[ROWS - 2] * nearby)
    heat_rows[ROWS - 1] = TIME_STEP * (
        nearby - outer_flow[ROWS - 1] * ((8.0 * nearby - far) * (1.0 / 12.0))
    )
    west1, west2 = shift(halo_we[0, 0, 1], 1), shift(halo_we[0, 0, 1], 2)
    east1, east2 = shift(halo_we[0, 1, 1], -1), shift(halo_we[0, 1, 1], -2)
    column = lane & 3
    heat_cols = TIME_STEP * jnp.where(
        column == 0,
        west1 + lon_flow * (8.0 * west1 - west2),
        jnp.where(
            column == 1,
            -lon_flow * west2,
            jnp.where(column == 2, lon_flow * east2, east1 - lon_flow * (8.0 * east1 - east2)),
        ),
    )
    scaled_rows = {r: buoyancy * value for r, value in heat_rows.items()}
    send_edges(0, 1, even, odd, (scaled_rows, buoyancy * heat_cols))
    for r in range(ROWS):
        add = jnp.where(near_edge, shift(heat_cols, -4 * r), 0.0)
        if r in heat_rows:
            add = add + heat_rows[r]
        heat_out[r] = heat_out[r] + add
        add = buoyancy * add
        source[r] = source[r] + add
        flow[r, 0] = flow[r, 0] + add

    def step(k, carry):
        par = k & 1
        relax(completed(k - 1), source)
        even, odd = pack_all(flow_row)
        find(flow_row)

        @pl.when(k > 1)
        def _():
            wait_sent(k - 1, 1 - par, False)

        send_edges(k, 1 - par, even, odd)
        return carry

    wait_sent(0, 0, True)
    lax.fori_loop(1, ITERS - 1, step, 0)
    relax(completed(ITERS - 2), source, flow_out)
    last_par = (ITERS - 1) & 1
    wait_sent(ITERS - 2, 1 - last_par, False)
    wait_sent(ITERS - 1, last_par, False)
    wait_all(ITERS - 1, last_par, False)
    for n, value in enumerate(halo_share(ITERS - 1)):
        halo_out[n] = value


def deliver(heat_in, flow_in, halo_in, heat_out, flow_out, done, sem):
    for k in range(LEVELS):
        pltpu.make_async_copy(heat_in.at[:, k, :], heat_out.at[k], sem.at[0]).start()
    lane = lax.broadcasted_iota(jnp.int32, (LEVELS, COLS), 1)
    on_edge = (lane == 0) | (lane == COLS - 1)
    rows = with_halo(lambda r, i: flow_in[r, i], [halo_in[n] for n in range(8)], on_edge)

    def send(r):
        pltpu.make_async_copy(done.at[r], flow_out.at[:, :, r, :], sem.at[1]).start()

    lag = 4
    for r in range(ROWS):
        for i in range(3):
            done[r, i] = rows(r, i)
        if r >= lag:
            send(r - lag)
    for r in range(ROWS - lag, ROWS):
        send(r)
    pltpu.make_async_copy(heat_out, heat_out, sem.at[0]).wait()
    pltpu.make_async_copy(flow_out, flow_out, sem.at[1]).wait()


def solution(mesh):
    n_colat, n_lon = mesh.shape["colat"], mesh.shape["lon"]

    block = (LEVELS, COLS)
    heat_shape = jax.ShapeDtypeStruct((LEVELS, ROWS, COLS), jnp.float32)
    flow_shape = jax.ShapeDtypeStruct((3, LEVELS, ROWS, COLS), jnp.float32)
    heat_by_row = jax.ShapeDtypeStruct((ROWS, *block), jnp.float32)
    halo_shape = jax.ShapeDtypeStruct((8, *block), jnp.float32)
    vmem = pl.BlockSpec(memory_space=pltpu.VMEM)
    flow_by_row = jax.ShapeDtypeStruct((ROWS, 3, *block), jnp.float32)
    step = pl.pallas_call(
        lambda *refs: kernel(n_colat, n_lon, *refs),
        out_shape=(heat_by_row, flow_by_row, halo_shape),
        in_specs=[pl.BlockSpec(memory_space=pltpu.HBM)] * 5,
        out_specs=(vmem,) * 3,
        scratch_shapes=[
            pltpu.SMEM((LEVELS,), jnp.float32),
            pltpu.VMEM((1, 1, 4 * (COLS + ROWS)), jnp.int32),
            pltpu.VMEM((1, 1, 2 * (COLS + ROWS)), jnp.float32),
            pltpu.SemaphoreType.DMA((5,)),
            pltpu.VMEM((ROWS, 3, *block), jnp.float32),
            pltpu.VMEM((ROWS, *block), jnp.float32),
            pltpu.VMEM((ROWS, *block), jnp.float32),
            pltpu.VMEM((10, *block), jnp.float32),
            pltpu.VMEM((ITERS, 2, 5, *block), jnp.float32),
            pltpu.VMEM((ITERS, 2, 2, *block), jnp.float32),
            pltpu.VMEM((ITERS, 2, 5, *block), jnp.float32),
            pltpu.VMEM((ITERS, 2, 2, *block), jnp.float32),
            pltpu.SemaphoreType.DMA((2, 4)),
            pltpu.SemaphoreType.DMA((2, 4)),
        ],
        compiler_params=pltpu.CompilerParams(collective_id=0, has_side_effects=True, vmem_limit_bytes=8 << 20),
        name="mantle_step",
    )
    place = pl.pallas_call(
        deliver,
        out_shape=(heat_shape, flow_shape),
        in_specs=[vmem] * 3,
        out_specs=(pl.BlockSpec(memory_space=pltpu.HBM),) * 2,
        scratch_shapes=[
            pltpu.VMEM(flow_by_row.shape, jnp.float32),
            pltpu.SemaphoreType.DMA((2,)),
        ],
        compiler_params=pltpu.CompilerParams(vmem_limit_bytes=4 << 20),
        name="deliver",
    )

    def pinned(*args):
        return step(*(pltpu.with_memory_space_constraint(a, pltpu.HBM) for a in args))

    def on_device(heat, flow, stiffness, site, phase):
        heat_out, flow_out = place(
            *pinned(
                heat.reshape(heat_shape.shape), flow.reshape(flow_shape.shape), stiffness, site, phase,
            )
        )
        return heat_out.reshape(heat.shape), flow_out.reshape(flow.shape)

    return jax.shard_map(
        on_device,
        mesh=mesh,
        in_specs=(
            P("panel", None, "colat", "lon"),
            P("panel", None, None, "colat", "lon"),
            P(),
            P("panel", "colat", "lon"),
            P("panel", "colat", "lon"),
        ),
        out_specs=(P("panel", None, "colat", "lon"), P("panel", None, None, "colat", "lon")),
        check_vma=False,
    )
```

```python
import jax
import jax.numpy as jnp
from jax import lax
from jax.experimental import pallas as pl
from jax.experimental.pallas import tpu as pltpu
from jax.sharding import PartitionSpec as P

ITERS = 8
TIME_STEP = 0.1
BUOYANCY_FACTOR = 10.0
DRAG_COEF = 1.0
MESH = pl.DeviceIdType.MESH
LEVELS, ROWS, COLS = 8, 32, 128


def lane_take(value, index):
    return jnp.take_along_axis(value, index, axis=1, mode="promise_in_bounds")


def with_halo(rows, share, on_edge):
    def complete(r, i):
        by = (COLS - 1 - i * ROWS - r) % COLS
        value = rows(r, i) + jnp.where(on_edge, pltpu.roll(share[6 + (r & 1)], by, 1), 0.0)
        if r == 0:
            value = value + share[i]
        if r == ROWS - 1:
            value = value + share[3 + i]
        return value

    return complete


def kernel(
    n_colat, n_lon,
    heat_hbm, flow_hbm, stiff_hbm, site_hbm, phase_hbm,
    heat_out, flow_out, halo_out,
    stiff_in, site_in, phase_in, in_sem,
    flow, heat, source, found, send_ns, send_we, halo_ns, halo_we, send_sem, recv_sem,
):
    p, c, l = (lax.axis_index(a) for a in ("panel", "colat", "lon"))
    lane = lax.broadcasted_iota(jnp.int32, (LEVELS, COLS), 1)
    level = lax.broadcasted_iota(jnp.int32, (LEVELS, COLS), 0)
    north, south = (c == 0).astype(jnp.int32), (c == n_colat - 1).astype(jnp.int32)
    west, east = (l == 0).astype(jnp.int32), (l == n_lon - 1).astype(jnp.int32)
    at_rim = (north, south, west, east)

    def across(edge):
        return p + edge * (1 - 2 * p)

    sides = (
        ((across(north), c - 1 + north, l), 1 - north),
        ((across(south), c + 1 - south, l), south),
        ((across(west), c, l - 1 + west), 3 - west),
        ((across(east), c, l + 1 - east), 2 + east),
    )
    barrier = pltpu.get_barrier_semaphore()
    for device, _ in sides:
        pl.semaphore_signal(barrier, inc=1, device_id=device, device_id_type=MESH)
    small = [
        pltpu.make_async_copy(src, dst, in_sem.at[n])
        for n, (src, dst) in enumerate(
            ((site_hbm, site_in), (phase_hbm, phase_in), (stiff_hbm, stiff_in))
        )
    ]
    for copy in small:
        copy.start()
    for i in range(3):
        for k in range(LEVELS):
            pltpu.make_async_copy(flow_hbm.at[i, k], flow.at[:, i, k, :], in_sem.at[3]).start()
    for k in range(LEVELS):
        pltpu.make_async_copy(heat_hbm.at[k], heat.at[:, k, :], in_sem.at[4]).start()
    for copy in small:
        copy.wait()

    stiff = jnp.zeros((LEVELS, COLS), jnp.float32)
    for k in range(LEVELS):
        stiff = jnp.where(level == k, stiff_in[k], stiff)
    upper = jnp.where(level < LEVELS - 1, 0.5 * (stiff + pltpu.roll(stiff, LEVELS - 1, 0)), 0.0)
    lower = jnp.where(level > 0, 0.5 * (stiff + pltpu.roll(stiff, 1, 0)), 0.0)
    inverse = 1.0 / (DRAG_COEF + 4.0 * stiff + upper + lower)
    coef, above_coef, below_coef = stiff * inverse, upper * inverse, lower * inverse
    buoyancy = BUOYANCY_FACTOR * inverse

    zero = jnp.zeros((LEVELS, COLS), jnp.float32)
    is_even = (lane & 1) == 0
    on_edge = (lane == 0) | (lane == COLS - 1)

    def shift(value, by):
        return pltpu.roll(value, by % COLS, 1)

    def pick(flag, yes, no):
        return jnp.where(flag == 1, yes, no)

    slot_row, slot_part = lane & (ROWS - 1), lane >> 5
    heat_slot = (lane + 2 * west) & (COLS - 1)

    def sites(j):
        return jnp.broadcast_to(site_in[0, 0:1, COLS * j : COLS * (j + 1)], (LEVELS, COLS))

    ns_site = pick(north, sites(1), sites(2))
    ns_heat = (pick(north, sites(0), sites(2)), pick(north, sites(1), sites(3)))
    we_base = pick(west, 0, 2 * ROWS)
    we_site = lane_take(sites(4), we_base + west + 2 * slot_row)
    we_heat = lane_take(sites(4), we_base + 2 * (heat_slot >> 2) + (heat_slot & 1))
    ns_angle = jnp.broadcast_to(
        pick(north, phase_in[0, 0:1, 0:COLS], phase_in[0, 0:1, COLS : 2 * COLS]), (LEVELS, COLS)
    )
    tail = phase_in[0, 0:1, 2 * COLS : 2 * COLS + 2 * ROWS]
    tail = jnp.broadcast_to(jnp.concatenate([tail, tail], axis=1), (LEVELS, COLS))
    we_angle = lane_take(tail, pick(west, 0, ROWS) + slot_row)

    def heat_row(r):
        return heat[r]

    def collect(index, rows, count):
        at_row, at_col = index >> 7, index & (COLS - 1)
        values = [zero] * count
        for r in range(ROWS):
            here = at_row == r
            values = [
                jnp.where(here, lane_take(rows(r, i), at_col), v) for i, v in enumerate(values)
            ]
        return values

    def flow_row(r, i):
        return flow[r, i]

    def copy(k, par, first, side, arriving=False):
        device, facing = sides[side]
        ns = side < 2
        buf, halo = (send_ns, halo_ns) if ns else (send_we, halo_we)
        own, theirs = (side, facing) if ns else (side - 2, facing - 2)
        n = (5 if first else 3) if ns else (2 if first else 1)

        at, seen = (own, side) if arriving else (theirs, facing)
        return pltpu.make_async_remote_copy(
            src_ref=buf.at[k, own, 0:n],
            dst_ref=halo.at[k, at, 0:n],
            send_sem=send_sem.at[par, side],
            recv_sem=recv_sem.at[par, seen],
            device_id=device,
            device_id_type=MESH,
        )

    def start_rim(k, par, first, ns):
        side = south if ns else east
        buf, halo = (send_ns, halo_ns) if ns else (send_we, halo_we)
        n = (5 if first else 3) if ns else (2 if first else 1)
        at = side if ns else side + 2
        pltpu.make_async_remote_copy(
            src_ref=buf.at[k, side, 0:n],
            dst_ref=halo.at[k, side, 0:n],
            send_sem=send_sem.at[par, at],
            recv_sem=recv_sem.at[par, at],
            device_id=(1 - p, c, l),
            device_id_type=MESH,
        ).start()

    def on_rim(flag_a, flag_b):
        return pl.when((flag_a == 1) | (flag_b == 1))

    def start(k, par, first, side):
        copy(k, par, first, side).start()

    def wait_all(k, par, first, which=(0, 1, 2, 3)):
        for side in which:
            copy(k, par, first, side, arriving=True).wait_recv()

    def wait_sent(k, par, first):
        for side in range(4):
            copy(k, par, first, side).wait_send()

    def pack_all(rows):
        packed = [[zero, zero], [zero, zero]]
        for r in range(ROWS):
            for i in range(3):
                part = shift(jnp.where(on_edge, rows(r, i), 0.0), i * ROWS + r)
                packed[r & 1][(r >> 1) & 1] = packed[r & 1][(r >> 1) & 1] + part
        return packed[0][0] + packed[0][1], packed[1][0] + packed[1][1]

    def find(rows):
        @on_rim(north, south)
        def _():
            for i, v in enumerate(collect(ns_site, rows, 3)):
                found[i] = v

        @on_rim(west, east)
        def _():
            for i, v in enumerate(collect(we_site, rows, 3)):
                found[3 + i] = v

    def rotated(values, angle):
        a, b, d = values
        cos, sin = found[angle], found[angle + 1]
        return a, cos * b + sin * d, cos * d - sin * b

    def send_found_rows(k, par, first, patch):
        values = patch([found[i] for i in range(3)])
        for i, v in enumerate(rotated(values, 6)):
            send_ns[k, south, i] = v
        start_rim(k, par, first, True)

    def send_found_cols(k, par, first, patch):
        @on_rim(west, east)
        def _():
            a, b, d = rotated(patch([found[3 + i] for i in range(3)]), 8)
            send_we[k, east, 0] = jnp.where(slot_part == 0, a, jnp.where(slot_part == 1, b, d))
            start_rim(k, par, first, False)

    def send_inside(k, par, first, which=(2, 3, 0, 1)):
        for side in which:

            @pl.when(at_rim[side] == 0)
            def _(side=side):
                start(k, par, first, side)

    @on_rim(north, south)
    def _():
        found[6], found[7] = jnp.cos(ns_angle), jnp.sin(ns_angle)

    @on_rim(west, east)
    def _():
        found[8], found[9] = jnp.cos(we_angle), jnp.sin(we_angle)

    pltpu.make_async_copy(flow, flow, in_sem.at[3]).wait()
    even, odd = pack_all(flow_row)
    pltpu.make_async_copy(heat, heat, in_sem.at[4]).wait()
    near_edge = (lane < 2) | (lane >= COLS - 2)
    heat_packed = [zero, zero]
    for r in range(ROWS):
        part = shift(jnp.where(near_edge, heat_row(r), 0.0), 4 * r)
        heat_packed[r & 1] = heat_packed[r & 1] + part
    heat_packed = heat_packed[0] + heat_packed[1]
    for j in range(2):
        send_ns[0, 0, 3 + j] = heat_row(j)
        send_ns[0, 1, 3 + j] = heat_row(ROWS - 2 + j)
        send_we[0, j, 1] = heat_packed
    for i in range(3):
        send_ns[0, 0, i] = flow[0, i]
        send_ns[0, 1, i] = flow[ROWS - 1, i]
    send_we[0, 0, 0] = jnp.where(is_even, even, odd)
    send_we[0, 1, 0] = shift(jnp.where(is_even, odd, even), 1)


    @on_rim(north, south)
    def _():
        for j in range(2):
            send_ns[0, south, 3 + j] = collect(ns_heat[j], lambda r, _: heat_row(r), 1)[0]

    @on_rim(west, east)
    def _():
        send_we[0, east, 1] = collect(we_heat, lambda r, _: heat_row(r), 1)[0]

    find(flow_row)

    @on_rim(north, south)
    def _():
        for i, v in enumerate(rotated([found[i] for i in range(3)], 6)):
            send_ns[0, south, i] = v

    pl.semaphore_wait(barrier, 4)

    @on_rim(north, south)
    def _():
        start_rim(0, 0, True, True)

    send_inside(0, 0, True)

    send_found_cols(0, 0, True, lambda values: values)

    def relax(rows, source=None, result=flow):
        before = [zero] * 3
        now = [rows(0, i) for i in range(3)]
        for r in range(ROWS):
            after = [rows(r + 1, i) for i in range(3)] if r < ROWS - 1 else [zero] * 3
            for i in range(3):
                here = now[i]
                near = (
                    (before[i] + after[i])
                    + jnp.where(lane == 0, 0.0, shift(here, 1))
                    + jnp.where(lane == COLS - 1, 0.0, shift(here, -1))
                )
                value = (
                    coef * near
                    + above_coef * pltpu.roll(here, LEVELS - 1, 0)
                    + below_coef * pltpu.roll(here, 1, 0)
                )
                if i == 0 and source is not None:
                    value = value + source[r]
                result[r, i] = value
            before, now = now, after

    def halo_share(k):
        first_cols, last_cols = halo_we[k, 1, 0], shift(halo_we[k, 0, 0], 1)
        share = [coef * halo_ns[k, side, i] for side in range(2) for i in range(3)]
        share.append(coef * jnp.where(is_even, first_cols, last_cols))
        share.append(coef * jnp.where(is_even, last_cols, first_cols))
        return share

    def completed(k):
        return with_halo(lambda r, i: flow[r, i], halo_share(k), on_edge)

    def send_edges(k, par, even, odd, heat=None):
        on_side = north + south

        @pl.when(on_side == 1)
        def _():
            send_edges_as(True, k, par, even, odd, heat)

        @pl.when(on_side == 0)
        def _():
            send_edges_as(False, k, par, even, odd, heat)

    def send_edges_as(rim, k, par, even, odd, heat):
        if heat is None:
            wait_all(k, 1 - par, False, (0, 1))
        above = [coef * halo_ns[k, 0, i] for i in range(3)]
        below = [coef * halo_ns[k, 1, i] for i in range(3)]
        for i in range(3):
            even = even + shift(jnp.where(on_edge, above[i], 0.0), i * ROWS)
            odd = odd + shift(jnp.where(on_edge, below[i], 0.0), i * ROWS + ROWS - 1)
        if heat is not None:
            heat_rows, heat_cols = heat
            for r, value in heat_rows.items():
                part = shift(jnp.where(on_edge, value, 0.0), r)
                even, odd = (even, odd + part) if r & 1 else (even + part, odd)
        def patch_rows(index):
            at_row, at_col = index >> 7, index & (COLS - 1)
            adds = []
            for i in range(3):
                add = jnp.where(at_row == 0, lane_take(above[i], at_col), 0.0)
                add = add + jnp.where(at_row == ROWS - 1, lane_take(below[i], at_col), 0.0)
                if i == 0 and heat is not None:
                    for r, value in heat_rows.items():
                        add = add + jnp.where(at_row == r, lane_take(value, at_col), 0.0)
                    near = (at_col < 2) | (at_col >= COLS - 2)
                    cols = lane_take(heat_cols, (4 * at_row + at_col) & (COLS - 1))
                    add = add + jnp.where(near, cols, 0.0)
                adds.append(add)
            return adds

        def patch_cols(index, adds):
            at_row, at_col = index >> 7, index & (COLS - 1)
            adds = list(adds)
            for i in range(3):
                slot = i * ROWS + at_row
                add = jnp.where(at_col == 0, lane_take(last, slot), 0.0)
                add = add + jnp.where(at_col == COLS - 1, lane_take(first, slot), 0.0)
                adds[i] = adds[i] + add
            return adds

        west_edge, east_edge = jnp.where(is_even, even, odd), shift(jnp.where(is_even, odd, even), 1)
        outer = [[flow[0, i] + above[i] for i in range(3)], [flow[ROWS - 1, i] + below[i] for i in range(3)]]
        if rim:
            adds = patch_rows(ns_site)
        if heat is None:
            wait_all(k, 1 - par, False, (2, 3))
        last, first = coef * halo_we[k, 0, 0], coef * halo_we[k, 1, 0]
        to_west, to_east = last, first
        if heat is not None:
            at_first = lane_take(heat_cols, (4 * lane) & (COLS - 1))
            at_last = lane_take(heat_cols, (4 * lane - 1) & (COLS - 1))
            to_west = to_west + jnp.where(lane < ROWS, at_first, 0.0)
            to_east = to_east + jnp.where(lane < ROWS, at_last, 0.0)
        send_we[k + 1, 0, 0] = west_edge + to_west
        send_we[k + 1, 1, 0] = east_edge + to_east
        send_inside(k + 1, par, False, (2, 3))

        if rim:
            adds = patch_cols(ns_site, adds)
            send_found_rows(k + 1, par, False, lambda found: [f + add for f, add in zip(found, adds)])
        values = ([], [])
        for own, r in ((0, 0), (1, ROWS - 1)):
            for i in range(3):
                t = i * ROWS + r
                value = (
                    outer[own][i]
                    + jnp.where(lane == 0, shift(last, -t), 0.0)
                    + jnp.where(lane == COLS - 1, shift(first, COLS - 1 - t), 0.0)
                )
                if i == 0 and heat is not None:
                    cols = jnp.where(near_edge, shift(heat_cols, -4 * r), 0.0)
                    value = value + (heat_rows[r] + cols)
                values[own].append(value)
        for own in range(2):

            @pl.when(at_rim[own] == 0)
            def _(own=own):
                for i in range(3):
                    send_ns[k + 1, own, i] = values[own][i]
                start(k + 1, par, False, own)


        def patch(found):
            adds = patch_cols(we_site, patch_rows(we_site))
            return [f + add for f, add in zip(found, adds)]

        send_found_cols(k + 1, par, False, patch)

    def or_zero(r):
        return heat_row(r) if 0 <= r < ROWS else zero

    for r in range(ROWS):
        up2, up1, here, down1, down2 = (or_zero(r + j) for j in range(-2, 3))
        west1 = jnp.where(lane < 1, 0.0, shift(here, 1))
        west2 = jnp.where(lane < 2, 0.0, shift(here, 2))
        east1 = jnp.where(lane >= COLS - 1, 0.0, shift(here, -1))
        east2 = jnp.where(lane >= COLS - 2, 0.0, shift(here, -2))
        above = jnp.where(level == LEVELS - 1, here, pltpu.roll(here, LEVELS - 1, 0))
        below = jnp.where(level == 0, here, pltpu.roll(here, 1, 0))
        grad_colat = (8.0 * (down1 - up1) - (down2 - up2)) * (1.0 / 12.0)
        grad_lon = (8.0 * (east1 - west1) - (east2 - west2)) * (1.0 / 12.0)
        grad_rad = (above - below) * 0.5
        laplace = down1 + up1 + east1 + west1 + above + below - 6.0 * here
        advect = flow[r, 0] * grad_rad + flow[r, 1] * grad_colat + flow[r, 2] * grad_lon
        stepped = here + TIME_STEP * (laplace - advect)
        heat_out[r] = stepped
        source[r] = buoyancy * stepped
    outer_flow = {r: flow[r, 1] for r in (0, 1, ROWS - 2, ROWS - 1)}
    lon_flow = [zero, zero]
    for r in range(ROWS):
        part = shift(jnp.where(near_edge, flow[r, 2], 0.0), 4 * r)
        lon_flow[r & 1] = lon_flow[r & 1] + part
    lon_flow = (lon_flow[0] + lon_flow[1]) * (1.0 / 12.0)
    relax(flow_row, source)
    even, odd = pack_all(flow_row)
    find(flow_row)
    wait_all(0, 0, True)

    far, nearby = halo_ns[0, 0, 3], halo_ns[0, 0, 4]
    heat_rows = {
        0: TIME_STEP * (nearby + outer_flow[0] * ((8.0 * nearby - far) * (1.0 / 12.0))),
        1: (-TIME_STEP / 12.0) * (outer_flow[1] * nearby),
    }
    nearby, far = halo_ns[0, 1, 3], halo_ns[0, 1, 4]
    heat_rows[ROWS - 2] = (TIME_STEP / 12.0) * (outer_flow[ROWS - 2] * nearby)
    heat_rows[ROWS - 1] = TIME_STEP * (
        nearby - outer_flow[ROWS - 1] * ((8.0 * nearby - far) * (1.0 / 12.0))
    )
    west1, west2 = shift(halo_we[0, 0, 1], 1), shift(halo_we[0, 0, 1], 2)
    east1, east2 = shift(halo_we[0, 1, 1], -1), shift(halo_we[0, 1, 1], -2)
    column = lane & 3
    heat_cols = TIME_STEP * jnp.where(
        column == 0,
        west1 + lon_flow * (8.0 * west1 - west2),
        jnp.where(
            column == 1,
            -lon_flow * west2,
            jnp.where(column == 2, lon_flow * east2, east1 - lon_flow * (8.0 * east1 - east2)),
        ),
    )
    scaled_rows = {r: buoyancy * value for r, value in heat_rows.items()}
    send_edges(0, 1, even, odd, (scaled_rows, buoyancy * heat_cols))
    for r in range(ROWS):
        add = jnp.where(near_edge, shift(heat_cols, -4 * r), 0.0)
        if r in heat_rows:
            add = add + heat_rows[r]
        heat_out[r] = heat_out[r] + add
        add = buoyancy * add
        source[r] = source[r] + add
        flow[r, 0] = flow[r, 0] + add

    def step(k, carry):
        par = k & 1
        relax(completed(k - 1), source)
        even, odd = pack_all(flow_row)
        find(flow_row)

        @pl.when(k > 1)
        def _():
            wait_sent(k - 1, 1 - par, False)

        send_edges(k, 1 - par, even, odd)
        return carry

    wait_sent(0, 0, True)
    lax.fori_loop(1, ITERS - 1, step, 0)
    relax(completed(ITERS - 2), source, flow_out)
    last_par = (ITERS - 1) & 1
    wait_sent(ITERS - 2, 1 - last_par, False)
    wait_sent(ITERS - 1, last_par, False)
    wait_all(ITERS - 1, last_par, False)
    for n, value in enumerate(halo_share(ITERS - 1)):
        halo_out[n] = value


def deliver(heat_in, flow_in, halo_in, heat_out, flow_out, done, sem):
    for k in range(LEVELS):
        pltpu.make_async_copy(heat_in.at[:, k, :], heat_out.at[k], sem.at[0]).start()
    lane = lax.broadcasted_iota(jnp.int32, (LEVELS, COLS), 1)
    on_edge = (lane == 0) | (lane == COLS - 1)
    rows = with_halo(lambda r, i: flow_in[r, i], [halo_in[n] for n in range(8)], on_edge)

    def send(r):
        pltpu.make_async_copy(done.at[r], flow_out.at[:, :, r, :], sem.at[1]).start()

    lag = 4
    for r in range(ROWS):
        for i in range(3):
            done[r, i] = rows(r, i)
        if r >= lag:
            send(r - lag)
    for r in range(ROWS - lag, ROWS):
        send(r)
    pltpu.make_async_copy(heat_out, heat_out, sem.at[0]).wait()
    pltpu.make_async_copy(flow_out, flow_out, sem.at[1]).wait()


def solution(mesh):
    n_colat, n_lon = mesh.shape["colat"], mesh.shape["lon"]

    block = (LEVELS, COLS)
    heat_shape = jax.ShapeDtypeStruct((LEVELS, ROWS, COLS), jnp.float32)
    flow_shape = jax.ShapeDtypeStruct((3, LEVELS, ROWS, COLS), jnp.float32)
    heat_by_row = jax.ShapeDtypeStruct((ROWS, *block), jnp.float32)
    halo_shape = jax.ShapeDtypeStruct((8, *block), jnp.float32)
    vmem = pl.BlockSpec(memory_space=pltpu.VMEM)
    flow_by_row = jax.ShapeDtypeStruct((ROWS, 3, *block), jnp.float32)
    step = pl.pallas_call(
        lambda *refs: kernel(n_colat, n_lon, *refs),
        out_shape=(heat_by_row, flow_by_row, halo_shape),
        in_specs=[pl.BlockSpec(memory_space=pltpu.HBM)] * 5,
        out_specs=(vmem,) * 3,
        scratch_shapes=[
            pltpu.SMEM((LEVELS,), jnp.float32),
            pltpu.VMEM((1, 1, 4 * (COLS + ROWS)), jnp.int32),
            pltpu.VMEM((1, 1, 2 * (COLS + ROWS)), jnp.float32),
            pltpu.SemaphoreType.DMA((5,)),
            pltpu.VMEM((ROWS, 3, *block), jnp.float32),
            pltpu.VMEM((ROWS, *block), jnp.float32),
            pltpu.VMEM((ROWS, *block), jnp.float32),
            pltpu.VMEM((10, *block), jnp.float32),
            pltpu.VMEM((ITERS, 2, 5, *block), jnp.float32),
            pltpu.VMEM((ITERS, 2, 2, *block), jnp.float32),
            pltpu.VMEM((ITERS, 2, 5, *block), jnp.float32),
            pltpu.VMEM((ITERS, 2, 2, *block), jnp.float32),
            pltpu.SemaphoreType.DMA((2, 4)),
            pltpu.SemaphoreType.DMA((2, 4)),
        ],
        compiler_params=pltpu.CompilerParams(collective_id=0, has_side_effects=True, vmem_limit_bytes=8 << 20),
        name="mantle_step",
    )
    place = pl.pallas_call(
        deliver,
        out_shape=(heat_shape, flow_shape),
        in_specs=[vmem] * 3,
        out_specs=(pl.BlockSpec(memory_space=pltpu.HBM),) * 2,
        scratch_shapes=[
            pltpu.VMEM(flow_by_row.shape, jnp.float32),
            pltpu.SemaphoreType.DMA((2,)),
        ],
        compiler_params=pltpu.CompilerParams(vmem_limit_bytes=4 << 20),
        name="deliver",
    )

    def pinned(*args):
        return step(*(pltpu.with_memory_space_constraint(a, pltpu.HBM) for a in args))

    def on_device(heat, flow, stiffness, site, phase):
        heat_out, flow_out = place(
            *pinned(
                heat.reshape(heat_shape.shape), flow.reshape(flow_shape.shape), stiffness, site, phase,
            )
        )
        return heat_out.reshape(heat.shape), flow_out.reshape(flow.shape)

    return jax.shard_map(
        on_device,
        mesh=mesh,
        in_specs=(
            P("panel", None, "colat", "lon"),
            P("panel", None, None, "colat", "lon"),
            P(),
            P("panel", "colat", "lon"),
            P("panel", "colat", "lon"),
        ),
        out_specs=(P("panel", None, "colat", "lon"), P("panel", None, None, "colat", "lon")),
        check_vma=False,
    )
```

```python
import jax
import jax.numpy as jnp
from jax import lax
from jax.experimental import pallas as pl
from jax.experimental.pallas import tpu as pltpu
from jax.sharding import PartitionSpec as P

ITERS = 8
TIME_STEP = 0.1
BUOYANCY_FACTOR = 10.0
DRAG_COEF = 1.0
MESH = pl.DeviceIdType.MESH
LEVELS, ROWS, COLS = 8, 32, 128


def lane_take(value, index):
    return jnp.take_along_axis(value, index, axis=1, mode="promise_in_bounds")


def with_halo(rows, share, on_edge):
    def complete(r, i):
        by = (COLS - 1 - i * ROWS - r) % COLS
        value = rows(r, i) + jnp.where(on_edge, pltpu.roll(share[6 + (r & 1)], by, 1), 0.0)
        if r == 0:
            value = value + share[i]
        if r == ROWS - 1:
            value = value + share[3 + i]
        return value

    return complete


def kernel(
    n_colat, n_lon,
    heat_hbm, flow_hbm, stiff_hbm, site_hbm, phase_hbm,
    heat_out, flow_out, halo_out,
    stiff_in, site_in, phase_in, in_sem,
    flow, heat, source, found, send_ns, send_we, halo_ns, halo_we, send_sem, recv_sem,
):
    p, c, l = (lax.axis_index(a) for a in ("panel", "colat", "lon"))
    lane = lax.broadcasted_iota(jnp.int32, (LEVELS, COLS), 1)
    level = lax.broadcasted_iota(jnp.int32, (LEVELS, COLS), 0)
    north, south = (c == 0).astype(jnp.int32), (c == n_colat - 1).astype(jnp.int32)
    west, east = (l == 0).astype(jnp.int32), (l == n_lon - 1).astype(jnp.int32)
    at_rim = (north, south, west, east)

    def across(edge):
        return p + edge * (1 - 2 * p)

    sides = (
        ((across(north), c - 1 + north, l), 1 - north),
        ((across(south), c + 1 - south, l), south),
        ((across(west), c, l - 1 + west), 3 - west),
        ((across(east), c, l + 1 - east), 2 + east),
    )
    barrier = pltpu.get_barrier_semaphore()
    for device, _ in sides:
        pl.semaphore_signal(barrier, inc=1, device_id=device, device_id_type=MESH)
    small = [
        pltpu.make_async_copy(src, dst, in_sem.at[n])
        for n, (src, dst) in enumerate(
            ((site_hbm, site_in), (phase_hbm, phase_in), (stiff_hbm, stiff_in))
        )
    ]
    for copy in small:
        copy.start()
    for i in range(3):
        for k in range(LEVELS):
            pltpu.make_async_copy(flow_hbm.at[i, k], flow.at[:, i, k, :], in_sem.at[3]).start()
    for k in range(LEVELS):
        pltpu.make_async_copy(heat_hbm.at[k], heat.at[:, k, :], in_sem.at[4]).start()
    for copy in small:
        copy.wait()

    stiff = jnp.zeros((LEVELS, COLS), jnp.float32)
    for k in range(LEVELS):
        stiff = jnp.where(level == k, stiff_in[k], stiff)
    upper = jnp.where(level < LEVELS - 1, 0.5 * (stiff + pltpu.roll(stiff, LEVELS - 1, 0)), 0.0)
    lower = jnp.where(level > 0, 0.5 * (stiff + pltpu.roll(stiff, 1, 0)), 0.0)
    inverse = 1.0 / (DRAG_COEF + 4.0 * stiff + upper + lower)
    coef, above_coef, below_coef = stiff * inverse, upper * inverse, lower * inverse
    buoyancy = BUOYANCY_FACTOR * inverse

    zero = jnp.zeros((LEVELS, COLS), jnp.float32)
    is_even = (lane & 1) == 0
    on_edge = (lane == 0) | (lane == COLS - 1)

    def shift(value, by):
        return pltpu.roll(value, by % COLS, 1)

    def pick(flag, yes, no):
        return jnp.where(flag == 1, yes, no)

    slot_row, slot_part = lane & (ROWS - 1), lane >> 5
    heat_slot = (lane + 2 * west) & (COLS - 1)

    def sites(j):
        return jnp.broadcast_to(site_in[0, 0:1, COLS * j : COLS * (j + 1)], (LEVELS, COLS))

    ns_site = pick(north, sites(1), sites(2))
    ns_heat = (pick(north, sites(0), sites(2)), pick(north, sites(1), sites(3)))
    we_base = pick(west, 0, 2 * ROWS)
    we_site = lane_take(sites(4), we_base + west + 2 * slot_row)
    we_heat = lane_take(sites(4), we_base + 2 * (heat_slot >> 2) + (heat_slot & 1))
    ns_angle = jnp.broadcast_to(
        pick(north, phase_in[0, 0:1, 0:COLS], phase_in[0, 0:1, COLS : 2 * COLS]), (LEVELS, COLS)
    )
    tail = phase_in[0, 0:1, 2 * COLS : 2 * COLS + 2 * ROWS]
    tail = jnp.broadcast_to(jnp.concatenate([tail, tail], axis=1), (LEVELS, COLS))
    we_angle = lane_take(tail, pick(west, 0, ROWS) + slot_row)

    def heat_row(r):
        return heat[r]

    def collect(index, rows, count):
        at_row, at_col = index >> 7, index & (COLS - 1)
        values = [zero] * count
        for r in range(ROWS):
            here = at_row == r
            values = [
                jnp.where(here, lane_take(rows(r, i), at_col), v) for i, v in enumerate(values)
            ]
        return values

    def flow_row(r, i):
        return flow[r, i]

    def copy(k, par, first, side, arriving=False):
        device, facing = sides[side]
        ns = side < 2
        buf, halo = (send_ns, halo_ns) if ns else (send_we, halo_we)
        own, theirs = (side, facing) if ns else (side - 2, facing - 2)
        n = (5 if first else 3) if ns else (2 if first else 1)

        at, seen = (own, side) if arriving else (theirs, facing)
        return pltpu.make_async_remote_copy(
            src_ref=buf.at[k, own, 0:n],
            dst_ref=halo.at[k, at, 0:n],
            send_sem=send_sem.at[par, side],
            recv_sem=recv_sem.at[par, seen],
            device_id=device,
            device_id_type=MESH,
        )

    def start_rim(k, par, first, ns):
        side = south if ns else east
        buf, halo = (send_ns, halo_ns) if ns else (send_we, halo_we)
        n = (5 if first else 3) if ns else (2 if first else 1)
        at = side if ns else side + 2
        pltpu.make_async_remote_copy(
            src_ref=buf.at[k, side, 0:n],
            dst_ref=halo.at[k, side, 0:n],
            send_sem=send_sem.at[par, at],
            recv_sem=recv_sem.at[par, at],
            device_id=(1 - p, c, l),
            device_id_type=MESH,
        ).start()

    def on_rim(flag_a, flag_b):
        return pl.when((flag_a == 1) | (flag_b == 1))

    def start(k, par, first, side):
        copy(k, par, first, side).start()

    def wait_all(k, par, first, which=(0, 1, 2, 3)):
        for side in which:
            copy(k, par, first, side, arriving=True).wait_recv()

    def wait_sent(k, par, first):
        for side in range(4):
            copy(k, par, first, side).wait_send()

    def pack_all(rows):
        packed = [[zero, zero], [zero, zero]]
        for r in range(ROWS):
            for i in range(3):
                part = shift(jnp.where(on_edge, rows(r, i), 0.0), i * ROWS + r)
                packed[r & 1][(r >> 1) & 1] = packed[r & 1][(r >> 1) & 1] + part
        return packed[0][0] + packed[0][1], packed[1][0] + packed[1][1]

    def find(rows):
        @on_rim(north, south)
        def _():
            for i, v in enumerate(collect(ns_site, rows, 3)):
                found[i] = v

        @on_rim(west, east)
        def _():
            for i, v in enumerate(collect(we_site, rows, 3)):
                found[3 + i] = v

    def rotated(values, angle):
        a, b, d = values
        cos, sin = found[angle], found[angle + 1]
        return a, cos * b + sin * d, cos * d - sin * b

    def send_found_rows(k, par, first, patch):
        values = patch([found[i] for i in range(3)])
        for i, v in enumerate(rotated(values, 6)):
            send_ns[k, south, i] = v
        start_rim(k, par, first, True)

    def send_found_cols(k, par, first, patch):
        @on_rim(west, east)
        def _():
            a, b, d = rotated(patch([found[3 + i] for i in range(3)]), 8)
            send_we[k, east, 0] = jnp.where(slot_part == 0, a, jnp.where(slot_part == 1, b, d))
            start_rim(k, par, first, False)

    def send_inside(k, par, first, which=(2, 3, 0, 1)):
        for side in which:

            @pl.when(at_rim[side] == 0)
            def _(side=side):
                start(k, par, first, side)

    @on_rim(north, south)
    def _():
        found[6], found[7] = jnp.cos(ns_angle), jnp.sin(ns_angle)

    @on_rim(west, east)
    def _():
        found[8], found[9] = jnp.cos(we_angle), jnp.sin(we_angle)

    pltpu.make_async_copy(flow, flow, in_sem.at[3]).wait()
    even, odd = pack_all(flow_row)
    pltpu.make_async_copy(heat, heat, in_sem.at[4]).wait()
    near_edge = (lane < 2) | (lane >= COLS - 2)
    heat_packed = [zero, zero]
    for r in range(ROWS):
        part = shift(jnp.where(near_edge, heat_row(r), 0.0), 4 * r)
        heat_packed[r & 1] = heat_packed[r & 1] + part
    heat_packed = heat_packed[0] + heat_packed[1]
    for j in range(2):
        send_ns[0, 0, 3 + j] = heat_row(j)
        send_ns[0, 1, 3 + j] = heat_row(ROWS - 2 + j)
        send_we[0, j, 1] = heat_packed
    for i in range(3):
        send_ns[0, 0, i] = flow[0, i]
        send_ns[0, 1, i] = flow[ROWS - 1, i]
    send_we[0, 0, 0] = jnp.where(is_even, even, odd)
    send_we[0, 1, 0] = shift(jnp.where(is_even, odd, even), 1)


    @on_rim(north, south)
    def _():
        for j in range(2):
            send_ns[0, south, 3 + j] = collect(ns_heat[j], lambda r, _: heat_row(r), 1)[0]

    @on_rim(west, east)
    def _():
        send_we[0, east, 1] = collect(we_heat, lambda r, _: heat_row(r), 1)[0]

    find(flow_row)
    pl.semaphore_wait(barrier, 4)
    send_inside(0, 0, True)

    @on_rim(north, south)
    def _():
        send_found_rows(0, 0, True, lambda values: values)

    send_found_cols(0, 0, True, lambda values: values)

    def relax(rows, source=None, result=flow):
        before = [zero] * 3
        now = [rows(0, i) for i in range(3)]
        for r in range(ROWS):
            after = [rows(r + 1, i) for i in range(3)] if r < ROWS - 1 else [zero] * 3
            for i in range(3):
                here = now[i]
                near = (
                    (before[i] + after[i])
                    + jnp.where(lane == 0, 0.0, shift(here, 1))
                    + jnp.where(lane == COLS - 1, 0.0, shift(here, -1))
                )
                value = (
                    coef * near
                    + above_coef * pltpu.roll(here, LEVELS - 1, 0)
                    + below_coef * pltpu.roll(here, 1, 0)
                )
                if i == 0 and source is not None:
                    value = value + source[r]
                result[r, i] = value
            before, now = now, after

    def halo_share(k):
        first_cols, last_cols = halo_we[k, 1, 0], shift(halo_we[k, 0, 0], 1)
        share = [coef * halo_ns[k, side, i] for side in range(2) for i in range(3)]
        share.append(coef * jnp.where(is_even, first_cols, last_cols))
        share.append(coef * jnp.where(is_even, last_cols, first_cols))
        return share

    def completed(k):
        return with_halo(lambda r, i: flow[r, i], halo_share(k), on_edge)

    def send_edges(k, par, even, odd, heat=None):
        on_side = north + south

        @pl.when(on_side == 1)
        def _():
            send_edges_as(True, k, par, even, odd, heat)

        @pl.when(on_side == 0)
        def _():
            send_edges_as(False, k, par, even, odd, heat)

    def send_edges_as(rim, k, par, even, odd, heat):
        if heat is None:
            wait_all(k, 1 - par, False, (0, 1))
        above = [coef * halo_ns[k, 0, i] for i in range(3)]
        below = [coef * halo_ns[k, 1, i] for i in range(3)]
        for i in range(3):
            even = even + shift(jnp.where(on_edge, above[i], 0.0), i * ROWS)
            odd = odd + shift(jnp.where(on_edge, below[i], 0.0), i * ROWS + ROWS - 1)
        if heat is not None:
            heat_rows, heat_cols = heat
            for r, value in heat_rows.items():
                part = shift(jnp.where(on_edge, value, 0.0), r)
                even, odd = (even, odd + part) if r & 1 else (even + part, odd)
        def patch_rows(index):
            at_row, at_col = index >> 7, index & (COLS - 1)
            adds = []
            for i in range(3):
                add = jnp.where(at_row == 0, lane_take(above[i], at_col), 0.0)
                add = add + jnp.where(at_row == ROWS - 1, lane_take(below[i], at_col), 0.0)
                if i == 0 and heat is not None:
                    for r, value in heat_rows.items():
                        add = add + jnp.where(at_row == r, lane_take(value, at_col), 0.0)
                    near = (at_col < 2) | (at_col >= COLS - 2)
                    cols = lane_take(heat_cols, (4 * at_row + at_col) & (COLS - 1))
                    add = add + jnp.where(near, cols, 0.0)
                adds.append(add)
            return adds

        def patch_cols(index, adds):
            at_row, at_col = index >> 7, index & (COLS - 1)
            adds = list(adds)
            for i in range(3):
                slot = i * ROWS + at_row
                add = jnp.where(at_col == 0, lane_take(last, slot), 0.0)
                add = add + jnp.where(at_col == COLS - 1, lane_take(first, slot), 0.0)
                adds[i] = adds[i] + add
            return adds

        west_edge, east_edge = jnp.where(is_even, even, odd), shift(jnp.where(is_even, odd, even), 1)
        outer = [[flow[0, i] + above[i] for i in range(3)], [flow[ROWS - 1, i] + below[i] for i in range(3)]]
        if rim:
            adds = patch_rows(ns_site)
        if heat is None:
            wait_all(k, 1 - par, False, (2, 3))
        last, first = coef * halo_we[k, 0, 0], coef * halo_we[k, 1, 0]
        to_west, to_east = last, first
        if heat is not None:
            at_first = lane_take(heat_cols, (4 * lane) & (COLS - 1))
            at_last = lane_take(heat_cols, (4 * lane - 1) & (COLS - 1))
            to_west = to_west + jnp.where(lane < ROWS, at_first, 0.0)
            to_east = to_east + jnp.where(lane < ROWS, at_last, 0.0)
        send_we[k + 1, 0, 0] = west_edge + to_west
        send_we[k + 1, 1, 0] = east_edge + to_east
        send_inside(k + 1, par, False, (2, 3))

        if rim:
            adds = patch_cols(ns_site, adds)
            send_found_rows(k + 1, par, False, lambda found: [f + add for f, add in zip(found, adds)])
        values = ([], [])
        for own, r in ((0, 0), (1, ROWS - 1)):
            for i in range(3):
                t = i * ROWS + r
                value = (
                    outer[own][i]
                    + jnp.where(lane == 0, shift(last, -t), 0.0)
                    + jnp.where(lane == COLS - 1, shift(first, COLS - 1 - t), 0.0)
                )
                if i == 0 and heat is not None:
                    cols = jnp.where(near_edge, shift(heat_cols, -4 * r), 0.0)
                    value = value + (heat_rows[r] + cols)
                values[own].append(value)
        for own in range(2):

            @pl.when(at_rim[own] == 0)
            def _(own=own):
                for i in range(3):
                    send_ns[k + 1, own, i] = values[own][i]
                start(k + 1, par, False, own)


        def patch(found):
            adds = patch_cols(we_site, patch_rows(we_site))
            return [f + add for f, add in zip(found, adds)]

        send_found_cols(k + 1, par, False, patch)

    def or_zero(r):
        return heat_row(r) if 0 <= r < ROWS else zero

    for r in range(ROWS):
        up2, up1, here, down1, down2 = (or_zero(r + j) for j in range(-2, 3))
        west1 = jnp.where(lane < 1, 0.0, shift(here, 1))
        west2 = jnp.where(lane < 2, 0.0, shift(here, 2))
        east1 = jnp.where(lane >= COLS - 1, 0.0, shift(here, -1))
        east2 = jnp.where(lane >= COLS - 2, 0.0, shift(here, -2))
        above = jnp.where(level == LEVELS - 1, here, pltpu.roll(here, LEVELS - 1, 0))
        below = jnp.where(level == 0, here, pltpu.roll(here, 1, 0))
        grad_colat = (8.0 * (down1 - up1) - (down2 - up2)) * (1.0 / 12.0)
        grad_lon = (8.0 * (east1 - west1) - (east2 - west2)) * (1.0 / 12.0)
        grad_rad = (above - below) * 0.5
        laplace = down1 + up1 + east1 + west1 + above + below - 6.0 * here
        advect = flow[r, 0] * grad_rad + flow[r, 1] * grad_colat + flow[r, 2] * grad_lon
        stepped = here + TIME_STEP * (laplace - advect)
        heat_out[r] = stepped
        source[r] = buoyancy * stepped
    outer_flow = {r: flow[r, 1] for r in (0, 1, ROWS - 2, ROWS - 1)}
    lon_flow = [zero, zero]
    for r in range(ROWS):
        part = shift(jnp.where(near_edge, flow[r, 2], 0.0), 4 * r)
        lon_flow[r & 1] = lon_flow[r & 1] + part
    lon_flow = (lon_flow[0] + lon_flow[1]) * (1.0 / 12.0)
    relax(flow_row, source)
    even, odd = pack_all(flow_row)
    find(flow_row)
    wait_all(0, 0, True)

    far, nearby = halo_ns[0, 0, 3], halo_ns[0, 0, 4]
    heat_rows = {
        0: TIME_STEP * (nearby + outer_flow[0] * ((8.0 * nearby - far) * (1.0 / 12.0))),
        1: (-TIME_STEP / 12.0) * (outer_flow[1] * nearby),
    }
    nearby, far = halo_ns[0, 1, 3], halo_ns[0, 1, 4]
    heat_rows[ROWS - 2] = (TIME_STEP / 12.0) * (outer_flow[ROWS - 2] * nearby)
    heat_rows[ROWS - 1] = TIME_STEP * (
        nearby - outer_flow[ROWS - 1] * ((8.0 * nearby - far) * (1.0 / 12.0))
    )
    west1, west2 = shift(halo_we[0, 0, 1], 1), shift(halo_we[0, 0, 1], 2)
    east1, east2 = shift(halo_we[0, 1, 1], -1), shift(halo_we[0, 1, 1], -2)
    column = lane & 3
    heat_cols = TIME_STEP * jnp.where(
        column == 0,
        west1 + lon_flow * (8.0 * west1 - west2),
        jnp.where(
            column == 1,
            -lon_flow * west2,
            jnp.where(column == 2, lon_flow * east2, east1 - lon_flow * (8.0 * east1 - east2)),
        ),
    )
    scaled_rows = {r: buoyancy * value for r, value in heat_rows.items()}
    send_edges(0, 1, even, odd, (scaled_rows, buoyancy * heat_cols))
    for r in range(ROWS):
        add = jnp.where(near_edge, shift(heat_cols, -4 * r), 0.0)
        if r in heat_rows:
            add = add + heat_rows[r]
        heat_out[r] = heat_out[r] + add
        add = buoyancy * add
        source[r] = source[r] + add
        flow[r, 0] = flow[r, 0] + add

    def step(k, carry):
        par = k & 1
        relax(completed(k - 1), source)
        even, odd = pack_all(flow_row)
        find(flow_row)

        @pl.when(k > 1)
        def _():
            wait_sent(k - 1, 1 - par, False)

        send_edges(k, 1 - par, even, odd)
        return carry

    wait_sent(0, 0, True)
    lax.fori_loop(1, ITERS - 1, step, 0)
    relax(completed(ITERS - 2), source, flow_out)
    last_par = (ITERS - 1) & 1
    wait_sent(ITERS - 2, 1 - last_par, False)
    wait_sent(ITERS - 1, last_par, False)
    wait_all(ITERS - 1, last_par, False)
    for n, value in enumerate(halo_share(ITERS - 1)):
        halo_out[n] = value


def deliver(heat_in, flow_in, halo_in, heat_out, flow_out, done, sem):
    for k in range(LEVELS):
        pltpu.make_async_copy(heat_in.at[:, k, :], heat_out.at[k], sem.at[0]).start()
    lane = lax.broadcasted_iota(jnp.int32, (LEVELS, COLS), 1)
    on_edge = (lane == 0) | (lane == COLS - 1)
    rows = with_halo(lambda r, i: flow_in[r, i], [halo_in[n] for n in range(8)], on_edge)

    def send(r):
        pltpu.make_async_copy(done.at[r], flow_out.at[:, :, r, :], sem.at[1]).start()

    lag = 2
    for r in range(ROWS):
        for i in range(3):
            done[r, i] = rows(r, i)
        if r >= lag:
            send(r - lag)
    for r in range(ROWS - lag, ROWS):
        send(r)
    pltpu.make_async_copy(heat_out, heat_out, sem.at[0]).wait()
    pltpu.make_async_copy(flow_out, flow_out, sem.at[1]).wait()


def solution(mesh):
    n_colat, n_lon = mesh.shape["colat"], mesh.shape["lon"]

    block = (LEVELS, COLS)
    heat_shape = jax.ShapeDtypeStruct((LEVELS, ROWS, COLS), jnp.float32)
    flow_shape = jax.ShapeDtypeStruct((3, LEVELS, ROWS, COLS), jnp.float32)
    heat_by_row = jax.ShapeDtypeStruct((ROWS, *block), jnp.float32)
    halo_shape = jax.ShapeDtypeStruct((8, *block), jnp.float32)
    vmem = pl.BlockSpec(memory_space=pltpu.VMEM)
    flow_by_row = jax.ShapeDtypeStruct((ROWS, 3, *block), jnp.float32)
    step = pl.pallas_call(
        lambda *refs: kernel(n_colat, n_lon, *refs),
        out_shape=(heat_by_row, flow_by_row, halo_shape),
        in_specs=[pl.BlockSpec(memory_space=pltpu.HBM)] * 5,
        out_specs=(vmem,) * 3,
        scratch_shapes=[
            pltpu.SMEM((LEVELS,), jnp.float32),
            pltpu.VMEM((1, 1, 4 * (COLS + ROWS)), jnp.int32),
            pltpu.VMEM((1, 1, 2 * (COLS + ROWS)), jnp.float32),
            pltpu.SemaphoreType.DMA((5,)),
            pltpu.VMEM((ROWS, 3, *block), jnp.float32),
            pltpu.VMEM((ROWS, *block), jnp.float32),
            pltpu.VMEM((ROWS, *block), jnp.float32),
            pltpu.VMEM((10, *block), jnp.float32),
            pltpu.VMEM((ITERS, 2, 5, *block), jnp.float32),
            pltpu.VMEM((ITERS, 2, 2, *block), jnp.float32),
            pltpu.VMEM((ITERS, 2, 5, *block), jnp.float32),
            pltpu.VMEM((ITERS, 2, 2, *block), jnp.float32),
            pltpu.SemaphoreType.DMA((2, 4)),
            pltpu.SemaphoreType.DMA((2, 4)),
        ],
        compiler_params=pltpu.CompilerParams(collective_id=0, has_side_effects=True, vmem_limit_bytes=8 << 20),
        name="mantle_step",
    )
    place = pl.pallas_call(
        deliver,
        out_shape=(heat_shape, flow_shape),
        in_specs=[vmem] * 3,
        out_specs=(pl.BlockSpec(memory_space=pltpu.HBM),) * 2,
        scratch_shapes=[
            pltpu.VMEM(flow_by_row.shape, jnp.float32),
            pltpu.SemaphoreType.DMA((2,)),
        ],
        compiler_params=pltpu.CompilerParams(vmem_limit_bytes=4 << 20),
        name="deliver",
    )

    def pinned(*args):
        return step(*(pltpu.with_memory_space_constraint(a, pltpu.HBM) for a in args))

    def on_device(heat, flow, stiffness, site, phase):
        heat_out, flow_out = place(
            *pinned(
                heat.reshape(heat_shape.shape), flow.reshape(flow_shape.shape), stiffness, site, phase,
            )
        )
        return heat_out.reshape(heat.shape), flow_out.reshape(flow.shape)

    return jax.shard_map(
        on_device,
        mesh=mesh,
        in_specs=(
            P("panel", None, "colat", "lon"),
            P("panel", None, None, "colat", "lon"),
            P(),
            P("panel", "colat", "lon"),
            P("panel", "colat", "lon"),
        ),
        out_specs=(P("panel", None, "colat", "lon"), P("panel", None, None, "colat", "lon")),
        check_vma=False,
    )
```
